128 devices in a mesh: unit: 16 (over x, y), tm: 8 (over z, core).
Axes of the slice: x: 4, y: 4, z: 4, core: 2. Of those that a mesh axis runs over, the one named last changes fastest.
Arguments:
- spikes: int32 [4096, 16384], P('tm', 'unit'), may hold values from 0 to 2
- stimulus: bfloat16 [4096, 64], P('tm'), may hold values from -6 to 6
- bias: float32 [16384], P('unit'), may hold values from -1.5 to 0
- hist_weight: float32 [10, 16384], P(None, 'unit'), may hold values from -0.9 to 0.9
- stim_filter: bfloat16 [16384, 64], P('unit'), may hold values from -0.5 to 0.5
- coupling_mix: float32 [10], replicated, may hold values from -3 to 3
- coupling_target: int32 [128, 4], P('unit'), may hold values from 0 to 127, as said below
- coupling_weight: bfloat16 [128, 4, 128, 128], P('unit'), may hold values from -0.059814453 to 0.059814453
Outputs:
- grad_bias: float32 [16384], P('unit')
- grad_hist: float32 [10, 16384], P(None, 'unit')
- grad_stim: float32 [16384, 64], P(('unit', 'tm'))
- grad_coupling: float32 [128, 4, 128, 128], P('unit', None, 'tm')
The draws below stay inside these ranges and needn't reach their ends.
Inputs may be any that keep to these rules, and one draw needn't show every extreme that they name: `coupling_target`: the 4 entries of a row are distinct. Among the rows of one device (8 aligned rows), the targets owned by any one device (tiles k * 8 to k * 8 + 7) are at most 2 distinct tiles, and every owner that is named gets exactly 2.
All inputs are finite; a program needn't handle non-finite values.
Results may differ from the reference program's by a relative error of at most 0.0041.
Values may be sent and summed in bfloat16 or wider, within the bound.
A program may use at most 256 MiB of HBM per device.

```python
import math
import jax
import jax.numpy as jnp
from jax import lax

UNITS_DEV = 1024
TILE = 128
FAN = 4
CAP = 2
NB = 10
LAG = 128
STIM = 64
UNITS = 16384
TIME = 4096
TILES = 128
N_UNIT = 16


def draw_coupling_target(key, part):
    per_dev = UNITS_DEV // TILE
    picks = FAN // CAP
    first_key, second_key, third_key = jax.random.split(key, 3)
    favour = jax.random.randint(first_key, (N_UNIT,), 0, 1 << 16)
    noise = jax.random.randint(second_key, (N_UNIT, per_dev, N_UNIT), 0, 1 << 16)
    owner_score = (noise + favour[None, None, :]) * N_UNIT + jnp.arange(N_UNIT, dtype=jnp.int32)[None, None, :]
    owners = lax.top_k(owner_score, picks)[1].astype(jnp.int32)
    pair_noise = jax.random.randint(third_key, (N_UNIT, N_UNIT, per_dev), 0, 1 << 16)
    pair_score = pair_noise * per_dev + jnp.arange(per_dev, dtype=jnp.int32)[None, None, :]
    pairs = lax.top_k(pair_score, CAP)[1].astype(jnp.int32)
    source_dev = jnp.arange(N_UNIT, dtype=jnp.int32)[:, None, None]
    chosen = pairs[source_dev, owners]
    targets = owners[:, :, :, None] * per_dev + chosen
    return targets.reshape(N_UNIT * per_dev, FAN).astype(jnp.int32)


def plant(entries, stream_key, low, high):
    longest = entries.shape.index(max(entries.shape))
    spots = []
    for shift in (0, 1):
        where = [jax.random.randint(jax.random.fold_in(stream_key, axis), (), 0, length) for axis, length in enumerate(entries.shape)]
        where[longest] = (where[longest] + shift) % entries.shape[longest]
        spots.append(tuple(where))
    return entries.at[spots[0]].set(low).at[spots[1]].set(high)


def shard_levels(rng, extent, shards, least, largest):
    gain, own = 1.0, jax.random.fold_in(rng, 6)
    for axis_at, blocks in shards:
        heights = jnp.exp(jax.random.uniform(jax.random.fold_in(own, axis_at), (blocks,), jnp.float32, least / len(shards), largest / len(shards)))
        gain = gain * jnp.repeat(heights, extent[axis_at] // blocks).reshape([-1 if axis == axis_at else 1 for axis in range(len(extent))])
    return gain


def normal_values(key, extent, deviation, reach, cuts=(), kind=jnp.bfloat16):
    level = shard_levels(key, extent, cuts, -0.22, 0.18) if cuts else 1.0
    drawn = jax.random.normal(key, extent, jnp.float32) * deviation * level
    return jnp.minimum(jnp.maximum(drawn, -reach), reach).astype(kind)


def setup_inputs(seed: int = 0) -> dict:
    seeds = jax.random.split(jax.random.key(seed), 9)
    return {
        "spikes": plant(jax.random.randint(seeds[0], (TIME, UNITS), 0, 3), jax.random.fold_in(seeds[0], 1), 0, 2).astype(jnp.int32),
        "stimulus": normal_values(seeds[1], (TIME, STIM), 1.0, 6.0, ((0, 8),)),
        "bias": jnp.clip(-1.5 + 1.5 * jax.random.uniform(seeds[2], (UNITS,), jnp.float32) ** shard_levels(seeds[2], (UNITS,), ((0, 16),), -0.2, 0.2), -1.5, 0.0),
        "hist_weight": normal_values(seeds[3], (NB, UNITS), 0.15, 0.9, ((1, 16),), jnp.float32),
        "stim_filter": normal_values(seeds[4], (UNITS, STIM), 0.08, 0.5, ((0, 16),)),
        "coupling_mix": normal_values(seeds[5], (NB,), 0.5, 3.0, (), jnp.float32),
        "coupling_target": draw_coupling_target(jax.random.fold_in(seeds[8], 71), 0),
        "coupling_weight": normal_values(seeds[7], (TILES, FAN, TILE, TILE), 0.01, 0.059814453, ((0, 16),)),
    }


def raised_cosine(count, lag):
    low = math.log(2.0)
    high = math.log(lag + 1.0)
    spacing = (high - low) / (count - 1)
    stretched = jnp.log(jnp.arange(1, lag + 1).astype(jnp.float32) + 1.0)
    centers = low + spacing * jnp.arange(count).astype(jnp.float32)
    phases = jnp.clip((stretched[None, :] - centers[:, None]) * (math.pi / (2.0 * spacing)), -math.pi, math.pi)
    shapes = 0.5 * (1.0 + jnp.cos(phases))
    return (shapes / jnp.sum(shapes, axis=1, keepdims=True)).astype(jnp.bfloat16)


def filtered(counts, flipped):
    signal = counts.astype(jnp.float32).transpose(1, 0)[:, None, :]
    result = lax.conv_general_dilated(signal, flipped, (1,), [(LAG, 0)], dimension_numbers=("NCH", "OIH", "NCH"), precision=lax.Precision.HIGHEST)
    return result.transpose(1, 2, 0)


def reference(spikes, stimulus, bias, hist_weight, stim_filter, coupling_mix, coupling_target, coupling_weight):
    time_len = spikes.shape[0]
    basis = raised_cosine(NB, LAG)
    kernel = jnp.concatenate([jnp.zeros((NB, 1), jnp.float32), basis.astype(jnp.float32)], axis=1)
    flipped = kernel[:, ::-1][:, None, :]
    tiles = spikes.reshape(time_len, TILES, TILE).transpose(1, 0, 2)

    def first_pass(tile_counts):
        history = filtered(tile_counts, flipped)
        return jnp.sum(coupling_mix[:, None, None] * history, axis=0).astype(jnp.bfloat16)

    mixed = lax.map(first_pass, tiles)
    per_dev = UNITS_DEV // TILE
    mixed_dev = mixed.reshape(N_UNIT, per_dev, time_len, TILE)
    target_dev = coupling_target.reshape(N_UNIT, per_dev, FAN)
    weight_dev = coupling_weight.reshape(N_UNIT, per_dev, FAN, TILE, TILE)

    def add_device(total, pieces):
        mixed_here, target_here, weight_here = pieces
        products = jnp.einsum("stk,sfkn->sftn", mixed_here.astype(jnp.float32), weight_here.astype(jnp.float32))
        partial_sum = jnp.zeros((TILES, time_len, TILE), jnp.float32).at[target_here.reshape(-1)].add(products.reshape(-1, time_len, TILE))
        rounded = lax.optimization_barrier(partial_sum.astype(jnp.bfloat16)).astype(jnp.float32)
        return total + rounded, None

    coupling, _ = lax.scan(add_device, jnp.zeros((TILES, time_len, TILE), jnp.float32), (mixed_dev, target_dev, weight_dev))
    filter_tiles = stim_filter.reshape(TILES, TILE, STIM)
    bias_tiles = bias.reshape(TILES, TILE)
    weight_tiles = hist_weight.reshape(NB, TILES, TILE).transpose(1, 0, 2)
    stim_float = stimulus.astype(jnp.float32)

    def second_pass(pieces):
        tile_counts, filter_tile, bias_tile, weight_tile, coupling_tile = pieces
        history = filtered(tile_counts, flipped)
        drive = jnp.einsum("tc,uc->tu", stim_float, filter_tile.astype(jnp.float32))
        logit = bias_tile[None, :] + drive + jnp.sum(history * weight_tile[:, None, :], axis=0) + coupling_tile
        resid = tile_counts.astype(jnp.float32) - jnp.exp(logit)
        resid_bf = resid.astype(jnp.bfloat16)
        grad_b = jnp.sum(resid, axis=0) / time_len
        grad_h = jnp.sum(history * resid[None, :, :], axis=1) / time_len
        grad_s = jnp.einsum("tu,tc->uc", resid_bf.astype(jnp.float32), stim_float) / time_len
        return grad_b, grad_h, grad_s, resid_bf

    grad_b, grad_h, grad_s, resid_tiles = lax.map(second_pass, (tiles, filter_tiles, bias_tiles, weight_tiles, coupling))

    def grad_tile(pieces):
        mixed_tile, target_row = pieces
        chosen = resid_tiles[target_row]
        return jnp.einsum("tk,ftn->fkn", mixed_tile.astype(jnp.float32), chosen.astype(jnp.float32)) / time_len

    grad_coupling = lax.map(grad_tile, (mixed, coupling_target))
    grad_bias = grad_b.reshape(UNITS)
    grad_hist = grad_h.transpose(1, 0, 2).reshape(NB, UNITS)
    grad_stim = grad_s.reshape(UNITS, STIM)
    return grad_bias, grad_hist, grad_stim, grad_coupling
```

```python
import math

import jax
import jax.numpy as jnp
from jax import lax
from jax.sharding import PartitionSpec as P

TILE = 128
FAN = 4
CAP = 2
NB = 10
LAG = 128


def passed_along(value, axis, steps):
    count = lax.axis_size(axis)
    leading, last = (max(0, -steps), min(count, count - steps))
    return lax.ppermute(value, axis, [(source, source + steps) for source in range(leading, last)])


def raised_cosine(count, lag):
    low = math.log(2.0)
    high = math.log(lag + 1.0)
    spacing = (high - low) / (count - 1)
    stretched = jnp.log(jnp.arange(1, lag + 1).astype(jnp.float32) + 1.0)
    centers = low + spacing * jnp.arange(count).astype(jnp.float32)
    phases = jnp.clip(
        (stretched[None, :] - centers[:, None]) * (math.pi / (2.0 * spacing)), -math.pi, math.pi
    )
    shapes = 0.5 * (1.0 + jnp.cos(phases))
    return (shapes / jnp.sum(shapes, axis=1, keepdims=True)).astype(jnp.bfloat16)


def shards(
    spikes, stimulus, bias, hist_weight, stim_filter, coupling_mix, coupling_target, coupling_weight
):
    time_dev, units_dev = spikes.shape
    tiles_dev = units_dev // TILE
    unit_count = lax.axis_size("unit")
    time_count = lax.axis_size("tm")
    time_total = time_dev * time_count
    blocks = time_dev // LAG
    counts_bf = spikes.astype(jnp.bfloat16)
    previous = passed_along(counts_bf[time_dev - LAG :], "tm", 1)
    extended = jnp.concatenate([previous, counts_bf], axis=0)
    basis = raised_cosine(NB, LAG)
    period = jnp.concatenate([basis[:, ::-1], jnp.zeros((NB, LAG + 1), jnp.bfloat16)], axis=1)
    toeplitz = jnp.tile(period, (1, LAG))[:, : 2 * LAG * LAG].reshape(NB, LAG, 2 * LAG)
    windows = jnp.stack([extended[w * LAG : (w + 2) * LAG] for w in range(blocks)])
    history_blocks = jnp.einsum(
        "brc,wcu->bwru", toeplitz, windows, preferred_element_type=jnp.float32
    ).reshape(NB, time_dev, units_dev)
    mixed = jnp.sum(coupling_mix[:, None, None] * history_blocks, axis=0).astype(jnp.bfloat16)
    mixed_tiles = mixed.reshape(time_dev, tiles_dev, TILE)
    slot_count = unit_count * CAP
    flat_target = coupling_target.reshape(-1)
    entry_count = flat_target.shape[0]
    owner = flat_target // tiles_dev
    local_tile = flat_target % tiles_dev
    entry_index = jnp.arange(entry_count, dtype=jnp.int32)
    same_tile = flat_target[:, None] == flat_target[None, :]
    first_seen = jnp.logical_not(
        jnp.any(same_tile & (entry_index[None, :] < entry_index[:, None]), axis=1)
    )
    lower_rank = (
        (owner[:, None] == owner[None, :])
        & (local_tile[None, :] < local_tile[:, None])
        & first_seen[None, :]
    )
    slot_of = owner * CAP + jnp.sum(lower_rank.astype(jnp.int32), axis=1)
    slot_hit = slot_of[None, :] == jnp.arange(slot_count, dtype=jnp.int32)[:, None]
    slot_ids = jnp.max(jnp.where(slot_hit, local_tile[None, :], -1), axis=1)
    slot_table = slot_hit.reshape(slot_count, tiles_dev, FAN).astype(jnp.bfloat16)
    slot_weight = jnp.einsum(
        "csf,sfkn->cskn", slot_table, coupling_weight, preferred_element_type=jnp.float32
    ).astype(jnp.bfloat16)
    partials = jnp.einsum(
        "tsk,cskn->ctn", mixed_tiles, slot_weight, preferred_element_type=jnp.float32
    ).astype(jnp.bfloat16)
    received, received_ids = (
        lax.all_to_all(
            partials.reshape(unit_count, CAP, time_dev, TILE),
            "unit",
            split_axis=0,
            concat_axis=0,
            tiled=True,
        ),
        lax.all_to_all(
            slot_ids.reshape(unit_count, CAP), "unit", split_axis=0, concat_axis=0, tiled=True
        ),
    )
    flat_ids = received_ids.reshape(-1)
    placing = (flat_ids[None, :] == jnp.arange(tiles_dev, dtype=jnp.int32)[:, None]).astype(
        jnp.bfloat16
    )
    coupling = jnp.einsum(
        "jc,ctn->tjn",
        placing,
        received.reshape(slot_count, time_dev, TILE),
        preferred_element_type=jnp.float32,
    ).reshape(time_dev, units_dev)
    drive = jnp.einsum("tc,uc->tu", stimulus, stim_filter, preferred_element_type=jnp.float32)
    logit = (
        bias[None, :] + drive + jnp.sum(history_blocks * hist_weight[:, None, :], axis=0) + coupling
    )
    resid = spikes.astype(jnp.float32) - jnp.exp(logit)
    resid_bf = resid.astype(jnp.bfloat16)
    bias_total, hist_total = lax.psum(
        (jnp.sum(resid, axis=0), jnp.sum(history_blocks * resid[None, :, :], axis=1)), "tm"
    )
    grad_bias = bias_total / time_total
    grad_hist = hist_total / time_total
    resid_tiles = resid_bf.reshape(time_dev, tiles_dev, TILE).transpose(1, 0, 2)
    outgoing = jnp.einsum(
        "jc,jtn->ctn", placing, resid_tiles, preferred_element_type=jnp.float32
    ).astype(jnp.bfloat16)
    slots = lax.all_to_all(
        outgoing.reshape(unit_count, CAP, time_dev, TILE),
        "unit",
        split_axis=0,
        concat_axis=0,
        tiled=True,
    ).reshape(slot_count, time_dev, TILE)
    selected = jnp.einsum(
        "ce,ctn->etn", slot_hit.astype(jnp.bfloat16), slots, preferred_element_type=jnp.float32
    ).astype(jnp.bfloat16).reshape(tiles_dev, FAN, time_dev, TILE)
    coupling_terms = jnp.einsum(
        "tsk,sftn->sfkn", mixed_tiles, selected, preferred_element_type=jnp.float32
    )
    grad_coupling = (
        lax.psum_scatter(coupling_terms, "tm", scatter_dimension=2, tiled=True) / time_total
    )
    stim_terms = jnp.einsum("tu,tc->uc", resid_bf, stimulus, preferred_element_type=jnp.float32)
    grad_stim = lax.psum_scatter(stim_terms, "tm", scatter_dimension=0, tiled=True) / time_total
    return (grad_bias, grad_hist, grad_stim, grad_coupling)


def solution(mesh):
    return jax.shard_map(
        shards,
        mesh=mesh,
        in_specs=(
            P("tm", "unit"),
            P("tm", None),
            P("unit"),
            P(None, "unit"),
            P("unit", None),
            P(),
            P("unit", None),
            P("unit", None, None, None),
        ),
        out_specs=(
            P("unit"),
            P(None, "unit"),
            P(("unit", "tm"), None),
            P("unit", None, "tm", None),
        ),
        check_vma=False,
    )
```

```python
import functools
import math

import jax
import jax.numpy as jnp
import ml_dtypes
import numpy as np
from jax import lax
from jax.experimental import pallas as pl
from jax.experimental.pallas import tpu as pltpu
from jax.sharding import PartitionSpec as P

TILE = 128
FAN = 4
CAP = 2
NB = 10
LAG = 128
SIDE = 4
PEERS = SIDE * SIDE
SLOTS = PEERS * CAP
TILES_DEV = 8
UNITS_DEV = TILES_DEV * TILE
TIME_DEV = 512
CHUNKS = TIME_DEV // LAG
STIM = 64
TM = 8
WIDE = 2 * TILE
ENTRIES = TILES_DEV * FAN
MESH = pl.DeviceIdType.MESH
F32 = jnp.float32
BF16 = jnp.bfloat16


def toeplitz_table():
    low = math.log(2.0)
    spacing = (math.log(LAG + 1.0) - low) / (NB - 1)
    stretched = np.log(np.arange(1, LAG + 1) + 1.0)
    centers = low + spacing * np.arange(NB)
    phases = (stretched[None, :] - centers[:, None]) * (math.pi / (2.0 * spacing))
    shapes = 0.5 * (1.0 + np.cos(np.clip(phases, -math.pi, math.pi)))
    basis = (shapes / shapes.sum(axis=1, keepdims=True)).astype(np.float32)
    table = np.zeros((NB, LAG, 2 * LAG), np.float32)
    for row in range(LAG):
        table[:, row, row : row + LAG] = basis[:, ::-1]
    return table.reshape(NB * LAG, 2 * LAG).astype(ml_dtypes.bfloat16)


def plan_kernel(target, named, weight_at, slot_at):
    unit = lax.axis_index("unit")
    here_x, here_y = unit // SIDE, unit % SIDE

    @pl.loop(0, PEERS)
    def _(owner):
        named[owner * CAP] = TILES_DEV
        named[owner * CAP + 1] = -1

    @pl.loop(0, SLOTS * TILES_DEV)
    def _(place):
        weight_at[place] = ENTRIES

    @pl.loop(0, ENTRIES)
    def _(entry):
        tile = target[entry // FAN, entry % FAN]
        at = (tile // TILES_DEV) * CAP
        local = tile % TILES_DEV
        named[at] = jnp.minimum(named[at], local)
        named[at + 1] = jnp.maximum(named[at + 1], local)

    @pl.loop(0, ENTRIES)
    def _(entry):
        tile = target[entry // FAN, entry % FAN]
        owner = tile // TILES_DEV
        local = tile % TILES_DEV
        rank = (local == named[owner * CAP + 1]).astype(jnp.int32)
        step_x = lax.rem(owner // SIDE - here_x + SIDE, SIDE)
        step_y = lax.rem(owner % SIDE - here_y + SIDE, SIDE)
        slot = (step_x * SIDE + step_y) * CAP + rank
        slot_at[entry] = slot
        weight_at[slot * TILES_DEV + entry // FAN] = entry


def main_kernel(
    named,
    weight_at,
    slot_at,
    mix,
    spikes,
    stim,
    bias,
    hist_weight,
    filt,
    weights_hbm,
    toeplitz,
    out_bias,
    out_hist,
    out_stim,
    out_coupling,
    ext,
    halo,
    weights,
    hist,
    mixed,
    base,
    partial_out,
    partial_in,
    stage,
    resid_tiles,
    resid_rows,
    resid_out,
    resid_in,
    names,
    grad,
    stats,
    stats_in,
    stim_sum,
    stim_in,
    pair_in,
    pair_out,
    zed_in,
    sem_weights,
    sem_halo,
    sem_names,
    sem_a_send,
    sem_a_recv,
    sem_b_send,
    sem_b_recv,
    sem_stats_send,
    sem_stats_recv,
    sem_stim_send,
    sem_stim_recv,
    sem_pair,
    sem_zed,
):
    unit = lax.axis_index("unit")
    tm = lax.axis_index("tm")
    here_x, here_y = unit // SIDE, unit % SIDE
    here_z, core = tm // 2, tm % 2

    def ahead(step):
        return lax.rem(here_x + step // SIDE, SIDE) * SIDE + lax.rem(here_y + step % SIDE, SIDE)

    def behind(step):
        return lax.rem(here_x - step // SIDE + SIDE, SIDE) * SIDE + lax.rem(
            here_y - step % SIDE + SIDE, SIDE
        )

    def offset(turn):
        step = lax.rem(turn * 5, PEERS)
        step_x, step_y = step // SIDE, step % SIDE
        step_x = lax.rem(step_x + core * (SIDE - step_x + SIDE - step_x), SIDE)
        step_y = lax.rem(step_y + core * (SIDE - step_y + SIDE - step_y), SIDE)
        return step_x * SIDE + step_y

    def around(step):
        return lax.rem(tm + step, TM)

    barrier = pltpu.get_barrier_semaphore()

    @pl.loop(1, PEERS)
    def _(step):
        pl.semaphore_signal(barrier, inc=1, device_id=(ahead(step), tm), device_id_type=MESH)

    @pl.loop(1, TM)
    def _(step):
        pl.semaphore_signal(barrier, inc=1, device_id=(unit, around(step)), device_id_type=MESH)

    weights_copy = pltpu.make_async_copy(
        weights_hbm, weights.at[pl.ds(0, ENTRIES)], sem_weights.at[0]
    )
    weights_copy.start()
    weights[ENTRIES] = jnp.zeros((TILE, TILE), BF16)
    stage[SLOTS] = jnp.zeros((TILE, TILE), BF16)
    stats[...] = jnp.zeros_like(stats)
    stim_sum[...] = jnp.zeros_like(stim_sum)

    @pl.loop(0, CHUNKS)
    def _(chunk):
        rows = pl.ds(pl.multiple_of(chunk * LAG, LAG), LAG)
        later = pl.ds(pl.multiple_of(chunk * LAG + LAG, LAG), LAG)
        ext[later, :] = spikes[rows, :].astype(BF16)

    pl.semaphore_wait(barrier, PEERS - 1 + TM - 1)

    halo_copy = pltpu.make_async_remote_copy(
        src_ref=ext.at[pl.ds(TIME_DEV, LAG)],
        dst_ref=halo,
        send_sem=sem_halo.at[0],
        recv_sem=sem_halo.at[1],
        device_id=(unit, around(1)),
        device_id_type=MESH,
    )
    halo_copy.start()

    def names_copy(step):
        return pltpu.make_async_remote_copy(
            src_ref=named,
            dst_ref=names.at[step],
            send_sem=sem_names.at[0, step],
            recv_sem=sem_names.at[1, step],
            device_id=(ahead(step), tm),
            device_id_type=MESH,
        )

    @pl.loop(1, PEERS)
    def _(step):
        names_copy(step).start()

    def partial_copy(chunk, step):
        pair = pl.ds(step * CAP, CAP)
        return pltpu.make_async_remote_copy(
            src_ref=partial_out.at[chunk, pair],
            dst_ref=partial_in.at[chunk, pair],
            send_sem=sem_a_send.at[chunk, step],
            recv_sem=sem_a_recv.at[chunk, step],
            device_id=(ahead(step), tm),
            device_id_type=MESH,
        )

    def resid_copy(chunk, step):
        pair = pl.ds(step * CAP, CAP)
        return pltpu.make_async_remote_copy(
            src_ref=resid_out.at[chunk, pair],
            dst_ref=resid_in.at[chunk, pair],
            send_sem=sem_b_send.at[chunk, step],
            recv_sem=sem_b_recv.at[chunk, step],
            device_id=(behind(step), tm),
            device_id_type=MESH,
        )

    weights_copy.wait()

    @pl.loop(0, CHUNKS)
    def _(turn):
        chunk = lax.rem(turn + 1, CHUNKS)
        start = pl.multiple_of(chunk * LAG, LAG)
        rows = pl.ds(start, LAG)

        @pl.when(turn == CHUNKS - 1)
        def _():
            halo_copy.wait()
            ext[pl.ds(0, LAG), :] = halo[...] * jnp.minimum(tm, 1).astype(BF16)

        @pl.loop(0, UNITS_DEV // WIDE)
        def _(part):
            left = pl.multiple_of(part * WIDE, WIDE)
            wide = pl.ds(left, WIDE)
            hist[...] = jnp.dot(
                toeplitz[...], ext[pl.ds(start, 2 * LAG), wide], preferred_element_type=F32
            )
            drive = bias[:, wide] + lax.dot_general(
                stim[rows, :],
                filt[wide, :],
                (((1,), (1,)), ((), ())),
                preferred_element_type=F32,
            )
            for half in range(2):
                inner = slice(half * TILE, (half + 1) * TILE)
                cols = pl.ds(pl.multiple_of(left + half * TILE, TILE), TILE)
                blend = jnp.zeros((LAG, TILE), F32)
                own = drive[:, inner]
                for b in range(NB):
                    h = hist[b * LAG : (b + 1) * LAG, inner]
                    blend = blend + mix[b] * h
                    own = own + hist_weight[b : b + 1, cols] * h
                mixed[rows, cols] = blend.astype(BF16)
                base[rows, cols] = own

        @pl.loop(1, PEERS + 1)
        def _(visit):
            step = offset(visit)
            total = jnp.zeros((LAG, WIDE), F32)
            for s in range(0, TILES_DEV, 2):
                at = step * (CAP * TILES_DEV) + s
                top = jnp.concatenate(
                    [weights[weight_at[at]], weights[weight_at[at + TILES_DEV]]], axis=1
                )
                low = jnp.concatenate(
                    [weights[weight_at[at + 1]], weights[weight_at[at + TILES_DEV + 1]]], axis=1
                )
                total = total + jnp.dot(
                    mixed[rows, s * TILE : (s + 2) * TILE],
                    jnp.concatenate([top, low], axis=0),
                    preferred_element_type=F32,
                )
            partial_out[chunk, step * CAP] = total[:, :TILE].astype(BF16)
            partial_out[chunk, step * CAP + 1] = total[:, TILE:].astype(BF16)

            @pl.when(step > 0)
            def _():
                partial_copy(chunk, step).start()

    @pl.loop(1, PEERS)
    def _(step):
        names_copy(step).wait()

    for k in range(CAP * PEERS):
        names[0, k] = named[k]

    @pl.loop(0, CHUNKS)
    def _(turn):
        chunk = lax.rem(turn + 1, CHUNKS)
        start = pl.multiple_of(chunk * LAG, LAG)
        rows = pl.ds(start, LAG)
        spike_rows = pl.ds(pl.multiple_of(start + LAG, LAG), LAG)

        for k in range(CAP):
            stage[k] = partial_out[chunk, k]

        @pl.loop(1, PEERS)
        def _(step):
            partial_copy(chunk, step).wait_recv()
            for k in range(CAP):
                stage[step * CAP + k] = partial_in[chunk, step * CAP + k]

        @pl.loop(0, UNITS_DEV // WIDE)
        def _(part):
            left = pl.multiple_of(part * WIDE, WIDE)
            wide = pl.ds(left, WIDE)
            hist[...] = jnp.dot(
                toeplitz[...], ext[pl.ds(start, 2 * LAG), wide], preferred_element_type=F32
            )
            for half in range(2):
                inner = slice(half * TILE, (half + 1) * TILE)
                cols = pl.ds(pl.multiple_of(left + half * TILE, TILE), TILE)
                tile = part * 2 + half

                coupling = jnp.zeros((LAG, TILE), F32)
                for step in range(PEERS):
                    first = names[step, unit * CAP]
                    second = names[step, unit * CAP + 1]
                    at = jnp.where(
                        first == tile,
                        step * CAP,
                        jnp.where(second == tile, step * CAP + 1, SLOTS),
                    )
                    coupling = coupling + stage[at].astype(F32)
                resid = ext[spike_rows, cols].astype(F32) - jnp.exp(base[rows, cols] + coupling)
                rounded = resid.astype(BF16)
                resid_tiles[tile] = rounded
                resid_rows[:, cols] = rounded
                stats[NB : NB + 1, cols] += jnp.sum(resid, axis=0, keepdims=True)
                for b in range(NB):
                    h = hist[b * LAG : (b + 1) * LAG, inner]
                    stats[b : b + 1, cols] += jnp.sum(h * resid, axis=0, keepdims=True)

        @pl.loop(1, PEERS + 1)
        def _(visit):
            step = offset(visit)
            first = jnp.minimum(names[step, unit * CAP], TILES_DEV - 1)
            second = jnp.maximum(names[step, unit * CAP + 1], 0)
            resid_out[chunk, step * CAP] = resid_tiles[first]
            resid_out[chunk, step * CAP + 1] = resid_tiles[second]

            @pl.when(step > 0)
            def _():
                resid_copy(chunk, step).start()

        for block in range(TM):
            stim_sum[block] += lax.dot_general(
                stim[rows, :],
                resid_rows[:, block * TILE : (block + 1) * TILE],
                (((0,), (0,)), ((), ())),
                preferred_element_type=F32,
            )

    def stats_copy(step):
        return pltpu.make_async_remote_copy(
            src_ref=stats,
            dst_ref=stats_in.at[tm],
            send_sem=sem_stats_send.at[step],
            recv_sem=sem_stats_recv.at[step],
            device_id=(unit, around(step)),
            device_id_type=MESH,
        )

    def stim_copy(step):
        return pltpu.make_async_remote_copy(
            src_ref=stim_sum.at[around(step)],
            dst_ref=stim_in.at[step],
            send_sem=sem_stim_send.at[step],
            recv_sem=sem_stim_recv.at[step],
            device_id=(unit, around(step)),
            device_id_type=MESH,
        )

    @pl.loop(1, TM)
    def _(step):
        stats_copy(step).start()
        stim_copy(step).start()

    grad[...] = jnp.zeros_like(grad)

    @pl.loop(0, CHUNKS)
    def _(turn):
        chunk = lax.rem(turn + 1, CHUNKS)
        rows = pl.ds(pl.multiple_of(chunk * LAG, LAG), LAG)

        for k in range(CAP):
            stage[k] = resid_out[chunk, k]

        @pl.loop(1, PEERS)
        def _(step):
            resid_copy(chunk, step).wait_recv()
            for k in range(CAP):
                stage[step * CAP + k] = resid_in[chunk, step * CAP + k]

        for s in range(TILES_DEV):
            chosen = jnp.concatenate([stage[slot_at[s * FAN + f]] for f in range(FAN)], axis=1)
            grad[s] += lax.dot_general(
                mixed[rows, s * TILE : (s + 1) * TILE],
                chosen,
                (((0,), (0,)), ((), ())),
                preferred_element_type=F32,
            )

    share = TILE // TM

    def pair_copy(z):
        return pltpu.make_async_remote_copy(
            src_ref=grad.at[:, pl.ds(pl.multiple_of((z * 2 + 1 - core) * share, share), share)],
            dst_ref=pair_in.at[z],
            send_sem=sem_pair.at[0, z],
            recv_sem=sem_pair.at[1, z],
            device_id=(unit, here_z * 2 + 1 - core),
            device_id_type=MESH,
        )

    def zed_copy(step):
        z = lax.rem(here_z + step, SIDE)
        return pltpu.make_async_remote_copy(
            src_ref=pair_out.at[z],
            dst_ref=zed_in.at[step],
            send_sem=sem_zed.at[0, step],
            recv_sem=sem_zed.at[1, step],
            device_id=(unit, z * 2 + core),
            device_id_type=MESH,
        )

    for step in (1, 2, 3, 0):
        pair_copy(lax.rem(here_z + step, SIDE)).start()

    def both(z):
        kept = pl.ds(pl.multiple_of((z * 2 + core) * share, share), share)
        return grad[:, kept, :] + pair_in[z]

    for step in (1, 2, 3):
        z = lax.rem(here_z + step, SIDE)
        pair_copy(z).wait_recv()
        pair_out[z] = both(z).astype(pair_out.dtype)
        zed_copy(step).start()
    pair_copy(here_z).wait_recv()
    final = both(here_z)

    time_total = float(TIME_DEV * TM)
    stats_in[tm] = stats[...]

    @pl.loop(1, TM)
    def _(step):
        stats_copy(step).wait()
        stim_copy(step).wait()

    total = stats_in[0]
    for block in range(1, TM):
        total = total + stats_in[block]
    out_hist[...] = total[:NB] / time_total
    out_bias[...] = total[NB : NB + 1] / time_total
    stim_total = stim_sum[tm]
    for step in range(1, TM):
        stim_total = stim_total + stim_in[step]
    out_stim[...] = stim_total / time_total

    for step in (1, 2, 3):
        zed_copy(step).wait_recv()
        final = final + zed_in[step].astype(F32)
    final = final / time_total
    for f in range(FAN):
        out_coupling[:, f] = final[:, :, f * TILE : (f + 1) * TILE]

    @pl.loop(0, CHUNKS)
    def _(chunk):
        @pl.loop(1, PEERS)
        def _(step):
            partial_copy(chunk, step).wait_send()
            resid_copy(chunk, step).wait_send()

    @pl.loop(0, SIDE)
    def _(z):
        pair_copy(z).wait_send()

    for step in (1, 2, 3):
        zed_copy(step).wait_send()


def shards(
    spikes, stimulus, bias, hist_weight, stim_filter, coupling_mix, coupling_target, coupling_weight
):
    smem = pl.BlockSpec(memory_space=pltpu.SMEM)
    vmem = pl.BlockSpec(memory_space=pltpu.VMEM)
    anywhere = pl.BlockSpec(memory_space=pl.ANY)
    named, weight_at, slot_at = pl.pallas_call(
        plan_kernel,
        out_shape=[
            jax.ShapeDtypeStruct((SLOTS,), jnp.int32),
            jax.ShapeDtypeStruct((SLOTS * TILES_DEV,), jnp.int32),
            jax.ShapeDtypeStruct((ENTRIES,), jnp.int32),
        ],
        in_specs=[smem],
        out_specs=[smem] * 3,
    )(coupling_target)
    dma = pltpu.SemaphoreType.DMA
    grad_bias, grad_hist, grad_stim, grad_coupling = pl.pallas_call(
        main_kernel,
        out_shape=[
            jax.ShapeDtypeStruct((1, UNITS_DEV), F32),
            jax.ShapeDtypeStruct((NB, UNITS_DEV), F32),
            jax.ShapeDtypeStruct((STIM, TILE), F32),
            jax.ShapeDtypeStruct((TILES_DEV, FAN, TILE // TM, TILE), F32),
        ],
        in_specs=[smem] * 4 + [vmem] * 5 + [anywhere, vmem],
        out_specs=[vmem] * 4,
        scratch_shapes=[
            pltpu.VMEM((TIME_DEV + LAG, UNITS_DEV), BF16),
            pltpu.VMEM((LAG, UNITS_DEV), BF16),
            pltpu.VMEM((ENTRIES + 1, TILE, TILE), BF16),
            pltpu.VMEM((NB * LAG, WIDE), F32),
            pltpu.VMEM((TIME_DEV, UNITS_DEV), BF16),
            pltpu.VMEM((TIME_DEV, UNITS_DEV), F32),
            pltpu.VMEM((CHUNKS, SLOTS, LAG, TILE), BF16),
            pltpu.VMEM((CHUNKS, SLOTS, LAG, TILE), BF16),
            pltpu.VMEM((SLOTS + 1, LAG, TILE), BF16),
            pltpu.VMEM((TILES_DEV, LAG, TILE), BF16),
            pltpu.VMEM((LAG, UNITS_DEV), BF16),
            pltpu.VMEM((CHUNKS, SLOTS, LAG, TILE), BF16),
            pltpu.VMEM((CHUNKS, SLOTS, LAG, TILE), BF16),
            pltpu.SMEM((PEERS, SLOTS), jnp.int32),
            pltpu.VMEM((TILES_DEV, TILE, FAN * TILE), F32),
            pltpu.VMEM((16, UNITS_DEV), F32),
            pltpu.VMEM((TM, 16, UNITS_DEV), F32),
            pltpu.VMEM((TM, STIM, TILE), F32),
            pltpu.VMEM((TM, STIM, TILE), F32),
            pltpu.VMEM((SIDE, TILES_DEV, TILE // TM, FAN * TILE), F32),
            pltpu.VMEM((SIDE, TILES_DEV, TILE // TM, FAN * TILE), F32),
            pltpu.VMEM((SIDE, TILES_DEV, TILE // TM, FAN * TILE), F32),
            dma((1,)),
            dma((2,)),
            dma((2, PEERS)),
            dma((CHUNKS, PEERS)),
            dma((CHUNKS, PEERS)),
            dma((CHUNKS, PEERS)),
            dma((CHUNKS, PEERS)),
            dma((TM,)),
            dma((TM,)),
            dma((TM,)),
            dma((TM,)),
            dma((2, SIDE)),
            dma((2, SIDE)),
        ],
        compiler_params=pltpu.CompilerParams(
            collective_id=0, has_side_effects=True, vmem_limit_bytes=56 * 1024 * 1024
        ),
    )(
        named,
        weight_at,
        slot_at,
        coupling_mix,
        spikes,
        stimulus,
        bias.reshape(1, UNITS_DEV),
        hist_weight,
        stim_filter,
        coupling_weight.reshape(ENTRIES, TILE, TILE),
        jnp.asarray(toeplitz_table()),
    )
    return (grad_bias.reshape(UNITS_DEV), grad_hist, grad_stim.T, grad_coupling)


def solution(mesh):
    return jax.shard_map(
        shards,
        mesh=mesh,
        in_specs=(
            P("tm", "unit"),
            P("tm", None),
            P("unit"),
            P(None, "unit"),
            P("unit", None),
            P(),
            P("unit", None),
            P("unit", None, None, None),
        ),
        out_specs=(
            P("unit"),
            P(None, "unit"),
            P(("unit", "tm"), None),
            P("unit", None, "tm", None),
        ),
        check_vma=False,
    )
```

```python
import functools
import math

import jax
import jax.numpy as jnp
import ml_dtypes
import numpy as np
from jax import lax
from jax.experimental import pallas as pl
from jax.experimental.pallas import tpu as pltpu
from jax.sharding import PartitionSpec as P

TILE = 128
FAN = 4
CAP = 2
NB = 10
LAG = 128
SIDE = 4
PEERS = SIDE * SIDE
SLOTS = PEERS * CAP
TILES_DEV = 8
UNITS_DEV = TILES_DEV * TILE
TIME_DEV = 512
CHUNKS = TIME_DEV // LAG
STIM = 64
TM = 8
WIDE = 2 * TILE
ENTRIES = TILES_DEV * FAN
MESH = pl.DeviceIdType.MESH
F32 = jnp.float32
BF16 = jnp.bfloat16


def toeplitz_table():
    low = math.log(2.0)
    spacing = (math.log(LAG + 1.0) - low) / (NB - 1)
    stretched = np.log(np.arange(1, LAG + 1) + 1.0)
    centers = low + spacing * np.arange(NB)
    phases = (stretched[None, :] - centers[:, None]) * (math.pi / (2.0 * spacing))
    shapes = 0.5 * (1.0 + np.cos(np.clip(phases, -math.pi, math.pi)))
    basis = (shapes / shapes.sum(axis=1, keepdims=True)).astype(np.float32)
    table = np.zeros((NB, LAG, 2 * LAG), np.float32)
    for row in range(LAG):
        table[:, row, row : row + LAG] = basis[:, ::-1]
    return table.reshape(NB * LAG, 2 * LAG).astype(ml_dtypes.bfloat16)


def main_kernel(
    target,
    mix,
    spikes_hbm,
    stim_hbm,
    bias_hbm,
    hist_weight_hbm,
    filt_hbm,
    weights_hbm,
    toeplitz_hbm,
    out_stats,
    out_stim,
    out_coupling,
    spikes,
    stim,
    bias,
    hist_weight,
    filt,
    toeplitz,
    blend_filter,
    ext,
    halo,
    weights,
    hist,
    mixed,
    partial_out,
    partial_in,
    stage,
    resid_tiles,
    resid_rows,
    resid_out,
    resid_in,
    named,
    names,
    grad,
    stats,
    stats_in,
    stim_sum,
    stim_in,
    pair_in,
    pair_out,
    zed_in,
    sem_load,
    sem_spikes,
    sem_halo,
    sem_names,
    sem_a_send,
    sem_a_recv,
    sem_b_send,
    sem_b_recv,
    sem_stats_send,
    sem_stats_recv,
    sem_stim_send,
    sem_stim_recv,
    sem_pair,
    sem_zed,
):
    unit = lax.axis_index("unit")
    tm = lax.axis_index("tm")
    here_x, here_y = unit // SIDE, unit % SIDE
    here_z, core = tm // 2, tm % 2

    def ahead(step):
        return lax.rem(here_x + step // SIDE, SIDE) * SIDE + lax.rem(here_y + step % SIDE, SIDE)

    def behind(step):
        return lax.rem(here_x - step // SIDE + SIDE, SIDE) * SIDE + lax.rem(
            here_y - step % SIDE + SIDE, SIDE
        )

    def offset(turn):
        step = lax.rem(turn * 5, PEERS)
        step_x, step_y = step // SIDE, step % SIDE
        step_x = lax.rem(step_x + core * (SIDE - step_x + SIDE - step_x), SIDE)
        step_y = lax.rem(step_y + core * (SIDE - step_y + SIDE - step_y), SIDE)
        return step_x * SIDE + step_y

    def around(step):
        return lax.rem(tm + step, TM)

    barrier = pltpu.get_barrier_semaphore()

    @pl.loop(1, PEERS)
    def _(step):
        pl.semaphore_signal(barrier, inc=1, device_id=(ahead(step), tm), device_id_type=MESH)

    @pl.loop(1, TM)
    def _(step):
        pl.semaphore_signal(barrier, inc=1, device_id=(unit, around(step)), device_id_type=MESH)

    def spikes_copy(chunk):
        rows = pl.ds(pl.multiple_of(chunk * LAG, LAG), LAG)
        return pltpu.make_async_copy(
            spikes_hbm.at[rows, :], spikes.at[rows, :], sem_spikes.at[chunk]
        )

    loads = [
        pltpu.make_async_copy(source, place, sem_load.at[k])
        for k, (source, place) in enumerate(
            (
                (toeplitz_hbm, toeplitz),
                (weights_hbm, weights.at[pl.ds(0, ENTRIES)]),
                (stim_hbm, stim),
                (bias_hbm, bias),
                (hist_weight_hbm, hist_weight),
                (filt_hbm, filt),
            )
        )
    ]
    spikes_copy(0).start()
    spikes_copy(1).start()
    loads[0].start()
    spikes_copy(3).start()
    loads[1].start()
    spikes_copy(2).start()
    for load in loads[2:]:
        load.start()

    @pl.loop(0, PEERS)
    def _(owner):
        first, last = owner * TILES_DEV, owner * TILES_DEV + TILES_DEV - 1
        low, high = jnp.int32(PEERS * TILES_DEV), jnp.int32(-1)
        for s in range(TILES_DEV):
            for f in range(FAN):
                tile = target[f, s]
                low = jnp.where(tile >= first, jnp.minimum(low, tile), low)
                high = jnp.where(tile <= last, jnp.maximum(high, tile), high)
        named[owner * CAP] = low
        named[owner * CAP + 1] = high

    weights[ENTRIES] = jnp.zeros((TILE, TILE), BF16)
    stage[SLOTS] = jnp.zeros((TILE, TILE), BF16)
    stats[...] = jnp.zeros_like(stats)
    stim_sum[...] = jnp.zeros_like(stim_sum)
    grad[...] = jnp.zeros_like(grad)

    def take_spikes(chunk):
        spikes_copy(chunk).wait()
        ext[(chunk + 1) * LAG : (chunk + 2) * LAG, :] = spikes[
            chunk * LAG : (chunk + 1) * LAG, :
        ].astype(BF16)

    take_spikes(0)
    take_spikes(1)
    loads[0].wait()
    combined = jnp.zeros((LAG, 2 * LAG), F32)
    for b in range(NB):
        combined = combined + mix[b] * toeplitz[b * LAG : (b + 1) * LAG, :].astype(F32)
    upper = combined.astype(BF16)
    blend_filter[:LAG, :] = upper
    blend_filter[LAG:, :] = (combined - upper.astype(F32)).astype(BF16)
    take_spikes(3)

    pl.semaphore_wait(barrier, PEERS - 1 + TM - 1)

    halo_copy = pltpu.make_async_remote_copy(
        src_ref=ext.at[pl.ds(TIME_DEV, LAG)],
        dst_ref=halo,
        send_sem=sem_halo.at[0],
        recv_sem=sem_halo.at[1],
        device_id=(unit, around(1)),
        device_id_type=MESH,
    )
    halo_copy.start()

    def names_copy(step):
        return pltpu.make_async_remote_copy(
            src_ref=named,
            dst_ref=names.at[step],
            send_sem=sem_names.at[0, step],
            recv_sem=sem_names.at[1, step],
            device_id=(ahead(step), tm),
            device_id_type=MESH,
        )

    @pl.loop(1, PEERS)
    def _(step):
        names_copy(step).start()

    def partial_copy(chunk, step):
        pair = pl.ds(step * CAP, CAP)
        return pltpu.make_async_remote_copy(
            src_ref=partial_out.at[chunk, pair],
            dst_ref=partial_in.at[chunk, pair],
            send_sem=sem_a_send.at[chunk, step],
            recv_sem=sem_a_recv.at[chunk, step],
            device_id=(ahead(step), tm),
            device_id_type=MESH,
        )

    def resid_copy(chunk, step):
        pair = pl.ds(step * CAP, CAP)
        return pltpu.make_async_remote_copy(
            src_ref=resid_out.at[chunk, pair],
            dst_ref=resid_in.at[chunk, pair],
            send_sem=sem_b_send.at[chunk, step],
            recv_sem=sem_b_recv.at[chunk, step],
            device_id=(behind(step), tm),
            device_id_type=MESH,
        )

    loads[1].wait()

    @pl.loop(0, CHUNKS)
    def _(turn):
        chunk = lax.rem(turn + 1, CHUNKS)
        start = pl.multiple_of(chunk * LAG, LAG)
        rows = pl.ds(start, LAG)

        @pl.when(turn == 1)
        def _():
            take_spikes(2)

        @pl.when(turn == CHUNKS - 1)
        def _():
            halo_copy.wait()
            ext[pl.ds(0, LAG), :] = halo[...] * jnp.minimum(tm, 1).astype(BF16)

        @pl.loop(0, UNITS_DEV // WIDE)
        def _(part):
            wide = pl.ds(pl.multiple_of(part * WIDE, WIDE), WIDE)
            both = jnp.dot(
                blend_filter[...], ext[pl.ds(start, 2 * LAG), wide], preferred_element_type=F32
            )
            mixed[rows, wide] = (both[:LAG] + both[LAG:]).astype(BF16)

        @pl.loop(1, PEERS + 1)
        def _(visit):
            step = offset(visit)
            owner = ahead(step)
            low, high = named[owner * CAP], named[owner * CAP + 1]

            def weight_of(s, tile):
                at = jnp.int32(ENTRIES)
                for f in range(FAN):
                    at = jnp.where(target[f, s] == tile, s * FAN + f, at)
                return weights[at]

            total = jnp.zeros((LAG, WIDE), F32)
            for s in range(0, TILES_DEV, 2):
                block = jnp.concatenate(
                    [
                        jnp.concatenate([weight_of(s, low), weight_of(s, high)], axis=1),
                        jnp.concatenate([weight_of(s + 1, low), weight_of(s + 1, high)], axis=1),
                    ],
                    axis=0,
                )
                total = total + jnp.dot(
                    mixed[rows, s * TILE : (s + 2) * TILE], block, preferred_element_type=F32
                )
            partial_out[chunk, step * CAP] = total[:, :TILE].astype(BF16)
            partial_out[chunk, step * CAP + 1] = total[:, TILE:].astype(BF16)

            @pl.when(step > 0)
            def _():
                partial_copy(chunk, step).start()

    @pl.loop(1, PEERS)
    def _(step):
        names_copy(step).wait()

    for k in range(CAP * PEERS):
        names[0, k] = named[k]
    for load in loads[2:]:
        load.wait()

    @pl.loop(0, CHUNKS)
    def _(turn):
        chunk = lax.rem(turn + 1, CHUNKS)
        start = pl.multiple_of(chunk * LAG, LAG)
        rows = pl.ds(start, LAG)
        spike_rows = pl.ds(pl.multiple_of(start + LAG, LAG), LAG)

        for k in range(CAP):
            stage[k] = partial_out[chunk, k]

        @pl.loop(1, PEERS)
        def _(step):
            partial_copy(chunk, step).wait_recv()
            for k in range(CAP):
                stage[step * CAP + k] = partial_in[chunk, step * CAP + k]

        @pl.loop(0, UNITS_DEV // WIDE)
        def _(part):
            left = pl.multiple_of(part * WIDE, WIDE)
            wide = pl.ds(left, WIDE)
            hist[...] = jnp.dot(
                toeplitz[...], ext[pl.ds(start, 2 * LAG), wide], preferred_element_type=F32
            )
            drive = bias[:, wide] + lax.dot_general(
                stim[:, rows], filt[:, wide], (((0,), (0,)), ((), ())), preferred_element_type=F32
            )
            for half in range(2):
                inner = slice(half * TILE, (half + 1) * TILE)
                cols = pl.ds(pl.multiple_of(left + half * TILE, TILE), TILE)
                tile = unit * TILES_DEV + part * 2 + half

                logit = drive[:, inner]
                for b in range(NB):
                    h = hist[b * LAG : (b + 1) * LAG, inner]
                    logit = logit + hist_weight[b : b + 1, cols] * h
                coupling = jnp.zeros((LAG, TILE), F32)
                for step in range(PEERS):
                    first = names[step, unit * CAP]
                    second = names[step, unit * CAP + 1]
                    at = jnp.where(
                        first == tile,
                        step * CAP,
                        jnp.where(second == tile, step * CAP + 1, SLOTS),
                    )
                    coupling = coupling + stage[at].astype(F32)
                resid = ext[spike_rows, cols].astype(F32) - jnp.exp(logit + coupling)
                rounded = resid.astype(BF16)
                resid_tiles[part * 2 + half] = rounded
                resid_rows[:, cols] = rounded
                stats[NB : NB + 1, cols] += jnp.sum(resid, axis=0, keepdims=True)
                for b in range(NB):
                    h = hist[b * LAG : (b + 1) * LAG, inner]
                    stats[b : b + 1, cols] += jnp.sum(h * resid, axis=0, keepdims=True)

        @pl.loop(1, PEERS + 1)
        def _(visit):
            step = offset(visit)
            for k in range(CAP):
                tile = names[step, unit * CAP + k] - unit * TILES_DEV
                tile = jnp.minimum(jnp.maximum(tile, 0), TILES_DEV - 1)
                resid_out[chunk, step * CAP + k] = resid_tiles[tile]

            @pl.when(step > 0)
            def _():
                resid_copy(chunk, step).start()

        for block in range(TM):
            stim_sum[block] += lax.dot_general(
                stim[:, rows],
                resid_rows[:, block * TILE : (block + 1) * TILE],
                (((1,), (0,)), ((), ())),
                preferred_element_type=F32,
            )

    def stats_copy(step):
        return pltpu.make_async_remote_copy(
            src_ref=stats,
            dst_ref=stats_in.at[tm],
            send_sem=sem_stats_send.at[step],
            recv_sem=sem_stats_recv.at[step],
            device_id=(unit, around(step)),
            device_id_type=MESH,
        )

    def stim_copy(step):
        return pltpu.make_async_remote_copy(
            src_ref=stim_sum.at[around(step)],
            dst_ref=stim_in.at[step],
            send_sem=sem_stim_send.at[step],
            recv_sem=sem_stim_recv.at[step],
            device_id=(unit, around(step)),
            device_id_type=MESH,
        )

    @pl.loop(1, TM)
    def _(step):
        stats_copy(step).start()
        stim_copy(step).start()

    def slot_of(s, f):
        owner = target[f, s] // TILES_DEV
        step_x = lax.rem(owner // SIDE - here_x + SIDE, SIDE)
        step_y = lax.rem(owner % SIDE - here_y + SIDE, SIDE)
        rank = (target[f, s] == named[owner * CAP + 1]).astype(jnp.int32)
        return (step_x * SIDE + step_y) * CAP + rank

    @pl.loop(0, CHUNKS)
    def _(turn):
        chunk = lax.rem(turn + 1, CHUNKS)
        rows = pl.ds(pl.multiple_of(chunk * LAG, LAG), LAG)

        for k in range(CAP):
            stage[k] = resid_out[chunk, k]

        @pl.loop(1, PEERS)
        def _(step):
            resid_copy(chunk, step).wait_recv()
            partial_copy(chunk, step).wait_send()
            for k in range(CAP):
                stage[step * CAP + k] = resid_in[chunk, step * CAP + k]

        for s in range(TILES_DEV):
            chosen = jnp.concatenate([stage[slot_of(s, f)] for f in range(FAN)], axis=1)
            grad[s] += lax.dot_general(
                mixed[rows, s * TILE : (s + 1) * TILE],
                chosen,
                (((0,), (0,)), ((), ())),
                preferred_element_type=F32,
            )

    share = TILE // TM

    def pair_copy(z):
        return pltpu.make_async_remote_copy(
            src_ref=grad.at[:, pl.ds(pl.multiple_of((z * 2 + 1 - core) * share, share), share)],
            dst_ref=pair_in.at[z],
            send_sem=sem_pair.at[0, z],
            recv_sem=sem_pair.at[1, z],
            device_id=(unit, here_z * 2 + 1 - core),
            device_id_type=MESH,
        )

    def zed_copy(step):
        z = lax.rem(here_z + step, SIDE)
        return pltpu.make_async_remote_copy(
            src_ref=pair_out.at[z],
            dst_ref=zed_in.at[step],
            send_sem=sem_zed.at[0, step],
            recv_sem=sem_zed.at[1, step],
            device_id=(unit, z * 2 + core),
            device_id_type=MESH,
        )

    for step in (1, 2, 3, 0):
        pair_copy(lax.rem(here_z + step, SIDE)).start()

    def both(z):
        kept = pl.ds(pl.multiple_of((z * 2 + core) * share, share), share)
        return grad[:, kept, :] + pair_in[z]

    for step in (1, 2, 3):
        z = lax.rem(here_z + step, SIDE)
        pair_copy(z).wait_recv()
        pair_out[z] = both(z).astype(pair_out.dtype)
        zed_copy(step).start()
    pair_copy(here_z).wait_recv()
    final = both(here_z)

    stats_in[tm] = stats[...]

    @pl.loop(1, TM)
    def _(step):
        stats_copy(step).wait()
        stim_copy(step).wait()

    total = stats_in[0]
    for block in range(1, TM):
        total = total + stats_in[block]
    out_stats[...] = total
    stim_total = stim_sum[tm]
    for step in range(1, TM):
        stim_total = stim_total + stim_in[step]
    out_stim[...] = stim_total

    @pl.loop(0, CHUNKS)
    def _(chunk):
        @pl.loop(1, PEERS)
        def _(step):
            resid_copy(chunk, step).wait_send()

    @pl.loop(0, SIDE)
    def _(z):
        pair_copy(z).wait_send()

    for step in (1, 2, 3):
        zed_copy(step).wait()
        final = final + zed_in[step].astype(F32)
    out_coupling[...] = final


def finish_kernel(stats, stim, coupling, out_bias, out_hist, out_stim, out_coupling):
    time_total = float(TIME_DEV * TM)
    out_hist[...] = stats[:NB, :] / time_total
    out_bias[...] = stats[NB : NB + 1, :] / time_total
    out_stim[...] = stim[...] / time_total
    for f in range(FAN):
        out_coupling[:, f] = coupling[:, :, f * TILE : (f + 1) * TILE] / time_total


def shards(
    spikes, stimulus, bias, hist_weight, stim_filter, coupling_mix, coupling_target, coupling_weight
):
    smem = pl.BlockSpec(memory_space=pltpu.SMEM)
    vmem = pl.BlockSpec(memory_space=pltpu.VMEM)
    anywhere = pl.BlockSpec(memory_space=pl.ANY)
    dma = pltpu.SemaphoreType.DMA
    share = TILE // TM
    sums = pl.pallas_call(
        main_kernel,
        out_shape=[
            jax.ShapeDtypeStruct((16, UNITS_DEV), F32),
            jax.ShapeDtypeStruct((STIM, TILE), F32),
            jax.ShapeDtypeStruct((TILES_DEV, share, FAN * TILE), F32),
        ],
        in_specs=[smem] * 2 + [anywhere] * 7,
        out_specs=[vmem] * 3,
        scratch_shapes=[
            pltpu.VMEM((TIME_DEV, UNITS_DEV), jnp.int32),
            pltpu.VMEM((STIM, TIME_DEV), BF16),
            pltpu.VMEM((1, UNITS_DEV), F32),
            pltpu.VMEM((NB, UNITS_DEV), F32),
            pltpu.VMEM((STIM, UNITS_DEV), BF16),
            pltpu.VMEM((NB * LAG, 2 * LAG), BF16),
            pltpu.VMEM((2 * LAG, 2 * LAG), BF16),
            pltpu.VMEM((TIME_DEV + LAG, UNITS_DEV), BF16),
            pltpu.VMEM((LAG, UNITS_DEV), BF16),
            pltpu.VMEM((ENTRIES + 1, TILE, TILE), BF16),
            pltpu.VMEM((NB * LAG, WIDE), F32),
            pltpu.VMEM((TIME_DEV, UNITS_DEV), BF16),
            pltpu.VMEM((CHUNKS, SLOTS, LAG, TILE), BF16),
            pltpu.VMEM((CHUNKS, SLOTS, LAG, TILE), BF16),
            pltpu.VMEM((SLOTS + 1, LAG, TILE), BF16),
            pltpu.VMEM((TILES_DEV, LAG, TILE), BF16),
            pltpu.VMEM((LAG, UNITS_DEV), BF16),
            pltpu.VMEM((CHUNKS, SLOTS, LAG, TILE), BF16),
            pltpu.VMEM((CHUNKS, SLOTS, LAG, TILE), BF16),
            pltpu.SMEM((SLOTS,), jnp.int32),
            pltpu.SMEM((PEERS, SLOTS), jnp.int32),
            pltpu.VMEM((TILES_DEV, TILE, FAN * TILE), F32),
            pltpu.VMEM((16, UNITS_DEV), F32),
            pltpu.VMEM((TM, 16, UNITS_DEV), F32),
            pltpu.VMEM((TM, STIM, TILE), F32),
            pltpu.VMEM((TM, STIM, TILE), F32),
            pltpu.VMEM((SIDE, TILES_DEV, share, FAN * TILE), F32),
            pltpu.VMEM((SIDE, TILES_DEV, share, FAN * TILE), BF16),
            pltpu.VMEM((SIDE, TILES_DEV, share, FAN * TILE), BF16),
            dma((6,)),
            dma((CHUNKS,)),
            dma((2,)),
            dma((2, PEERS)),
            dma((CHUNKS, PEERS)),
            dma((CHUNKS, PEERS)),
            dma((CHUNKS, PEERS)),
            dma((CHUNKS, PEERS)),
            dma((TM,)),
            dma((TM,)),
            dma((TM,)),
            dma((TM,)),
            dma((2, SIDE)),
            dma((2, SIDE)),
        ],
        compiler_params=pltpu.CompilerParams(
            collective_id=0, has_side_effects=True, vmem_limit_bytes=56 * 1024 * 1024
        ),
    )(
        coupling_target.T,
        coupling_mix,
        spikes,
        stimulus.T,
        bias.reshape(1, UNITS_DEV),
        hist_weight,
        stim_filter.T,
        coupling_weight.reshape(ENTRIES, TILE, TILE),
        jnp.asarray(toeplitz_table()),
    )
    grad_bias, grad_hist, grad_stim, grad_coupling = pl.pallas_call(
        finish_kernel,
        out_shape=[
            jax.ShapeDtypeStruct((1, UNITS_DEV), F32),
            jax.ShapeDtypeStruct((NB, UNITS_DEV), F32),
            jax.ShapeDtypeStruct((STIM, TILE), F32),
            jax.ShapeDtypeStruct((TILES_DEV, FAN, share, TILE), F32),
        ],
        in_specs=[vmem] * 3,
        out_specs=[vmem] * 4,
    )(*sums)
    return (grad_bias.reshape(UNITS_DEV), grad_hist, grad_stim.T, grad_coupling)


def solution(mesh):
    return jax.shard_map(
        shards,
        mesh=mesh,
        in_specs=(
            P("tm", "unit"),
            P("tm", None),
            P("unit"),
            P(None, "unit"),
            P("unit", None),
            P(),
            P("unit", None),
            P("unit", None, None, None),
        ),
        out_specs=(
            P("unit"),
            P(None, "unit"),
            P(("unit", "tm"), None),
            P("unit", None, "tm", None),
        ),
        check_vma=False,
    )
```

```python
import functools
import math

import jax
import jax.numpy as jnp
import ml_dtypes
import numpy as np
from jax import lax
from jax.experimental import pallas as pl
from jax.experimental.pallas import tpu as pltpu
from jax.sharding import PartitionSpec as P

TILE = 128
FAN = 4
CAP = 2
NB = 10
LAG = 128
SIDE = 4
PEERS = SIDE * SIDE
SLOTS = PEERS * CAP
TILES_DEV = 8
UNITS_DEV = TILES_DEV * TILE
TIME_DEV = 512
CHUNKS = TIME_DEV // LAG
STIM = 64
TM = 8
WIDE = 2 * TILE
ENTRIES = TILES_DEV * FAN
MESH = pl.DeviceIdType.MESH
F32 = jnp.float32
BF16 = jnp.bfloat16


def toeplitz_table():
    low = math.log(2.0)
    spacing = (math.log(LAG + 1.0) - low) / (NB - 1)
    stretched = np.log(np.arange(1, LAG + 1) + 1.0)
    centers = low + spacing * np.arange(NB)
    phases = (stretched[None, :] - centers[:, None]) * (math.pi / (2.0 * spacing))
    shapes = 0.5 * (1.0 + np.cos(np.clip(phases, -math.pi, math.pi)))
    basis = (shapes / shapes.sum(axis=1, keepdims=True)).astype(np.float32)
    table = np.zeros((NB, LAG, 2 * LAG), np.float32)
    for row in range(LAG):
        table[:, row, row : row + LAG] = basis[:, ::-1]
    return table.reshape(NB * LAG, 2 * LAG).astype(ml_dtypes.bfloat16)


def main_kernel(
    target,
    mix,
    spikes_hbm,
    stim_hbm,
    bias_hbm,
    hist_weight_hbm,
    filt_hbm,
    weights_hbm,
    toeplitz_hbm,
    out_stats,
    out_stim,
    out_coupling,
    spikes,
    stim,
    bias,
    hist_weight,
    filt,
    toeplitz,
    blend_filter,
    ext,
    halo,
    weights,
    hist,
    mixed,
    partial_out,
    partial_in,
    stage,
    resid_tiles,
    resid_rows,
    resid_out,
    resid_in,
    named,
    names,
    grad,
    stats,
    stats_in,
    stim_sum,
    stim_in,
    pair_in,
    pair_out,
    zed_in,
    final,
    sem_load,
    sem_spikes,
    sem_halo,
    sem_names,
    sem_a_send,
    sem_a_recv,
    sem_b_send,
    sem_b_recv,
    sem_stats,
    sem_stim,
    sem_pair,
    sem_zed,
):
    unit = lax.axis_index("unit")
    tm = lax.axis_index("tm")
    here_x, here_y = unit // SIDE, unit % SIDE
    here_z, core = tm // 2, tm % 2

    def ahead(step):
        return lax.rem(here_x + step // SIDE, SIDE) * SIDE + lax.rem(here_y + step % SIDE, SIDE)

    def behind(step):
        return lax.rem(here_x - step // SIDE + SIDE, SIDE) * SIDE + lax.rem(
            here_y - step % SIDE + SIDE, SIDE
        )

    def offset(turn):
        step = lax.rem(turn * 5, PEERS)
        step_x, step_y = step // SIDE, step % SIDE
        step_x = lax.rem(step_x + core * (SIDE - step_x + SIDE - step_x), SIDE)
        step_y = lax.rem(step_y + core * (SIDE - step_y + SIDE - step_y), SIDE)
        return step_x * SIDE + step_y

    def around(step):
        return lax.rem(tm + step, TM)

    barrier = pltpu.get_barrier_semaphore()

    @pl.loop(1, PEERS)
    def _(step):
        pl.semaphore_signal(barrier, inc=1, device_id=(ahead(step), tm), device_id_type=MESH)

    @pl.loop(1, TM)
    def _(step):
        pl.semaphore_signal(barrier, inc=1, device_id=(unit, around(step)), device_id_type=MESH)

    def spikes_copy(chunk):
        rows = pl.ds(pl.multiple_of(chunk * LAG, LAG), LAG)
        return pltpu.make_async_copy(
            spikes_hbm.at[rows, :], spikes.at[rows, :], sem_spikes.at[chunk]
        )

    loads = [
        pltpu.make_async_copy(source, place, sem_load.at[k])
        for k, (source, place) in enumerate(
            (
                (toeplitz_hbm, toeplitz),
                (weights_hbm, weights.at[pl.ds(0, ENTRIES)]),
                (stim_hbm, stim),
                (bias_hbm, bias),
                (hist_weight_hbm, hist_weight),
                (filt_hbm, filt),
            )
        )
    ]
    spikes_copy(0).start()
    spikes_copy(1).start()
    loads[0].start()
    spikes_copy(3).start()
    loads[1].start()
    spikes_copy(2).start()
    for load in loads[2:]:
        load.start()

    @pl.loop(0, PEERS)
    def _(owner):
        first, last = owner * TILES_DEV, owner * TILES_DEV + TILES_DEV - 1
        low, high = jnp.int32(PEERS * TILES_DEV), jnp.int32(-1)
        for s in range(TILES_DEV):
            for f in range(FAN):
                tile = target[f, s]
                low = jnp.where(tile >= first, jnp.minimum(low, tile), low)
                high = jnp.where(tile <= last, jnp.maximum(high, tile), high)
        named[owner * CAP] = low
        named[owner * CAP + 1] = high

    weights[ENTRIES] = jnp.zeros((TILE, TILE), BF16)
    stage[SLOTS] = jnp.zeros((TILE, TILE), BF16)
    stats[...] = jnp.zeros_like(stats)
    stim_sum[...] = jnp.zeros_like(stim_sum)
    grad[...] = jnp.zeros_like(grad)

    def take_spikes(chunk):
        spikes_copy(chunk).wait()
        ext[(chunk + 1) * LAG : (chunk + 2) * LAG, :] = spikes[
            chunk * LAG : (chunk + 1) * LAG, :
        ].astype(BF16)

    take_spikes(0)
    take_spikes(1)
    loads[0].wait()
    combined = jnp.zeros((LAG, 2 * LAG), F32)
    for b in range(NB):
        combined = combined + mix[b] * toeplitz[b * LAG : (b + 1) * LAG, :].astype(F32)
    upper = combined.astype(BF16)
    blend_filter[:LAG, :] = upper
    blend_filter[LAG:, :] = (combined - upper.astype(F32)).astype(BF16)

    def mix_rows(chunk):
        start = pl.multiple_of(chunk * LAG, LAG)
        for part in range(UNITS_DEV // WIDE):
            wide = slice(part * WIDE, (part + 1) * WIDE)
            both = jnp.dot(
                blend_filter[...], ext[pl.ds(start, 2 * LAG), wide], preferred_element_type=F32
            )
            mixed[pl.ds(start, LAG), wide] = (both[:LAG] + both[LAG:]).astype(BF16)

    mix_rows(1)
    take_spikes(3)
    loads[1].wait()
    pl.semaphore_wait(barrier, PEERS - 1 + TM - 1)

    halo_copy = pltpu.make_async_remote_copy(
        src_ref=ext.at[pl.ds(TIME_DEV, LAG)],
        dst_ref=halo,
        send_sem=sem_halo.at[0],
        recv_sem=sem_halo.at[1],
        device_id=(unit, around(1)),
        device_id_type=MESH,
    )

    def names_copy(step):
        return pltpu.make_async_remote_copy(
            src_ref=named,
            dst_ref=names.at[step],
            send_sem=sem_names.at[0, step],
            recv_sem=sem_names.at[1, step],
            device_id=(ahead(step), tm),
            device_id_type=MESH,
        )

    def partial_copy(chunk, step, count=1):
        pair = pl.ds(step * CAP, count * CAP)
        return pltpu.make_async_remote_copy(
            src_ref=partial_out.at[chunk, pair],
            dst_ref=partial_in.at[chunk, pair],
            send_sem=sem_a_send.at[chunk],
            recv_sem=sem_a_recv.at[chunk],
            device_id=(ahead(step), tm),
            device_id_type=MESH,
        )

    def resid_copy(chunk, step, count=1):
        pair = pl.ds(step * CAP, count * CAP)
        return pltpu.make_async_remote_copy(
            src_ref=resid_out.at[chunk, pair],
            dst_ref=resid_in.at[chunk, pair],
            send_sem=sem_b_send.at[chunk],
            recv_sem=sem_b_recv.at[chunk],
            device_id=(behind(step), tm),
            device_id_type=MESH,
        )

    @pl.loop(0, CHUNKS)
    def _(turn):
        chunk = lax.rem(turn + 1, CHUNKS)
        start = pl.multiple_of(chunk * LAG, LAG)
        rows = pl.ds(start, LAG)

        @pl.when(turn == 1)
        def _():
            take_spikes(2)

        @pl.when(turn == CHUNKS - 1)
        def _():
            halo_copy.wait()
            ext[pl.ds(0, LAG), :] = halo[...] * jnp.minimum(tm, 1).astype(BF16)

        @pl.when(turn > 0)
        def _():
            mix_rows(chunk)

        @pl.loop(1, PEERS + 1)
        def _(visit):
            step = offset(visit)
            owner = ahead(step)
            low, high = named[owner * CAP], named[owner * CAP + 1]

            def weight_of(s, tile):
                at = jnp.int32(ENTRIES)
                for f in range(FAN):
                    at = jnp.where(target[f, s] == tile, s * FAN + f, at)
                return weights[at]

            total = jnp.zeros((LAG, WIDE), F32)
            for s in range(0, TILES_DEV, 2):
                block = jnp.concatenate(
                    [
                        jnp.concatenate([weight_of(s, low), weight_of(s, high)], axis=1),
                        jnp.concatenate([weight_of(s + 1, low), weight_of(s + 1, high)], axis=1),
                    ],
                    axis=0,
                )
                total = total + jnp.dot(
                    mixed[rows, s * TILE : (s + 2) * TILE], block, preferred_element_type=F32
                )
            partial_out[chunk, step * CAP] = total[:, :TILE].astype(BF16)
            partial_out[chunk, step * CAP + 1] = total[:, TILE:].astype(BF16)

            @pl.when(step > 0)
            def _():
                partial_copy(chunk, step).start()

                @pl.when(turn == 0)
                def _():
                    names_copy(step).start()

        @pl.when(turn == 0)
        def _():
            halo_copy.start()

    @pl.loop(1, PEERS)
    def _(step):
        names_copy(step).wait()

    for k in range(CAP * PEERS):
        names[0, k] = named[k]
    for load in loads[2:]:
        load.wait()

    @pl.loop(0, CHUNKS)
    def _(turn):
        chunk = lax.rem(turn + 1, CHUNKS)
        start = pl.multiple_of(chunk * LAG, LAG)
        rows = pl.ds(start, LAG)
        spike_rows = pl.ds(pl.multiple_of(start + LAG, LAG), LAG)

        for k in range(CAP):
            stage[k] = partial_out[chunk, k]

        partial_copy(chunk, 1, PEERS - 1).wait_recv()
        stage[CAP:SLOTS] = partial_in[chunk, CAP:]

        @pl.loop(0, UNITS_DEV // WIDE)
        def _(part):
            left = pl.multiple_of(part * WIDE, WIDE)
            wide = pl.ds(left, WIDE)
            hist[...] = jnp.dot(
                toeplitz[...], ext[pl.ds(start, 2 * LAG), wide], preferred_element_type=F32
            )
            drive = bias[:, wide] + lax.dot_general(
                stim[:, rows], filt[:, wide], (((0,), (0,)), ((), ())), preferred_element_type=F32
            )
            for half in range(2):
                inner = slice(half * TILE, (half + 1) * TILE)
                cols = pl.ds(pl.multiple_of(left + half * TILE, TILE), TILE)
                tile = unit * TILES_DEV + part * 2 + half

                logit = drive[:, inner]
                for b in range(NB):
                    h = hist[b * LAG : (b + 1) * LAG, inner]
                    logit = logit + hist_weight[b : b + 1, cols] * h
                coupling = jnp.zeros((LAG, TILE), F32)
                for step in range(PEERS):
                    first = names[step, unit * CAP]
                    second = names[step, unit * CAP + 1]
                    at = jnp.where(
                        first == tile,
                        step * CAP,
                        jnp.where(second == tile, step * CAP + 1, SLOTS),
                    )
                    coupling = coupling + stage[at].astype(F32)
                resid = ext[spike_rows, cols].astype(F32) - jnp.exp(logit + coupling)
                rounded = resid.astype(BF16)
                resid_tiles[part * 2 + half] = rounded
                resid_rows[:, cols] = rounded
                stats[NB : NB + 1, cols] += jnp.sum(resid, axis=0, keepdims=True)
                for b in range(NB):
                    h = hist[b * LAG : (b + 1) * LAG, inner]
                    stats[b : b + 1, cols] += jnp.sum(h * resid, axis=0, keepdims=True)

        @pl.loop(1, PEERS + 1)
        def _(visit):
            step = offset(visit)
            for k in range(CAP):
                tile = names[step, unit * CAP + k] - unit * TILES_DEV
                tile = jnp.minimum(jnp.maximum(tile, 0), TILES_DEV - 1)
                resid_out[chunk, step * CAP + k] = resid_tiles[tile]

            @pl.when(step > 0)
            def _():
                resid_copy(chunk, step).start()

        for block in range(TM):
            stim_sum[block] += lax.dot_general(
                stim[:, rows],
                resid_rows[:, block * TILE : (block + 1) * TILE],
                (((1,), (0,)), ((), ())),
                preferred_element_type=F32,
            )

    def stats_copy(step):
        return pltpu.make_async_remote_copy(
            src_ref=stats,
            dst_ref=stats_in.at[step],
            send_sem=sem_stats.at[0],
            recv_sem=sem_stats.at[1],
            device_id=(unit, around(step)),
            device_id_type=MESH,
        )

    def stim_copy(step):
        return pltpu.make_async_remote_copy(
            src_ref=stim_sum.at[around(step)],
            dst_ref=stim_in.at[step],
            send_sem=sem_stim.at[0],
            recv_sem=sem_stim.at[1],
            device_id=(unit, around(step)),
            device_id_type=MESH,
        )

    def all_arrived(place, sems):
        others = place.at[pl.ds(1, TM - 1)]
        pltpu.make_async_remote_copy(
            src_ref=others,
            dst_ref=others,
            send_sem=sems.at[0],
            recv_sem=sems.at[1],
            device_id=(unit, around(1)),
            device_id_type=MESH,
        ).wait()

    @pl.loop(1, TM)
    def _(step):
        stats_copy(step).start()
        stim_copy(step).start()

    def slot_of(s, f):
        owner = target[f, s] // TILES_DEV
        step_x = lax.rem(owner // SIDE - here_x + SIDE, SIDE)
        step_y = lax.rem(owner % SIDE - here_y + SIDE, SIDE)
        rank = (target[f, s] == named[owner * CAP + 1]).astype(jnp.int32)
        return (step_x * SIDE + step_y) * CAP + rank

    def take_resid(chunk):
        for k in range(CAP):
            stage[k] = resid_out[chunk, k]
        partial_copy(chunk, 1, PEERS - 1).wait_send()
        resid_copy(chunk, 1, PEERS - 1).wait_recv()
        stage[CAP:SLOTS] = resid_in[chunk, CAP:]

    def add_grad(chunk, s):
        chosen = jnp.concatenate([stage[slot_of(s, f)] for f in range(FAN)], axis=1)
        grad[s] += lax.dot_general(
            mixed[pl.ds(pl.multiple_of(chunk * LAG, LAG), LAG), s * TILE : (s + 1) * TILE],
            chosen,
            (((0,), (0,)), ((), ())),
            preferred_element_type=F32,
        )

    @pl.loop(1, CHUNKS)
    def _(chunk):
        take_resid(chunk)
        for s in range(TILES_DEV):
            add_grad(chunk, s)

    share = TILE // TM
    half_tiles = TILES_DEV // 2

    def pair_copy(half, z):
        given = pl.ds(pl.multiple_of((z * 2 + 1 - core) * share, share), share)
        return pltpu.make_async_remote_copy(
            src_ref=grad.at[pl.ds(half * half_tiles, half_tiles), given],
            dst_ref=pair_in.at[half, z],
            send_sem=sem_pair.at[0, half, z],
            recv_sem=sem_pair.at[1, half, z],
            device_id=(unit, here_z * 2 + 1 - core),
            device_id_type=MESH,
        )

    def zed_copy(half, step):
        z = lax.rem(here_z + step, SIDE)
        return pltpu.make_async_remote_copy(
            src_ref=pair_out.at[half, z],
            dst_ref=zed_in.at[half, step],
            send_sem=sem_zed.at[0, half, step],
            recv_sem=sem_zed.at[1, half, step],
            device_id=(unit, z * 2 + core),
            device_id_type=MESH,
        )

    def both(half, z):
        kept = pl.ds(pl.multiple_of((z * 2 + core) * share, share), share)
        return grad[half * half_tiles : (half + 1) * half_tiles, kept, :] + pair_in[half, z]

    take_resid(0)
    for half in range(2):
        for s in range(half * half_tiles, (half + 1) * half_tiles):
            add_grad(0, s)
        for step in (2, 1, 3, 0):
            pair_copy(half, lax.rem(here_z + step, SIDE)).start()
    for half in range(2):
        for step in (2, 1, 3):
            z = lax.rem(here_z + step, SIDE)
            pair_copy(half, z).wait_recv()
            pair_out[half, z] = both(half, z).astype(pair_out.dtype)
            zed_copy(half, step).start()
    for half in range(2):
        pair_copy(half, here_z).wait_recv()
        final[half * half_tiles : (half + 1) * half_tiles] = both(half, here_z)

    all_arrived(stats_in, sem_stats)
    all_arrived(stim_in, sem_stim)
    stats_in[0] = stats[...]
    total = stats_in[tm]
    for block in range(1, TM):
        total = total + stats_in[lax.rem(tm - block + TM, TM)]
    out_stats[...] = total
    stim_total = stim_sum[tm]
    for step in range(1, TM):
        stim_total = stim_total + stim_in[step]
    out_stim[...] = stim_total

    for chunk in range(CHUNKS):
        resid_copy(chunk, 1, PEERS - 1).wait_send()

    for half in range(2):
        for z in range(SIDE):
            pair_copy(half, z).wait_send()
    for half in range(2):
        tiles = slice(half * half_tiles, (half + 1) * half_tiles)
        total = final[tiles]
        for step in (1, 2, 3):
            zed_copy(half, step).wait()
            total = total + zed_in[half, step].astype(F32)
        out_coupling[tiles] = total


def finish_kernel(stats, stim, coupling, out_bias, out_hist, out_stim, out_coupling):
    time_total = float(TIME_DEV * TM)
    out_hist[...] = stats[:NB, :] / time_total
    out_bias[...] = stats[NB : NB + 1, :] / time_total
    out_stim[...] = stim[...] / time_total
    for f in range(FAN):
        out_coupling[:, f] = coupling[:, :, f * TILE : (f + 1) * TILE] / time_total


def shards(
    spikes, stimulus, bias, hist_weight, stim_filter, coupling_mix, coupling_target, coupling_weight
):
    smem = pl.BlockSpec(memory_space=pltpu.SMEM)
    vmem = pl.BlockSpec(memory_space=pltpu.VMEM)
    anywhere = pl.BlockSpec(memory_space=pl.ANY)
    dma = pltpu.SemaphoreType.DMA
    share = TILE // TM
    sums = pl.pallas_call(
        main_kernel,
        out_shape=[
            jax.ShapeDtypeStruct((16, UNITS_DEV), F32),
            jax.ShapeDtypeStruct((STIM, TILE), F32),
            jax.ShapeDtypeStruct((TILES_DEV, share, FAN * TILE), F32),
        ],
        in_specs=[smem] * 2 + [anywhere] * 7,
        out_specs=[vmem] * 3,
        scratch_shapes=[
            pltpu.VMEM((TIME_DEV, UNITS_DEV), jnp.int32),
            pltpu.VMEM((STIM, TIME_DEV), BF16),
            pltpu.VMEM((1, UNITS_DEV), F32),
            pltpu.VMEM((NB, UNITS_DEV), F32),
            pltpu.VMEM((STIM, UNITS_DEV), BF16),
            pltpu.VMEM((NB * LAG, 2 * LAG), BF16),
            pltpu.VMEM((2 * LAG, 2 * LAG), BF16),
            pltpu.VMEM((TIME_DEV + LAG, UNITS_DEV), BF16),
            pltpu.VMEM((LAG, UNITS_DEV), BF16),
            pltpu.VMEM((ENTRIES + 1, TILE, TILE), BF16),
            pltpu.VMEM((NB * LAG, WIDE), F32),
            pltpu.VMEM((TIME_DEV, UNITS_DEV), BF16),
            pltpu.VMEM((CHUNKS, SLOTS, LAG, TILE), BF16),
            pltpu.VMEM((CHUNKS, SLOTS, LAG, TILE), BF16),
            pltpu.VMEM((SLOTS + 1, LAG, TILE), BF16),
            pltpu.VMEM((TILES_DEV, LAG, TILE), BF16),
            pltpu.VMEM((LAG, UNITS_DEV), BF16),
            pltpu.VMEM((CHUNKS, SLOTS, LAG, TILE), BF16),
            pltpu.VMEM((CHUNKS, SLOTS, LAG, TILE), BF16),
            pltpu.SMEM((SLOTS,), jnp.int32),
            pltpu.SMEM((PEERS, SLOTS), jnp.int32),
            pltpu.VMEM((TILES_DEV, TILE, FAN * TILE), F32),
            pltpu.VMEM((16, UNITS_DEV), F32),
            pltpu.VMEM((TM, 16, UNITS_DEV), F32),
            pltpu.VMEM((TM, STIM, TILE), F32),
            pltpu.VMEM((TM, STIM, TILE), F32),
            pltpu.VMEM((2, SIDE, TILES_DEV // 2, share, FAN * TILE), F32),
            pltpu.VMEM((2, SIDE, TILES_DEV // 2, share, FAN * TILE), BF16),
            pltpu.VMEM((2, SIDE, TILES_DEV // 2, share, FAN * TILE), BF16),
            pltpu.VMEM((TILES_DEV, share, FAN * TILE), F32),
            dma((6,)),
            dma((CHUNKS,)),
            dma((2,)),
            dma((2, PEERS)),
            dma((CHUNKS,)),
            dma((CHUNKS,)),
            dma((CHUNKS,)),
            dma((CHUNKS,)),
            dma((2,)),
            dma((2,)),
            dma((2, 2, SIDE)),
            dma((2, 2, SIDE)),
        ],
        compiler_params=pltpu.CompilerParams(
            collective_id=0, has_side_effects=True, vmem_limit_bytes=56 * 1024 * 1024
        ),
    )(
        coupling_target.T,
        coupling_mix,
        spikes,
        stimulus.T,
        bias.reshape(1, UNITS_DEV),
        hist_weight,
        stim_filter.T,
        coupling_weight.reshape(ENTRIES, TILE, TILE),
        jnp.asarray(toeplitz_table()),
    )
    grad_bias, grad_hist, grad_stim, grad_coupling = pl.pallas_call(
        finish_kernel,
        out_shape=[
            jax.ShapeDtypeStruct((1, UNITS_DEV), F32),
            jax.ShapeDtypeStruct((NB, UNITS_DEV), F32),
            jax.ShapeDtypeStruct((STIM, TILE), F32),
            jax.ShapeDtypeStruct((TILES_DEV, FAN, share, TILE), F32),
        ],
        in_specs=[vmem] * 3,
        out_specs=[vmem] * 4,
    )(*sums)
    return (grad_bias.reshape(UNITS_DEV), grad_hist, grad_stim.T, grad_coupling)


def solution(mesh):
    return jax.shard_map(
        shards,
        mesh=mesh,
        in_specs=(
            P("tm", "unit"),
            P("tm", None),
            P("unit"),
            P(None, "unit"),
            P("unit", None),
            P(),
            P("unit", None),
            P("unit", None, None, None),
        ),
        out_specs=(
            P("unit"),
            P(None, "unit"),
            P(("unit", "tm"), None),
            P("unit", None, "tm", None),
        ),
        check_vma=False,
    )
```

```python
import functools
import math

import jax
import jax.numpy as jnp
import ml_dtypes
import numpy as np
from jax import lax
from jax.experimental import pallas as pl
from jax.experimental.pallas import tpu as pltpu
from jax.sharding import PartitionSpec as P

TILE = 128
FAN = 4
CAP = 2
NB = 10
LAG = 128
SIDE = 4
PEERS = SIDE * SIDE
HALF = LAG // 2
SLOTS = PEERS * CAP
TILES_DEV = 8
UNITS_DEV = TILES_DEV * TILE
TIME_DEV = 512
CHUNKS = TIME_DEV // LAG
STIM = 64
TM = 8
WIDE = 2 * TILE
ENTRIES = TILES_DEV * FAN
MESH = pl.DeviceIdType.MESH
F32 = jnp.float32
BF16 = jnp.bfloat16


def toeplitz_table():
    low = math.log(2.0)
    spacing = (math.log(LAG + 1.0) - low) / (NB - 1)
    stretched = np.log(np.arange(1, LAG + 1) + 1.0)
    centers = low + spacing * np.arange(NB)
    phases = (stretched[None, :] - centers[:, None]) * (math.pi / (2.0 * spacing))
    shapes = 0.5 * (1.0 + np.cos(np.clip(phases, -math.pi, math.pi)))
    basis = (shapes / shapes.sum(axis=1, keepdims=True)).astype(np.float32)
    table = np.zeros((NB, LAG, 2 * LAG), np.float32)
    for row in range(LAG):
        table[:, row, row : row + LAG] = basis[:, ::-1]
    return table.reshape(NB * LAG, 2 * LAG).astype(ml_dtypes.bfloat16)


def main_kernel(
    target,
    mix,
    spikes_hbm,
    stim_hbm,
    bias_hbm,
    hist_weight_hbm,
    filt_hbm,
    weights_hbm,
    toeplitz_hbm,
    out_stats,
    out_stim,
    out_coupling,
    spikes,
    stim,
    bias,
    hist_weight,
    filt,
    toeplitz,
    blend_filter,
    ext,
    halo,
    weights,
    hist,
    mixed,
    partial_out,
    partial_in,
    dense,
    far_in,
    near_in,
    stage,
    resid_rows,
    resid_out,
    got,
    pick,
    resid_in,
    names,
    grad,
    stats,
    stats_in,
    stim_sum,
    stim_in,
    pair_in,
    pair_out,
    zed_in,
    final,
    sem_load,
    sem_spikes,
    sem_halo,
    sem_names,
    sem_send,
    sem_recv,
    sem_stats,
    sem_stim,
    sem_pair,
    sem_zed,
):
    unit = lax.axis_index("unit")
    tm = lax.axis_index("tm")
    here_x, here_y = unit // SIDE, unit % SIDE
    here_z, core = tm // 2, tm % 2

    def device(step_x, step_y):
        return lax.rem(here_x + step_x, SIDE) * SIDE + lax.rem(here_y + step_y, SIDE)

    def ahead(step):
        return device(step // SIDE, step % SIDE)

    def along(half, step):
        return device(0, step) if half else device(step, 0)

    def across(half, step):
        return device(step, 0) if half else device(0, step)

    def around(step):
        return lax.rem(tm + step, TM)

    barrier = pltpu.get_barrier_semaphore()

    @pl.loop(1, PEERS)
    def _(step):
        pl.semaphore_signal(barrier, inc=1, device_id=(ahead(step), tm), device_id_type=MESH)

    @pl.loop(1, TM)
    def _(step):
        pl.semaphore_signal(barrier, inc=1, device_id=(unit, around(step)), device_id_type=MESH)

    def spikes_copy(chunk):
        rows = pl.ds(pl.multiple_of(chunk * LAG, LAG), LAG)
        return pltpu.make_async_copy(
            spikes_hbm.at[rows, :], spikes.at[rows, :], sem_spikes.at[chunk]
        )

    loads = [
        pltpu.make_async_copy(source, place, sem_load.at[k])
        for k, (source, place) in enumerate(
            (
                (toeplitz_hbm, toeplitz),
                (weights_hbm, weights.at[pl.ds(0, ENTRIES)]),
                (stim_hbm, stim),
                (bias_hbm, bias),
                (hist_weight_hbm, hist_weight),
                (filt_hbm, filt),
            )
        )
    ]
    spikes_copy(0).start()
    spikes_copy(1).start()
    loads[0].start()
    spikes_copy(3).start()
    loads[1].start()
    spikes_copy(2).start()
    for load in loads[2:]:
        load.start()

    @pl.loop(0, PEERS)
    def _(owner):
        first, last = owner * TILES_DEV, owner * TILES_DEV + TILES_DEV - 1
        low, high = jnp.int32(PEERS * TILES_DEV), jnp.int32(-1)
        for s in range(TILES_DEV):
            for f in range(FAN):
                tile = target[f, s]
                low = jnp.where(tile >= first, jnp.minimum(low, tile), low)
                high = jnp.where(tile <= last, jnp.maximum(high, tile), high)
        names[unit, owner * CAP] = low
        names[unit, owner * CAP + 1] = high

    weights[ENTRIES] = jnp.zeros((TILE, TILE), BF16)
    for half in range(2):
        stage[half, SLOTS] = jnp.zeros((HALF, TILE), BF16)
    stats[...] = jnp.zeros_like(stats)
    stim_sum[...] = jnp.zeros_like(stim_sum)
    grad[...] = jnp.zeros_like(grad)

    def take_spikes(chunk):
        spikes_copy(chunk).wait()
        ext[(chunk + 1) * LAG : (chunk + 2) * LAG, :] = spikes[
            chunk * LAG : (chunk + 1) * LAG, :
        ].astype(BF16)

    take_spikes(0)
    take_spikes(1)
    loads[0].wait()
    combined = jnp.zeros((LAG, 2 * LAG), F32)
    for b in range(NB):
        combined = combined + mix[b] * toeplitz[b * LAG : (b + 1) * LAG, :].astype(F32)
    upper = combined.astype(BF16)
    blend_filter[:LAG, :] = upper
    blend_filter[LAG:, :] = (combined - upper.astype(F32)).astype(BF16)

    def mix_rows(chunk):
        start = pl.multiple_of(chunk * LAG, LAG)
        for part in range(UNITS_DEV // WIDE):
            wide = slice(part * WIDE, (part + 1) * WIDE)
            both = jnp.dot(
                blend_filter[...], ext[pl.ds(start, 2 * LAG), wide], preferred_element_type=F32
            )
            mixed[pl.ds(start, LAG), wide] = (both[:LAG] + both[LAG:]).astype(BF16)

    def visit_row(chunk, step_x):
        rows = pl.ds(pl.multiple_of(chunk * LAG, LAG), LAG)

        @pl.loop(0, SIDE)
        def _(step_y):
            owner = device(step_x, step_y)
            low, high = names[unit, owner * CAP], names[unit, owner * CAP + 1]

            def weight_of(s, tile):
                at = jnp.int32(ENTRIES)
                for f in range(FAN):
                    at = jnp.where(target[f, s] == tile, s * FAN + f, at)
                return weights[at]

            total = jnp.zeros((LAG, WIDE), F32)
            for s in range(0, TILES_DEV, 2):
                block = jnp.concatenate(
                    [
                        jnp.concatenate([weight_of(s, low), weight_of(s, high)], axis=1),
                        jnp.concatenate([weight_of(s + 1, low), weight_of(s + 1, high)], axis=1),
                    ],
                    axis=0,
                )
                total = total + jnp.dot(
                    mixed[rows, s * TILE : (s + 2) * TILE], block, preferred_element_type=F32
                )
            rounded = total.astype(BF16)
            for k in range(CAP):
                piece = rounded[:, k * TILE : (k + 1) * TILE]
                partial_out[chunk, 0, step_x, step_y, k] = piece[:HALF]
                partial_out[chunk, 1, step_y, step_x, k] = piece[HALF:]

    order = (1 + 2 * core, 3 - 2 * core, 2)
    mix_rows(1)
    loads[1].wait()
    visit_row(1, order[0])
    take_spikes(3)
    pl.semaphore_wait(barrier, PEERS - 1 + TM - 1)

    halo_copy = pltpu.make_async_remote_copy(
        src_ref=ext.at[pl.ds(TIME_DEV, LAG)],
        dst_ref=halo,
        send_sem=sem_halo.at[0],
        recv_sem=sem_halo.at[1],
        device_id=(unit, around(1)),
        device_id_type=MESH,
    )

    def names_copy(step):
        return pltpu.make_async_remote_copy(
            src_ref=names.at[unit],
            dst_ref=names.at[unit],
            send_sem=sem_names.at[0, step],
            recv_sem=sem_names.at[1, step],
            device_id=(ahead(step), tm),
            device_id_type=MESH,
        )

    def copy(source, place, kind, chunk, receiver):
        return pltpu.make_async_remote_copy(
            src_ref=source,
            dst_ref=place,
            send_sem=sem_send.at[kind],
            recv_sem=sem_recv.at[kind, chunk],
            device_id=(receiver, tm),
            device_id_type=MESH,
        )

    def arrived(place, kind, chunk):
        copy(place, place, kind, chunk, along(0, 1)).wait_recv()

    def lower(half_ref):
        return half_ref.at[pl.ds(0, TILES_DEV // 2)]

    def upper(half_ref):
        return half_ref.at[pl.ds(TILES_DEV // 2, TILES_DEV // 2)]

    def send_partials(turn, chunk):
        @pl.when(turn == 1)
        def _():
            take_spikes(2)

        @pl.when(turn == CHUNKS - 1)
        def _():
            halo_copy.wait()
            ext[pl.ds(0, LAG), :] = halo[...] * jnp.minimum(tm, 1).astype(BF16)

        @pl.when(turn > 0)
        def _():
            mix_rows(chunk)
            visit_row(chunk, order[0])

        def send(half, step):
            copy(
                partial_out.at[chunk, half, step],
                partial_in.at[chunk, half, step],
                0,
                chunk,
                along(half, step),
            ).start()

        send(0, order[0])
        for step in order[1:]:
            visit_row(chunk, step)
            send(0, step)
        visit_row(chunk, 0)
        for step in order:
            send(1, step)

        @pl.when(turn == 0)
        def _():
            @pl.loop(1, PEERS)
            def _(step):
                names_copy(step).start()

            halo_copy.start()

    def add_sources(chunk):
        arrived(partial_in.at[chunk, :, pl.ds(1, SIDE - 1)], 0, chunk)
        for half in range(2):
            stage[half, : SLOTS // SIDE] = partial_out[chunk, half, 0].reshape(
                SLOTS // SIDE, HALF, TILE
            )
            stage[half, SLOTS // SIDE : SLOTS] = partial_in[chunk, half, 1:].reshape(
                SLOTS - SLOTS // SIDE, HALF, TILE
            )

            @pl.loop(0, SIDE)
            def _(step):
                owner = across(half, step)

                @pl.loop(0, TILES_DEV)
                def _(local):
                    tile = owner * TILES_DEV + local
                    total = jnp.zeros((HALF, TILE), F32)
                    for back in range(SIDE):
                        source = along(half, (SIDE - back) % SIDE)
                        first = back * (SIDE * CAP) + step * CAP
                        at = jnp.where(
                            names[source, owner * CAP] == tile,
                            first,
                            jnp.where(names[source, owner * CAP + 1] == tile, first + 1, SLOTS),
                        )
                        total = total + stage[half, at].astype(F32)
                    dense[chunk, half, step, local] = total.astype(BF16)

            far = dense.at[chunk, half, 2]
            copy(lower(far), far_in.at[chunk, half, 0], 1, chunk, across(half, 1)).start()
            copy(upper(far), far_in.at[chunk, half, 1], 1, chunk, across(half, 3)).start()

    def pass_sums(chunk):
        arrived(far_in.at[chunk], 1, chunk)
        middle = TILES_DEV // 2
        for half in range(2):
            dense[chunk, half, 1, :middle] = (
                dense[chunk, half, 1, :middle].astype(F32) + far_in[chunk, half, 0].astype(F32)
            ).astype(BF16)
            dense[chunk, half, 3, middle:] = (
                dense[chunk, half, 3, middle:].astype(F32) + far_in[chunk, half, 1].astype(F32)
            ).astype(BF16)
            for place, step in ((0, 1), (1, 3)):
                copy(
                    dense.at[chunk, half, step],
                    near_in.at[chunk, half, place],
                    2,
                    chunk,
                    across(half, step),
                ).start()

    def make_resid(chunk):
        start = pl.multiple_of(chunk * LAG, LAG)
        rows = pl.ds(start, LAG)
        spike_rows = pl.ds(pl.multiple_of(start + LAG, LAG), LAG)
        arrived(near_in.at[chunk], 2, chunk)

        @pl.loop(0, UNITS_DEV // WIDE)
        def _(part):
            left = pl.multiple_of(part * WIDE, WIDE)
            wide = pl.ds(left, WIDE)
            hist[...] = jnp.dot(
                toeplitz[...], ext[pl.ds(start, 2 * LAG), wide], preferred_element_type=F32
            )
            drive = bias[:, wide] + lax.dot_general(
                stim[:, rows], filt[:, wide], (((0,), (0,)), ((), ())), preferred_element_type=F32
            )
            for side in range(2):
                inner = slice(side * TILE, (side + 1) * TILE)
                cols = pl.ds(pl.multiple_of(left + side * TILE, TILE), TILE)
                tile = part * 2 + side
                logit = drive[:, inner]
                for b in range(NB):
                    h = hist[b * LAG : (b + 1) * LAG, inner]
                    logit = logit + hist_weight[b : b + 1, cols] * h
                coupling = jnp.concatenate(
                    [
                        dense[chunk, half, 0, tile].astype(F32)
                        + near_in[chunk, half, 0, tile].astype(F32)
                        + near_in[chunk, half, 1, tile].astype(F32)
                        for half in range(2)
                    ],
                    axis=0,
                )
                resid = ext[spike_rows, cols].astype(F32) - jnp.exp(logit + coupling)
                rounded = resid.astype(BF16)
                for half in range(2):
                    resid_out[chunk, half, tile] = rounded[half * HALF : (half + 1) * HALF]
                resid_rows[:, cols] = rounded
                stats[NB : NB + 1, cols] += jnp.sum(resid, axis=0, keepdims=True)
                for b in range(NB):
                    h = hist[b * LAG : (b + 1) * LAG, inner]
                    stats[b : b + 1, cols] += jnp.sum(h * resid, axis=0, keepdims=True)

        for step, place in ((1, 1), (3, 0)):
            for half in range(2):
                copy(
                    resid_out.at[chunk, half],
                    got.at[chunk, half, place],
                    3,
                    chunk,
                    across(half, step),
                ).start()
        for block in range(TM):
            stim_sum[block] += lax.dot_general(
                stim[:, rows],
                resid_rows[:, block * TILE : (block + 1) * TILE],
                (((1,), (0,)), ((), ())),
                preferred_element_type=F32,
            )

    def forward_resid(chunk):
        arrived(got.at[chunk, :, pl.ds(0, 2)], 3, chunk)
        for half in range(2):
            far = got.at[chunk, half, 2]
            copy(
                lower(got.at[chunk, half, 1]), lower(far), 4, chunk, across(half, 1)
            ).start()
            copy(
                upper(got.at[chunk, half, 0]), upper(far), 4, chunk, across(half, 3)
            ).start()

    def send_named(chunk):
        arrived(got.at[chunk, :, 2], 4, chunk)
        for half in range(2):
            stage[half, :TILES_DEV] = resid_out[chunk, half]
            for step, place in ((1, 0), (2, 2), (3, 1)):
                stage[half, step * TILES_DEV : (step + 1) * TILES_DEV] = got[chunk, half, place]
            for receiver in (1, 3, 2, 0):

                @pl.loop(0, SIDE)
                def _(step):
                    owner = across(half, step)
                    for k in range(CAP):
                        local = (
                            names[along(half, receiver), owner * CAP + k] - owner * TILES_DEV
                        )
                        local = jnp.minimum(jnp.maximum(local, 0), TILES_DEV - 1)
                        pick[chunk, half, receiver, step, k] = stage[
                            half, step * TILES_DEV + local
                        ]

                if receiver:
                    copy(
                        pick.at[chunk, half, receiver],
                        resid_in.at[chunk, half, receiver],
                        5,
                        chunk,
                        along(half, receiver),
                    ).start()

    def take_resid(chunk):
        arrived(resid_in.at[chunk, :, pl.ds(1, SIDE - 1)], 5, chunk)
        for half in range(2):
            stage[half, : SLOTS // SIDE] = pick[chunk, half, 0].reshape(SLOTS // SIDE, HALF, TILE)
            stage[half, SLOTS // SIDE : SLOTS] = resid_in[chunk, half, 1:].reshape(
                SLOTS - SLOTS // SIDE, HALF, TILE
            )

    def chosen_tile(s, f):
        owner = target[f, s] // TILES_DEV
        gone_x = lax.rem(owner // SIDE - here_x + SIDE, SIDE)
        gone_y = lax.rem(owner % SIDE - here_y + SIDE, SIDE)
        back_x = lax.rem(SIDE - gone_x, SIDE)
        back_y = lax.rem(SIDE - gone_y, SIDE)
        rank = (target[f, s] == names[unit, owner * CAP + 1]).astype(jnp.int32)
        return jnp.concatenate(
            [
                stage[0, (back_x * SIDE + gone_y) * CAP + rank],
                stage[1, (back_y * SIDE + gone_x) * CAP + rank],
            ],
            axis=0,
        )

    def add_grad(chunk, s):
        grad[s] += lax.dot_general(
            mixed[pl.ds(pl.multiple_of(chunk * LAG, LAG), LAG), s * TILE : (s + 1) * TILE],
            jnp.concatenate([chosen_tile(s, f) for f in range(FAN)], axis=1),
            (((0,), (0,)), ((), ())),
            preferred_element_type=F32,
        )

    def stats_copy(step):
        return pltpu.make_async_remote_copy(
            src_ref=stats,
            dst_ref=stats_in.at[step],
            send_sem=sem_stats.at[0],
            recv_sem=sem_stats.at[1],
            device_id=(unit, around(step)),
            device_id_type=MESH,
        )

    def stim_copy(step):
        return pltpu.make_async_remote_copy(
            src_ref=stim_sum.at[around(step)],
            dst_ref=stim_in.at[step],
            send_sem=sem_stim.at[0],
            recv_sem=sem_stim.at[1],
            device_id=(unit, around(step)),
            device_id_type=MESH,
        )

    def all_arrived(place, sems):
        others = place.at[pl.ds(1, TM - 1)]
        pltpu.make_async_remote_copy(
            src_ref=others,
            dst_ref=others,
            send_sem=sems.at[0],
            recv_sem=sems.at[1],
            device_id=(unit, around(1)),
            device_id_type=MESH,
        ).wait()

    last = CHUNKS - 1

    def during(turn, delay, step):
        @pl.when((turn >= delay) & (turn < delay + CHUNKS))
        def _():
            step(lax.rem(turn - delay + 1, CHUNKS))

    @pl.loop(0, 6 + CHUNKS)
    def _(turn):
        during(turn, 0, functools.partial(send_partials, turn))

        @pl.when(turn == 2)
        def _():
            @pl.loop(1, PEERS)
            def _(step):
                names_copy(step).wait()

            for load in loads[2:]:
                load.wait()

        during(turn, 2, add_sources)
        during(turn, 3, pass_sums)
        during(turn, 4, make_resid)

        @pl.when(turn == 4 + last)
        def _():
            @pl.loop(1, TM)
            def _(step):
                stats_copy(step).start()
                stim_copy(step).start()

        during(turn, 5, forward_resid)
        during(turn, 6, send_named)

        @pl.when(turn >= 7)
        def _():
            chunk = lax.rem(turn - 7 + 1, CHUNKS)
            take_resid(chunk)
            for s in range(TILES_DEV):
                add_grad(chunk, s)

    share = TILE // TM
    half_tiles = TILES_DEV // 2

    def pair_copy(half, z):
        given = pl.ds(pl.multiple_of((z * 2 + 1 - core) * share, share), share)
        return pltpu.make_async_remote_copy(
            src_ref=grad.at[pl.ds(half * half_tiles, half_tiles), given],
            dst_ref=pair_in.at[half, z],
            send_sem=sem_pair.at[0, half, z],
            recv_sem=sem_pair.at[1, half, z],
            device_id=(unit, here_z * 2 + 1 - core),
            device_id_type=MESH,
        )

    def zed_copy(half, step):
        z = lax.rem(here_z + step, SIDE)
        return pltpu.make_async_remote_copy(
            src_ref=pair_out.at[half, z],
            dst_ref=zed_in.at[half, step],
            send_sem=sem_zed.at[0, half, step],
            recv_sem=sem_zed.at[1, half, step],
            device_id=(unit, z * 2 + core),
            device_id_type=MESH,
        )

    def both(half, z):
        kept = pl.ds(pl.multiple_of((z * 2 + core) * share, share), share)
        return grad[half * half_tiles : (half + 1) * half_tiles, kept, :] + pair_in[half, z]

    take_resid(0)
    for half in range(2):
        for s in range(half * half_tiles, (half + 1) * half_tiles):
            add_grad(0, s)
        for step in (2, 1, 3, 0):
            pair_copy(half, lax.rem(here_z + step, SIDE)).start()
    for half in range(2):
        for step in (2, 1, 3):
            z = lax.rem(here_z + step, SIDE)
            pair_copy(half, z).wait_recv()
            pair_out[half, z] = both(half, z).astype(pair_out.dtype)
            zed_copy(half, step).start()
    for half in range(2):
        pair_copy(half, here_z).wait_recv()
        final[half * half_tiles : (half + 1) * half_tiles] = both(half, here_z)

    all_arrived(stats_in, sem_stats)
    all_arrived(stim_in, sem_stim)
    stats_in[0] = stats[...]
    total = stats_in[tm]
    for block in range(1, TM):
        total = total + stats_in[lax.rem(tm - block + TM, TM)]
    out_stats[...] = total
    stim_total = stim_sum[tm]
    for step in range(1, TM):
        stim_total = stim_total + stim_in[step]
    out_stim[...] = stim_total

    others = pl.ds(1, SIDE - 1)
    for kind, place in enumerate(
        (
            partial_in.at[:, :, others],
            far_in,
            near_in,
            got.at[:, :, pl.ds(0, 2)],
            got.at[:, :, 2],
            resid_in.at[:, :, others],
        )
    ):
        copy(place, place, kind, 0, along(0, 1)).wait_send()
    for half in range(2):
        for z in range(SIDE):
            pair_copy(half, z).wait_send()
    for half in range(2):
        tiles = slice(half * half_tiles, (half + 1) * half_tiles)
        total = final[tiles]
        for step in (1, 2, 3):
            zed_copy(half, step).wait()
            total = total + zed_in[half, step].astype(F32)
        out_coupling[tiles] = total


def finish_kernel(stats, stim, coupling, out_bias, out_hist, out_stim, out_coupling):
    time_total = float(TIME_DEV * TM)
    out_hist[...] = stats[:NB, :] / time_total
    out_bias[...] = stats[NB : NB + 1, :] / time_total
    out_stim[...] = stim[...] / time_total
    for f in range(FAN):
        out_coupling[:, f] = coupling[:, :, f * TILE : (f + 1) * TILE] / time_total


def shards(
    spikes, stimulus, bias, hist_weight, stim_filter, coupling_mix, coupling_target, coupling_weight
):
    smem = pl.BlockSpec(memory_space=pltpu.SMEM)
    vmem = pl.BlockSpec(memory_space=pltpu.VMEM)
    anywhere = pl.BlockSpec(memory_space=pl.ANY)
    dma = pltpu.SemaphoreType.DMA
    share = TILE // TM
    sums = pl.pallas_call(
        main_kernel,
        out_shape=[
            jax.ShapeDtypeStruct((16, UNITS_DEV), F32),
            jax.ShapeDtypeStruct((STIM, TILE), F32),
            jax.ShapeDtypeStruct((TILES_DEV, share, FAN * TILE), F32),
        ],
        in_specs=[smem] * 2 + [anywhere] * 7,
        out_specs=[vmem] * 3,
        scratch_shapes=[
            pltpu.VMEM((TIME_DEV, UNITS_DEV), jnp.int32),
            pltpu.VMEM((STIM, TIME_DEV), BF16),
            pltpu.VMEM((1, UNITS_DEV), F32),
            pltpu.VMEM((NB, UNITS_DEV), F32),
            pltpu.VMEM((STIM, UNITS_DEV), BF16),
            pltpu.VMEM((NB * LAG, 2 * LAG), BF16),
            pltpu.VMEM((2 * LAG, 2 * LAG), BF16),
            pltpu.VMEM((TIME_DEV + LAG, UNITS_DEV), BF16),
            pltpu.VMEM((LAG, UNITS_DEV), BF16),
            pltpu.VMEM((ENTRIES + 1, TILE, TILE), BF16),
            pltpu.VMEM((NB * LAG, WIDE), F32),
            pltpu.VMEM((TIME_DEV, UNITS_DEV), BF16),
            pltpu.VMEM((CHUNKS, 2, SIDE, SIDE, CAP, HALF, TILE), BF16),
            pltpu.VMEM((CHUNKS, 2, SIDE, SIDE, CAP, HALF, TILE), BF16),
            pltpu.VMEM((CHUNKS, 2, SIDE, TILES_DEV, HALF, TILE), BF16),
            pltpu.VMEM((CHUNKS, 2, 2, TILES_DEV // 2, HALF, TILE), BF16),
            pltpu.VMEM((CHUNKS, 2, 2, TILES_DEV, HALF, TILE), BF16),
            pltpu.VMEM((2, SLOTS + 1, HALF, TILE), BF16),
            pltpu.VMEM((LAG, UNITS_DEV), BF16),
            pltpu.VMEM((CHUNKS, 2, TILES_DEV, HALF, TILE), BF16),
            pltpu.VMEM((CHUNKS, 2, SIDE - 1, TILES_DEV, HALF, TILE), BF16),
            pltpu.VMEM((CHUNKS, 2, SIDE, SIDE, CAP, HALF, TILE), BF16),
            pltpu.VMEM((CHUNKS, 2, SIDE, SIDE, CAP, HALF, TILE), BF16),
            pltpu.SMEM((PEERS, SLOTS), jnp.int32),
            pltpu.VMEM((TILES_DEV, TILE, FAN * TILE), F32),
            pltpu.VMEM((16, UNITS_DEV), F32),
            pltpu.VMEM((TM, 16, UNITS_DEV), F32),
            pltpu.VMEM((TM, STIM, TILE), F32),
            pltpu.VMEM((TM, STIM, TILE), F32),
            pltpu.VMEM((2, SIDE, TILES_DEV // 2, share, FAN * TILE), F32),
            pltpu.VMEM((2, SIDE, TILES_DEV // 2, share, FAN * TILE), BF16),
            pltpu.VMEM((2, SIDE, TILES_DEV // 2, share, FAN * TILE), BF16),
            pltpu.VMEM((TILES_DEV, share, FAN * TILE), F32),
            dma((6,)),
            dma((CHUNKS,)),
            dma((2,)),
            dma((2, PEERS)),
            dma((6,)),
            dma((6, CHUNKS)),
            dma((2,)),
            dma((2,)),
            dma((2, 2, SIDE)),
            dma((2, 2, SIDE)),
        ],
        compiler_params=pltpu.CompilerParams(
            collective_id=0, has_side_effects=True, vmem_limit_bytes=56 * 1024 * 1024
        ),
    )(
        coupling_target.T,
        coupling_mix,
        spikes,
        stimulus.T,
        bias.reshape(1, UNITS_DEV),
        hist_weight,
        stim_filter.T,
        coupling_weight.reshape(ENTRIES, TILE, TILE),
        jnp.asarray(toeplitz_table()),
    )
    grad_bias, grad_hist, grad_stim, grad_coupling = pl.pallas_call(
        finish_kernel,
        out_shape=[
            jax.ShapeDtypeStruct((1, UNITS_DEV), F32),
            jax.ShapeDtypeStruct((NB, UNITS_DEV), F32),
            jax.ShapeDtypeStruct((STIM, TILE), F32),
            jax.ShapeDtypeStruct((TILES_DEV, FAN, share, TILE), F32),
        ],
        in_specs=[vmem] * 3,
        out_specs=[vmem] * 4,
    )(*sums)
    return (grad_bias.reshape(UNITS_DEV), grad_hist, grad_stim.T, grad_coupling)


def solution(mesh):
    return jax.shard_map(
        shards,
        mesh=mesh,
        in_specs=(
            P("tm", "unit"),
            P("tm", None),
            P("unit"),
            P(None, "unit"),
            P("unit", None),
            P(),
            P("unit", None),
            P("unit", None, None, None),
        ),
        out_specs=(
            P("unit"),
            P(None, "unit"),
            P(("unit", "tm"), None),
            P("unit", None, "tm", None),
        ),
        check_vma=False,
    )
```

```python
import functools
import math

import jax
import jax.numpy as jnp
import ml_dtypes
import numpy as np
from jax import lax
from jax.experimental import pallas as pl
from jax.experimental.pallas import tpu as pltpu
from jax.sharding import PartitionSpec as P

TILE = 128
FAN = 4
CAP = 2
NB = 10
LAG = 128
SIDE = 4
PEERS = SIDE * SIDE
HALF = LAG // 2
SLOTS = PEERS * CAP
TILES_DEV = 8
UNITS_DEV = TILES_DEV * TILE
TIME_DEV = 512
CHUNKS = TIME_DEV // LAG
STIM = 64
TM = 8
WIDE = 2 * TILE
ENTRIES = TILES_DEV * FAN
MESH = pl.DeviceIdType.MESH
F32 = jnp.float32
BF16 = jnp.bfloat16


def toeplitz_table():
    low = math.log(2.0)
    spacing = (math.log(LAG + 1.0) - low) / (NB - 1)
    stretched = np.log(np.arange(1, LAG + 1) + 1.0)
    centers = low + spacing * np.arange(NB)
    phases = (stretched[None, :] - centers[:, None]) * (math.pi / (2.0 * spacing))
    shapes = 0.5 * (1.0 + np.cos(np.clip(phases, -math.pi, math.pi)))
    basis = (shapes / shapes.sum(axis=1, keepdims=True)).astype(np.float32)
    table = np.zeros((NB, LAG, 2 * LAG), np.float32)
    for row in range(LAG):
        table[:, row, row : row + LAG] = basis[:, ::-1]
    return table.reshape(NB * LAG, 2 * LAG).astype(ml_dtypes.bfloat16)


def main_kernel(
    target,
    mix,
    spikes_hbm,
    stim_hbm,
    bias_hbm,
    hist_weight_hbm,
    filt_hbm,
    weights_hbm,
    toeplitz_hbm,
    out_stats,
    out_stim,
    out_coupling,
    spikes,
    stim,
    bias,
    hist_weight,
    filt,
    toeplitz,
    blend_filter,
    ext,
    halo,
    weights,
    hist,
    mixed,
    partial_out,
    partial_in,
    dense,
    far_in,
    near_in,
    stage,
    resid_rows,
    resid_out,
    got,
    pick,
    resid_in,
    names,
    grad,
    stats,
    stats_in,
    stim_sum,
    stim_in,
    pair_in,
    pair_out,
    zed_far,
    zed_in,
    final,
    sem_load,
    sem_spikes,
    sem_halo,
    sem_names,
    sem_send,
    sem_recv,
    sem_stats,
    sem_stim,
    sem_pair,
    sem_far,
    sem_zed,
):
    unit = lax.axis_index("unit")
    tm = lax.axis_index("tm")
    here_x, here_y = unit // SIDE, unit % SIDE
    here_z, core = tm // 2, tm % 2

    def device(step_x, step_y):
        return lax.rem(here_x + step_x, SIDE) * SIDE + lax.rem(here_y + step_y, SIDE)

    def along(half, step):
        return device(0, step) if half else device(step, 0)

    def across(half, step):
        return device(step, 0) if half else device(0, step)

    def around(step):
        return lax.rem(tm + step, TM)

    barrier = pltpu.get_barrier_semaphore()

    for step in range(1, SIDE):
        for half in range(2):
            pl.semaphore_signal(
                barrier, inc=1, device_id=(along(half, step), tm), device_id_type=MESH
            )

    @pl.loop(1, TM)
    def _(step):
        pl.semaphore_signal(barrier, inc=1, device_id=(unit, around(step)), device_id_type=MESH)

    def spikes_copy(chunk):
        rows = pl.ds(pl.multiple_of(chunk * LAG, LAG), LAG)
        return pltpu.make_async_copy(
            spikes_hbm.at[rows, :], spikes.at[rows, :], sem_spikes.at[chunk]
        )

    loads = [
        pltpu.make_async_copy(source, place, sem_load.at[k])
        for k, (source, place) in enumerate(
            (
                (toeplitz_hbm, toeplitz),
                (weights_hbm, weights.at[pl.ds(0, ENTRIES)]),
                (stim_hbm, stim),
                (bias_hbm, bias),
                (hist_weight_hbm, hist_weight),
                (filt_hbm, filt),
            )
        )
    ]
    spikes_copy(0).start()
    spikes_copy(1).start()
    loads[0].start()
    spikes_copy(3).start()
    loads[1].start()
    spikes_copy(2).start()
    for load in loads[2:]:
        load.start()

    @pl.loop(0, PEERS)
    def _(owner):
        first, last = owner * TILES_DEV, owner * TILES_DEV + TILES_DEV - 1
        low, high = jnp.int32(PEERS * TILES_DEV), jnp.int32(-1)
        for s in range(TILES_DEV):
            for f in range(FAN):
                tile = target[f, s]
                low = jnp.where(tile >= first, jnp.minimum(low, tile), low)
                high = jnp.where(tile <= last, jnp.maximum(high, tile), high)
        names[unit, owner * CAP] = low
        names[unit, owner * CAP + 1] = high

    weights[ENTRIES] = jnp.zeros((TILE, TILE), BF16)
    for half in range(2):
        stage[half, SLOTS] = jnp.zeros((HALF, TILE), BF16)
    stats[...] = jnp.zeros_like(stats)
    stim_sum[...] = jnp.zeros_like(stim_sum)
    grad[...] = jnp.zeros_like(grad)

    def take_spikes(chunk):
        spikes_copy(chunk).wait()
        ext[(chunk + 1) * LAG : (chunk + 2) * LAG, :] = spikes[
            chunk * LAG : (chunk + 1) * LAG, :
        ].astype(BF16)

    take_spikes(0)
    take_spikes(1)
    loads[0].wait()
    combined = jnp.zeros((LAG, 2 * LAG), F32)
    for b in range(NB):
        combined = combined + mix[b] * toeplitz[b * LAG : (b + 1) * LAG, :].astype(F32)
    upper = combined.astype(BF16)
    blend_filter[:LAG, :] = upper
    blend_filter[LAG:, :] = (combined - upper.astype(F32)).astype(BF16)

    def mix_rows(chunk):
        start = pl.multiple_of(chunk * LAG, LAG)
        for part in range(UNITS_DEV // WIDE):
            wide = slice(part * WIDE, (part + 1) * WIDE)
            both = jnp.dot(
                blend_filter[...], ext[pl.ds(start, 2 * LAG), wide], preferred_element_type=F32
            )
            mixed[pl.ds(start, LAG), wide] = (both[:LAG] + both[LAG:]).astype(BF16)

    def visit(chunk, count, steps):
        rows = pl.ds(pl.multiple_of(chunk * LAG, LAG), LAG)

        @pl.loop(0, count)
        def _(turn):
            step_x, step_y = steps(turn)
            owner = device(step_x, step_y)
            low, high = names[unit, owner * CAP], names[unit, owner * CAP + 1]

            def weight_of(s, tile):
                at = jnp.int32(ENTRIES)
                for f in range(FAN):
                    at = jnp.where(target[f, s] == tile, s * FAN + f, at)
                return weights[at]

            total = jnp.zeros((LAG, WIDE), F32)
            for s in range(0, TILES_DEV, 2):
                block = jnp.concatenate(
                    [
                        jnp.concatenate([weight_of(s, low), weight_of(s, high)], axis=1),
                        jnp.concatenate([weight_of(s + 1, low), weight_of(s + 1, high)], axis=1),
                    ],
                    axis=0,
                )
                total = total + jnp.dot(
                    mixed[rows, s * TILE : (s + 2) * TILE], block, preferred_element_type=F32
                )
            rounded = total.astype(BF16)
            for k in range(CAP):
                piece = rounded[:, k * TILE : (k + 1) * TILE]
                partial_out[chunk, 0, step_x, step_y, k] = piece[:HALF]
                partial_out[chunk, 1, step_y, step_x, k] = piece[HALF:]

    order = (1 + 2 * core, 3 - 2 * core, 2)

    def visit_first(chunk):
        visit(chunk, SIDE, lambda turn: (order[0], turn))
        visit(chunk, 3, lambda turn: (2 * turn - turn // 2 * order[0], order[0]))

    mix_rows(1)
    loads[1].wait()
    visit_first(1)
    take_spikes(3)
    pl.semaphore_wait(barrier, 2 * (SIDE - 1) + TM - 1)

    halo_copy = pltpu.make_async_remote_copy(
        src_ref=ext.at[pl.ds(TIME_DEV, LAG)],
        dst_ref=halo,
        send_sem=sem_halo.at[0],
        recv_sem=sem_halo.at[1],
        device_id=(unit, around(1)),
        device_id_type=MESH,
    )

    def names_copy(half, step):
        return pltpu.make_async_remote_copy(
            src_ref=names.at[unit],
            dst_ref=names.at[unit],
            send_sem=sem_names.at[0, half, step],
            recv_sem=sem_names.at[1, half, step],
            device_id=(along(half, step), tm),
            device_id_type=MESH,
        )

    def copy(source, place, kind, chunk, receiver):
        return pltpu.make_async_remote_copy(
            src_ref=source,
            dst_ref=place,
            send_sem=sem_send.at[kind],
            recv_sem=sem_recv.at[kind, chunk],
            device_id=(receiver, tm),
            device_id_type=MESH,
        )

    def arrived(place, kind, chunk):
        copy(place, place, kind, chunk, along(0, 1)).wait_recv()

    def lower(half_ref):
        return half_ref.at[pl.ds(0, TILES_DEV // 2)]

    def upper(half_ref):
        return half_ref.at[pl.ds(TILES_DEV // 2, TILES_DEV // 2)]

    def send_partials(turn, chunk):
        @pl.when(turn == 1)
        def _():
            take_spikes(2)

        @pl.when(turn == CHUNKS - 1)
        def _():
            halo_copy.wait()
            ext[pl.ds(0, LAG), :] = halo[...] * jnp.minimum(tm, 1).astype(BF16)

        @pl.when(turn > 0)
        def _():
            mix_rows(chunk)
            visit_first(chunk)

        def send(half, step):
            copy(
                partial_out.at[chunk, half, step],
                partial_in.at[chunk, half, step],
                0,
                chunk,
                along(half, step),
            ).start()

        send(0, order[0])
        send(1, order[0])
        visit(chunk, 3, lambda turn: (order[1], 2 * turn - turn // 2 * order[0]))
        send(0, order[1])
        visit(chunk, 2, lambda turn: (2 * turn, order[1]))
        send(1, order[1])
        visit(chunk, 2, lambda turn: (order[2], 2 * turn))
        send(0, order[2])
        visit(chunk, 1, lambda turn: (0, order[2]))
        send(1, order[2])
        visit(chunk, 1, lambda turn: (0, 0))

        @pl.when(turn == 0)
        def _():
            for half in range(2):
                for step in range(1, SIDE):
                    names_copy(half, step).start()

            halo_copy.start()

    def add_sources(chunk):
        arrived(partial_in.at[chunk, :, pl.ds(1, SIDE - 1)], 0, chunk)
        for half in range(2):
            stage[half, : SLOTS // SIDE] = partial_out[chunk, half, 0].reshape(
                SLOTS // SIDE, HALF, TILE
            )
            stage[half, SLOTS // SIDE : SLOTS] = partial_in[chunk, half, 1:].reshape(
                SLOTS - SLOTS // SIDE, HALF, TILE
            )

            @pl.loop(0, SIDE)
            def _(step):
                owner = across(half, step)

                @pl.loop(0, TILES_DEV)
                def _(local):
                    tile = owner * TILES_DEV + local
                    total = jnp.zeros((HALF, TILE), F32)
                    for back in range(SIDE):
                        source = along(half, (SIDE - back) % SIDE)
                        first = back * (SIDE * CAP) + step * CAP
                        at = jnp.where(
                            names[source, owner * CAP] == tile,
                            first,
                            jnp.where(names[source, owner * CAP + 1] == tile, first + 1, SLOTS),
                        )
                        total = total + stage[half, at].astype(F32)
                    dense[chunk, half, step, local] = total.astype(BF16)

            far = dense.at[chunk, half, 2]
            copy(lower(far), far_in.at[chunk, half, 0], 1, chunk, across(half, 1)).start()
            copy(upper(far), far_in.at[chunk, half, 1], 1, chunk, across(half, 3)).start()

    def pass_sums(chunk):
        arrived(far_in.at[chunk], 1, chunk)
        middle = TILES_DEV // 2
        for half in range(2):
            dense[chunk, half, 1, :middle] = (
                dense[chunk, half, 1, :middle].astype(F32) + far_in[chunk, half, 0].astype(F32)
            ).astype(BF16)
            dense[chunk, half, 3, middle:] = (
                dense[chunk, half, 3, middle:].astype(F32) + far_in[chunk, half, 1].astype(F32)
            ).astype(BF16)
            for place, step in ((0, 1), (1, 3)):
                copy(
                    dense.at[chunk, half, step],
                    near_in.at[chunk, half, place],
                    2,
                    chunk,
                    across(half, step),
                ).start()

    def make_resid(chunk):
        start = pl.multiple_of(chunk * LAG, LAG)
        rows = pl.ds(start, LAG)
        spike_rows = pl.ds(pl.multiple_of(start + LAG, LAG), LAG)
        arrived(near_in.at[chunk], 2, chunk)

        @pl.loop(0, UNITS_DEV // WIDE)
        def _(part):
            left = pl.multiple_of(part * WIDE, WIDE)
            wide = pl.ds(left, WIDE)
            hist[...] = jnp.dot(
                toeplitz[...], ext[pl.ds(start, 2 * LAG), wide], preferred_element_type=F32
            )
            drive = bias[:, wide] + lax.dot_general(
                stim[:, rows], filt[:, wide], (((0,), (0,)), ((), ())), preferred_element_type=F32
            )
            for side in range(2):
                inner = slice(side * TILE, (side + 1) * TILE)
                cols = pl.ds(pl.multiple_of(left + side * TILE, TILE), TILE)
                tile = part * 2 + side
                logit = drive[:, inner]
                for b in range(NB):
                    h = hist[b * LAG : (b + 1) * LAG, inner]
                    logit = logit + hist_weight[b : b + 1, cols] * h
                coupling = jnp.concatenate(
                    [
                        dense[chunk, half, 0, tile].astype(F32)
                        + near_in[chunk, half, 0, tile].astype(F32)
                        + near_in[chunk, half, 1, tile].astype(F32)
                        for half in range(2)
                    ],
                    axis=0,
                )
                resid = ext[spike_rows, cols].astype(F32) - jnp.exp(logit + coupling)
                rounded = resid.astype(BF16)
                for half in range(2):
                    resid_out[chunk, half, tile] = rounded[half * HALF : (half + 1) * HALF]
                resid_rows[:, cols] = rounded
                stats[NB : NB + 1, cols] += jnp.sum(resid, axis=0, keepdims=True)
                for b in range(NB):
                    h = hist[b * LAG : (b + 1) * LAG, inner]
                    stats[b : b + 1, cols] += jnp.sum(h * resid, axis=0, keepdims=True)

        for step, place in ((1, 1), (3, 0)):
            for half in range(2):
                copy(
                    resid_out.at[chunk, half],
                    got.at[chunk, half, place],
                    3,
                    chunk,
                    across(half, step),
                ).start()
        for block in range(TM):
            stim_sum[block] += lax.dot_general(
                stim[:, rows],
                resid_rows[:, block * TILE : (block + 1) * TILE],
                (((1,), (0,)), ((), ())),
                preferred_element_type=F32,
            )

    def forward_resid(chunk):
        arrived(got.at[chunk, :, pl.ds(0, 2)], 3, chunk)
        for half in range(2):
            far = got.at[chunk, half, 2]
            copy(
                lower(got.at[chunk, half, 1]), lower(far), 4, chunk, across(half, 1)
            ).start()
            copy(
                upper(got.at[chunk, half, 0]), upper(far), 4, chunk, across(half, 3)
            ).start()

    def send_named(chunk):
        arrived(got.at[chunk, :, 2], 4, chunk)
        for half in range(2):
            stage[half, :TILES_DEV] = resid_out[chunk, half]
            for step, place in ((1, 0), (2, 2), (3, 1)):
                stage[half, step * TILES_DEV : (step + 1) * TILES_DEV] = got[chunk, half, place]
            for receiver in (1, 3, 2, 0):

                @pl.loop(0, SIDE)
                def _(step):
                    owner = across(half, step)
                    for k in range(CAP):
                        local = (
                            names[along(half, receiver), owner * CAP + k] - owner * TILES_DEV
                        )
                        local = jnp.minimum(jnp.maximum(local, 0), TILES_DEV - 1)
                        pick[chunk, half, receiver, step, k] = stage[
                            half, step * TILES_DEV + local
                        ]

                if receiver:
                    copy(
                        pick.at[chunk, half, receiver],
                        resid_in.at[chunk, half, receiver],
                        5,
                        chunk,
                        along(half, receiver),
                    ).start()

    def take_resid(chunk):
        arrived(resid_in.at[chunk, :, pl.ds(1, SIDE - 1)], 5, chunk)
        for half in range(2):
            stage[half, : SLOTS // SIDE] = pick[chunk, half, 0].reshape(SLOTS // SIDE, HALF, TILE)
            stage[half, SLOTS // SIDE : SLOTS] = resid_in[chunk, half, 1:].reshape(
                SLOTS - SLOTS // SIDE, HALF, TILE
            )

    def chosen_tile(s, f):
        owner = target[f, s] // TILES_DEV
        gone_x = lax.rem(owner // SIDE - here_x + SIDE, SIDE)
        gone_y = lax.rem(owner % SIDE - here_y + SIDE, SIDE)
        back_x = lax.rem(SIDE - gone_x, SIDE)
        back_y = lax.rem(SIDE - gone_y, SIDE)
        rank = (target[f, s] == names[unit, owner * CAP + 1]).astype(jnp.int32)
        return jnp.concatenate(
            [
                stage[0, (back_x * SIDE + gone_y) * CAP + rank],
                stage[1, (back_y * SIDE + gone_x) * CAP + rank],
            ],
            axis=0,
        )

    def add_grad(chunk, s):
        grad[s] += lax.dot_general(
            mixed[pl.ds(pl.multiple_of(chunk * LAG, LAG), LAG), s * TILE : (s + 1) * TILE],
            jnp.concatenate([chosen_tile(s, f) for f in range(FAN)], axis=1),
            (((0,), (0,)), ((), ())),
            preferred_element_type=F32,
        )

    def stats_copy(step):
        return pltpu.make_async_remote_copy(
            src_ref=stats,
            dst_ref=stats_in.at[step],
            send_sem=sem_stats.at[0],
            recv_sem=sem_stats.at[1],
            device_id=(unit, around(step)),
            device_id_type=MESH,
        )

    def stim_copy(step):
        return pltpu.make_async_remote_copy(
            src_ref=stim_sum.at[around(step)],
            dst_ref=stim_in.at[step],
            send_sem=sem_stim.at[0],
            recv_sem=sem_stim.at[1],
            device_id=(unit, around(step)),
            device_id_type=MESH,
        )

    def all_arrived(place, sems):
        others = place.at[pl.ds(1, TM - 1)]
        pltpu.make_async_remote_copy(
            src_ref=others,
            dst_ref=others,
            send_sem=sems.at[0],
            recv_sem=sems.at[1],
            device_id=(unit, around(1)),
            device_id_type=MESH,
        ).wait()

    last = CHUNKS - 1

    def during(turn, delay, step):
        @pl.when((turn >= delay) & (turn < delay + CHUNKS))
        def _():
            step(lax.rem(turn - delay + 1, CHUNKS))

    @pl.loop(0, 7 + CHUNKS)
    def _(turn):
        during(turn, 0, functools.partial(send_partials, turn))

        @pl.when(turn == 2)
        def _():
            for half in range(2):
                for step in range(1, SIDE):
                    names_copy(half, step).wait()

            for load in loads[2:]:
                load.wait()

        during(turn, 2, add_sources)
        during(turn, 3, pass_sums)
        during(turn, 4, make_resid)

        @pl.when(turn == 4 + last)
        def _():
            @pl.loop(1, TM)
            def _(step):
                stats_copy(step).start()
                stim_copy(step).start()

        during(turn, 5, forward_resid)
        during(turn, 6, send_named)

        @pl.when(turn >= 8)
        def _():
            chunk = lax.rem(turn - 8 + 1, CHUNKS)
            take_resid(chunk)
            for s in range(TILES_DEV):
                add_grad(chunk, s)

    share = TILE // TM
    half_tiles = TILES_DEV // 2

    def pair_copy(half, z):
        given = pl.ds(pl.multiple_of((z * 2 + 1 - core) * share, share), share)
        return pltpu.make_async_remote_copy(
            src_ref=grad.at[pl.ds(half * half_tiles, half_tiles), given],
            dst_ref=pair_in.at[half, z],
            send_sem=sem_pair.at[0, half, z],
            recv_sem=sem_pair.at[1, half, z],
            device_id=(unit, here_z * 2 + 1 - core),
            device_id_type=MESH,
        )

    forth, back = lax.rem(here_z + 1, SIDE), lax.rem(here_z + 3, SIDE)
    ways = (forth, back)

    def far_copy(half):
        return pltpu.make_async_remote_copy(
            src_ref=pair_out.at[half, lax.rem(here_z + 2, SIDE)],
            dst_ref=zed_far.at[half],
            send_sem=sem_far.at[0, half],
            recv_sem=sem_far.at[1, half],
            device_id=(unit, ways[half] * 2 + core),
            device_id_type=MESH,
        )

    def zed_copy(half, way):
        return pltpu.make_async_remote_copy(
            src_ref=pair_out.at[half, ways[way]],
            dst_ref=zed_in.at[half, way],
            send_sem=sem_zed.at[0, half, way],
            recv_sem=sem_zed.at[1, half, way],
            device_id=(unit, ways[way] * 2 + core),
            device_id_type=MESH,
        )

    def both(half, z):
        kept = pl.ds(pl.multiple_of((z * 2 + core) * share, share), share)
        return grad[half * half_tiles : (half + 1) * half_tiles, kept, :] + pair_in[half, z]

    take_resid(0)
    for half in range(2):
        for s in range(half * half_tiles, (half + 1) * half_tiles):
            add_grad(0, s)
        for step in (2, 3 - 2 * half, 1 + 2 * half, 0):
            pair_copy(half, lax.rem(here_z + step, SIDE)).start()
    for half in range(2):
        for z in (lax.rem(here_z + 2, SIDE), ways[1 - half]):
            pair_copy(half, z).wait_recv()
            pair_out[half, z] = both(half, z).astype(BF16)
        far_copy(half).start()
        zed_copy(half, 1 - half).start()
    for half in range(2):
        z = ways[half]
        pair_copy(half, z).wait_recv()
        own = both(half, z)
        far_copy(half).wait_recv()
        pair_out[half, z] = (own + zed_far[half].astype(F32)).astype(BF16)
        zed_copy(half, half).start()
    for half in range(2):
        pair_copy(half, here_z).wait_recv()
        final[half * half_tiles : (half + 1) * half_tiles] = both(half, here_z)

    all_arrived(stats_in, sem_stats)
    all_arrived(stim_in, sem_stim)
    stats_in[0] = stats[...]
    total = stats_in[tm]
    for block in range(1, TM):
        total = total + stats_in[lax.rem(tm - block + TM, TM)]
    out_stats[...] = total
    stim_total = stim_sum[tm]
    for step in range(1, TM):
        stim_total = stim_total + stim_in[step]
    out_stim[...] = stim_total

    others = pl.ds(1, SIDE - 1)
    for kind, place in enumerate(
        (
            partial_in.at[:, :, others],
            far_in,
            near_in,
            got.at[:, :, pl.ds(0, 2)],
            got.at[:, :, 2],
            resid_in.at[:, :, others],
        )
    ):
        copy(place, place, kind, 0, along(0, 1)).wait_send()
    for half in range(2):
        for z in range(SIDE):
            pair_copy(half, z).wait_send()
    for half in range(2):
        tiles = slice(half * half_tiles, (half + 1) * half_tiles)
        total = final[tiles]
        far_copy(half).wait_send()
        for way in range(2):
            zed_copy(half, way).wait()
            total = total + zed_in[half, way].astype(F32)
        out_coupling[tiles] = total


def finish_kernel(stats, stim, coupling, out_bias, out_hist, out_stim, out_coupling):
    time_total = float(TIME_DEV * TM)
    out_hist[...] = stats[:NB, :] / time_total
    out_bias[...] = stats[NB : NB + 1, :] / time_total
    out_stim[...] = stim[...] / time_total
    for f in range(FAN):
        out_coupling[:, f] = coupling[:, :, f * TILE : (f + 1) * TILE] / time_total


def shards(
    spikes, stimulus, bias, hist_weight, stim_filter, coupling_mix, coupling_target, coupling_weight
):
    smem = pl.BlockSpec(memory_space=pltpu.SMEM)
    vmem = pl.BlockSpec(memory_space=pltpu.VMEM)
    anywhere = pl.BlockSpec(memory_space=pl.ANY)
    dma = pltpu.SemaphoreType.DMA
    share = TILE // TM
    sums = pl.pallas_call(
        main_kernel,
        out_shape=[
            jax.ShapeDtypeStruct((16, UNITS_DEV), F32),
            jax.ShapeDtypeStruct((STIM, TILE), F32),
            jax.ShapeDtypeStruct((TILES_DEV, share, FAN * TILE), F32),
        ],
        in_specs=[smem] * 2 + [anywhere] * 7,
        out_specs=[vmem] * 3,
        scratch_shapes=[
            pltpu.VMEM((TIME_DEV, UNITS_DEV), jnp.int32),
            pltpu.VMEM((STIM, TIME_DEV), BF16),
            pltpu.VMEM((1, UNITS_DEV), F32),
            pltpu.VMEM((NB, UNITS_DEV), F32),
            pltpu.VMEM((STIM, UNITS_DEV), BF16),
            pltpu.VMEM((NB * LAG, 2 * LAG), BF16),
            pltpu.VMEM((2 * LAG, 2 * LAG), BF16),
            pltpu.VMEM((TIME_DEV + LAG, UNITS_DEV), BF16),
            pltpu.VMEM((LAG, UNITS_DEV), BF16),
            pltpu.VMEM((ENTRIES + 1, TILE, TILE), BF16),
            pltpu.VMEM((NB * LAG, WIDE), F32),
            pltpu.VMEM((TIME_DEV, UNITS_DEV), BF16),
            pltpu.VMEM((CHUNKS, 2, SIDE, SIDE, CAP, HALF, TILE), BF16),
            pltpu.VMEM((CHUNKS, 2, SIDE, SIDE, CAP, HALF, TILE), BF16),
            pltpu.VMEM((CHUNKS, 2, SIDE, TILES_DEV, HALF, TILE), BF16),
            pltpu.VMEM((CHUNKS, 2, 2, TILES_DEV // 2, HALF, TILE), BF16),
            pltpu.VMEM((CHUNKS, 2, 2, TILES_DEV, HALF, TILE), BF16),
            pltpu.VMEM((2, SLOTS + 1, HALF, TILE), BF16),
            pltpu.VMEM((LAG, UNITS_DEV), BF16),
            pltpu.VMEM((CHUNKS, 2, TILES_DEV, HALF, TILE), BF16),
            pltpu.VMEM((CHUNKS, 2, SIDE - 1, TILES_DEV, HALF, TILE), BF16),
            pltpu.VMEM((CHUNKS, 2, SIDE, SIDE, CAP, HALF, TILE), BF16),
            pltpu.VMEM((CHUNKS, 2, SIDE, SIDE, CAP, HALF, TILE), BF16),
            pltpu.SMEM((PEERS, SLOTS), jnp.int32),
            pltpu.VMEM((TILES_DEV, TILE, FAN * TILE), F32),
            pltpu.VMEM((16, UNITS_DEV), F32),
            pltpu.VMEM((TM, 16, UNITS_DEV), F32),
            pltpu.VMEM((TM, STIM, TILE), F32),
            pltpu.VMEM((TM, STIM, TILE), F32),
            pltpu.VMEM((2, SIDE, TILES_DEV // 2, share, FAN * TILE), F32),
            pltpu.VMEM((2, SIDE, TILES_DEV // 2, share, FAN * TILE), BF16),
            pltpu.VMEM((2, TILES_DEV // 2, share, FAN * TILE), BF16),
            pltpu.VMEM((2, 2, TILES_DEV // 2, share, FAN * TILE), BF16),
            pltpu.VMEM((TILES_DEV, share, FAN * TILE), F32),
            dma((6,)),
            dma((CHUNKS,)),
            dma((2,)),
            dma((2, 2, SIDE)),
            dma((6,)),
            dma((6, CHUNKS)),
            dma((2,)),
            dma((2,)),
            dma((2, 2, SIDE)),
            dma((2, 2)),
            dma((2, 2, 2)),
        ],
        compiler_params=pltpu.CompilerParams(
            collective_id=0, has_side_effects=True, vmem_limit_bytes=56 * 1024 * 1024
        ),
    )(
        coupling_target.T,
        coupling_mix,
        spikes,
        stimulus.T,
        bias.reshape(1, UNITS_DEV),
        hist_weight,
        stim_filter.T,
        coupling_weight.reshape(ENTRIES, TILE, TILE),
        jnp.asarray(toeplitz_table()),
    )
    grad_bias, grad_hist, grad_stim, grad_coupling = pl.pallas_call(
        finish_kernel,
        out_shape=[
            jax.ShapeDtypeStruct((1, UNITS_DEV), F32),
            jax.ShapeDtypeStruct((NB, UNITS_DEV), F32),
            jax.ShapeDtypeStruct((STIM, TILE), F32),
            jax.ShapeDtypeStruct((TILES_DEV, FAN, share, TILE), F32),
        ],
        in_specs=[vmem] * 3,
        out_specs=[vmem] * 4,
    )(*sums)
    return (grad_bias.reshape(UNITS_DEV), grad_hist, grad_stim.T, grad_coupling)


def solution(mesh):
    return jax.shard_map(
        shards,
        mesh=mesh,
        in_specs=(
            P("tm", "unit"),
            P("tm", None),
            P("unit"),
            P(None, "unit"),
            P("unit", None),
            P(),
            P("unit", None),
            P("unit", None, None, None),
        ),
        out_specs=(
            P("unit"),
            P(None, "unit"),
            P(("unit", "tm"), None),
            P("unit", None, "tm", None),
        ),
        check_vma=False,
    )
```

```python
import functools
import math

import jax
import jax.numpy as jnp
import ml_dtypes
import numpy as np
from jax import lax
from jax.experimental import pallas as pl
from jax.experimental.pallas import tpu as pltpu
from jax.sharding import PartitionSpec as P

TILE = 128
FAN = 4
CAP = 2
NB = 10
LAG = 128
SIDE = 4
PEERS = SIDE * SIDE
HALF = LAG // 2
SLOTS = PEERS * CAP
TILES_DEV = 8
UNITS_DEV = TILES_DEV * TILE
TIME_DEV = 512
CHUNKS = TIME_DEV // LAG
STIM = 64
TM = 8
WIDE = 2 * TILE
ENTRIES = TILES_DEV * FAN
MESH = pl.DeviceIdType.MESH
F32 = jnp.float32
BF16 = jnp.bfloat16


def toeplitz_table():
    low = math.log(2.0)
    spacing = (math.log(LAG + 1.0) - low) / (NB - 1)
    stretched = np.log(np.arange(1, LAG + 1) + 1.0)
    centers = low + spacing * np.arange(NB)
    phases = (stretched[None, :] - centers[:, None]) * (math.pi / (2.0 * spacing))
    shapes = 0.5 * (1.0 + np.cos(np.clip(phases, -math.pi, math.pi)))
    basis = (shapes / shapes.sum(axis=1, keepdims=True)).astype(np.float32)
    table = np.zeros((NB, LAG, 2 * LAG), np.float32)
    for row in range(LAG):
        table[:, row, row : row + LAG] = basis[:, ::-1]
    return table.reshape(NB * LAG, 2 * LAG).astype(ml_dtypes.bfloat16)


def main_kernel(
    target,
    mix,
    spikes_hbm,
    stim_hbm,
    bias_hbm,
    hist_weight_hbm,
    filt_hbm,
    weights_hbm,
    toeplitz_hbm,
    out_stats,
    out_stim,
    out_coupling,
    spikes,
    stim,
    bias,
    hist_weight,
    filt,
    toeplitz,
    blend_filter,
    ext,
    halo,
    weights,
    hist,
    mixed,
    partial_out,
    partial_in,
    dense,
    far_in,
    near_in,
    stage,
    resid_rows,
    resid_out,
    got,
    pick,
    resid_in,
    names,
    grad,
    stats,
    stats_in,
    stim_sum,
    stim_in,
    pair_in,
    pair_out,
    zed_far,
    zed_in,
    final,
    sem_load,
    sem_spikes,
    sem_halo,
    sem_names,
    sem_send,
    sem_recv,
    sem_stats,
    sem_stim,
    sem_pair,
    sem_far,
    sem_zed,
):
    unit = lax.axis_index("unit")
    tm = lax.axis_index("tm")
    here_x, here_y = unit // SIDE, unit % SIDE
    here_z, core = tm // 2, tm % 2

    def device(step_x, step_y):
        return lax.rem(here_x + step_x, SIDE) * SIDE + lax.rem(here_y + step_y, SIDE)

    def along(half, step):
        return device(0, step) if half else device(step, 0)

    def across(half, step):
        return device(step, 0) if half else device(0, step)

    def around(step):
        return lax.rem(tm + step, TM)

    barrier = pltpu.get_barrier_semaphore()

    for step in range(1, SIDE):
        for half in range(2):
            pl.semaphore_signal(
                barrier, inc=1, device_id=(along(half, step), tm), device_id_type=MESH
            )

    @pl.loop(1, TM)
    def _(step):
        pl.semaphore_signal(barrier, inc=1, device_id=(unit, around(step)), device_id_type=MESH)

    def spikes_copy(chunk):
        rows = pl.ds(pl.multiple_of(chunk * LAG, LAG), LAG)
        return pltpu.make_async_copy(
            spikes_hbm.at[rows, :], spikes.at[rows, :], sem_spikes.at[chunk]
        )

    loads = [
        pltpu.make_async_copy(source, place, sem_load.at[k])
        for k, (source, place) in enumerate(
            (
                (toeplitz_hbm, toeplitz),
                (weights_hbm, weights.at[pl.ds(0, ENTRIES)]),
                (stim_hbm, stim),
                (bias_hbm, bias),
                (hist_weight_hbm, hist_weight),
                (filt_hbm, filt),
            )
        )
    ]
    spikes_copy(0).start()
    spikes_copy(1).start()
    loads[0].start()
    spikes_copy(3).start()
    loads[1].start()
    spikes_copy(2).start()
    for load in loads[2:]:
        load.start()

    @pl.loop(0, PEERS)
    def _(owner):
        first, last = owner * TILES_DEV, owner * TILES_DEV + TILES_DEV - 1
        low, high = jnp.int32(PEERS * TILES_DEV), jnp.int32(-1)
        for s in range(TILES_DEV):
            for f in range(FAN):
                tile = target[f, s]
                low = jnp.where(tile >= first, jnp.minimum(low, tile), low)
                high = jnp.where(tile <= last, jnp.maximum(high, tile), high)
        names[unit, owner * CAP] = low
        names[unit, owner * CAP + 1] = high

    weights[ENTRIES] = jnp.zeros((TILE, TILE), BF16)
    for half in range(2):
        stage[half, SLOTS] = jnp.zeros((HALF, TILE), BF16)
    stats[...] = jnp.zeros_like(stats)
    stim_sum[...] = jnp.zeros_like(stim_sum)
    grad[...] = jnp.zeros_like(grad)

    def take_spikes(chunk):
        spikes_copy(chunk).wait()
        ext[(chunk + 1) * LAG : (chunk + 2) * LAG, :] = spikes[
            chunk * LAG : (chunk + 1) * LAG, :
        ].astype(BF16)

    take_spikes(0)
    take_spikes(1)
    loads[0].wait()
    combined = jnp.zeros((LAG, 2 * LAG), F32)
    for b in range(NB):
        combined = combined + mix[b] * toeplitz[b * LAG : (b + 1) * LAG, :].astype(F32)
    upper = combined.astype(BF16)
    blend_filter[:LAG, :] = upper
    blend_filter[LAG:, :] = (combined - upper.astype(F32)).astype(BF16)

    def mix_rows(chunk):
        start = pl.multiple_of(chunk * LAG, LAG)
        for part in range(UNITS_DEV // WIDE):
            wide = slice(part * WIDE, (part + 1) * WIDE)
            both = jnp.dot(
                blend_filter[...], ext[pl.ds(start, 2 * LAG), wide], preferred_element_type=F32
            )
            mixed[pl.ds(start, LAG), wide] = (both[:LAG] + both[LAG:]).astype(BF16)

    def visit(chunk, count, steps):
        rows = pl.ds(pl.multiple_of(chunk * LAG, LAG), LAG)

        @pl.loop(0, count)
        def _(turn):
            step_x, step_y = steps(turn)
            owner = device(step_x, step_y)
            low, high = names[unit, owner * CAP], names[unit, owner * CAP + 1]

            def weight_of(s, tile):
                at = jnp.int32(ENTRIES)
                for f in range(FAN):
                    at = jnp.where(target[f, s] == tile, s * FAN + f, at)
                return weights[at]

            total = jnp.zeros((LAG, WIDE), F32)
            for s in range(0, TILES_DEV, 2):
                block = jnp.concatenate(
                    [
                        jnp.concatenate([weight_of(s, low), weight_of(s, high)], axis=1),
                        jnp.concatenate([weight_of(s + 1, low), weight_of(s + 1, high)], axis=1),
                    ],
                    axis=0,
                )
                total = total + jnp.dot(
                    mixed[rows, s * TILE : (s + 2) * TILE], block, preferred_element_type=F32
                )
            rounded = total.astype(BF16)
            for k in range(CAP):
                piece = rounded[:, k * TILE : (k + 1) * TILE]
                partial_out[chunk, 0, step_x, step_y, k] = piece[:HALF]
                partial_out[chunk, 1, step_y, step_x, k] = piece[HALF:]

    order = (1 + 2 * core, 3 - 2 * core, 2)

    def visit_first(chunk):
        visit(chunk, SIDE, lambda turn: (order[0], turn))
        visit(chunk, 3, lambda turn: (2 * turn - turn // 2 * order[0], order[0]))

    mix_rows(1)
    loads[1].wait()
    visit_first(1)
    take_spikes(3)
    pl.semaphore_wait(barrier, 2 * (SIDE - 1) + TM - 1)

    halo_copy = pltpu.make_async_remote_copy(
        src_ref=ext.at[pl.ds(TIME_DEV, LAG)],
        dst_ref=halo,
        send_sem=sem_halo.at[0],
        recv_sem=sem_halo.at[1],
        device_id=(unit, around(1)),
        device_id_type=MESH,
    )

    def names_copy(half, step):
        return pltpu.make_async_remote_copy(
            src_ref=names.at[unit],
            dst_ref=names.at[unit],
            send_sem=sem_names.at[0, half, step],
            recv_sem=sem_names.at[1, half, step],
            device_id=(along(half, step), tm),
            device_id_type=MESH,
        )

    def copy(source, place, kind, chunk, receiver):
        return pltpu.make_async_remote_copy(
            src_ref=source,
            dst_ref=place,
            send_sem=sem_send.at[kind],
            recv_sem=sem_recv.at[kind, chunk],
            device_id=(receiver, tm),
            device_id_type=MESH,
        )

    def arrived(place, kind, chunk):
        copy(place, place, kind, chunk, along(0, 1)).wait_recv()

    def lower(half_ref):
        return half_ref.at[pl.ds(0, TILES_DEV // 2)]

    def upper(half_ref):
        return half_ref.at[pl.ds(TILES_DEV // 2, TILES_DEV // 2)]

    def send_partials(turn, chunk):
        @pl.when(turn == 1)
        def _():
            take_spikes(2)

        @pl.when(turn == CHUNKS - 1)
        def _():
            halo_copy.wait()
            ext[pl.ds(0, LAG), :] = halo[...] * jnp.minimum(tm, 1).astype(BF16)

        @pl.when(turn > 0)
        def _():
            mix_rows(chunk)
            visit_first(chunk)

        def send(half, step):
            copy(
                partial_out.at[chunk, half, step],
                partial_in.at[chunk, half, step],
                0,
                chunk,
                along(half, step),
            ).start()

        send(0, order[0])
        send(1, order[0])
        visit(chunk, 3, lambda turn: (order[1], 2 * turn - turn // 2 * order[0]))
        send(0, order[1])
        visit(chunk, 2, lambda turn: (2 * turn, order[1]))
        send(1, order[1])
        visit(chunk, 2, lambda turn: (order[2], 2 * turn))
        send(0, order[2])
        visit(chunk, 1, lambda turn: (0, order[2]))
        send(1, order[2])
        visit(chunk, 1, lambda turn: (0, 0))

        @pl.when(turn == 0)
        def _():
            for half in range(2):
                for step in range(1, SIDE):
                    names_copy(half, step).start()

            halo_copy.start()

    def add_sources(chunk):
        arrived(partial_in.at[chunk, :, pl.ds(1, SIDE - 1)], 0, chunk)
        for half in range(2):
            stage[half, : SLOTS // SIDE] = partial_out[chunk, half, 0].reshape(
                SLOTS // SIDE, HALF, TILE
            )
            stage[half, SLOTS // SIDE : SLOTS] = partial_in[chunk, half, 1:].reshape(
                SLOTS - SLOTS // SIDE, HALF, TILE
            )

            @pl.loop(0, SIDE)
            def _(step):
                owner = across(half, step)

                @pl.loop(0, TILES_DEV)
                def _(local):
                    tile = owner * TILES_DEV + local
                    total = jnp.zeros((HALF, TILE), F32)
                    for back in range(SIDE):
                        source = along(half, (SIDE - back) % SIDE)
                        first = back * (SIDE * CAP) + step * CAP
                        at = jnp.where(
                            names[source, owner * CAP] == tile,
                            first,
                            jnp.where(names[source, owner * CAP + 1] == tile, first + 1, SLOTS),
                        )
                        total = total + stage[half, at].astype(F32)
                    dense[chunk, half, step, local] = total.astype(BF16)

            far = dense.at[chunk, half, 2]
            copy(lower(far), far_in.at[chunk, half, 0], 1, chunk, across(half, 1)).start()
            copy(upper(far), far_in.at[chunk, half, 1], 1, chunk, across(half, 3)).start()

    def pass_sums(chunk):
        arrived(far_in.at[chunk], 1, chunk)
        middle = TILES_DEV // 2
        for half in range(2):
            dense[chunk, half, 1, :middle] = (
                dense[chunk, half, 1, :middle].astype(F32) + far_in[chunk, half, 0].astype(F32)
            ).astype(BF16)
            dense[chunk, half, 3, middle:] = (
                dense[chunk, half, 3, middle:].astype(F32) + far_in[chunk, half, 1].astype(F32)
            ).astype(BF16)
            for place, step in ((0, 1), (1, 3)):
                copy(
                    dense.at[chunk, half, step],
                    near_in.at[chunk, half, place],
                    2,
                    chunk,
                    across(half, step),
                ).start()

    def make_resid(chunk):
        start = pl.multiple_of(chunk * LAG, LAG)
        rows = pl.ds(start, LAG)
        spike_rows = pl.ds(pl.multiple_of(start + LAG, LAG), LAG)
        arrived(near_in.at[chunk], 2, chunk)

        @pl.loop(0, UNITS_DEV // WIDE)
        def _(part):
            left = pl.multiple_of(part * WIDE, WIDE)
            wide = pl.ds(left, WIDE)
            hist[...] = jnp.dot(
                toeplitz[...], ext[pl.ds(start, 2 * LAG), wide], preferred_element_type=F32
            )
            drive = bias[:, wide] + lax.dot_general(
                stim[:, rows], filt[:, wide], (((0,), (0,)), ((), ())), preferred_element_type=F32
            )
            for side in range(2):
                inner = slice(side * TILE, (side + 1) * TILE)
                cols = pl.ds(pl.multiple_of(left + side * TILE, TILE), TILE)
                tile = part * 2 + side
                logit = drive[:, inner]
                for b in range(NB):
                    h = hist[b * LAG : (b + 1) * LAG, inner]
                    logit = logit + hist_weight[b : b + 1, cols] * h
                coupling = jnp.concatenate(
                    [
                        dense[chunk, half, 0, tile].astype(F32)
                        + near_in[chunk, half, 0, tile].astype(F32)
                        + near_in[chunk, half, 1, tile].astype(F32)
                        for half in range(2)
                    ],
                    axis=0,
                )
                resid = ext[spike_rows, cols].astype(F32) - jnp.exp(logit + coupling)
                rounded = resid.astype(BF16)
                for half in range(2):
                    resid_out[chunk, half, tile] = rounded[half * HALF : (half + 1) * HALF]
                resid_rows[:, cols] = rounded
                stats[NB : NB + 1, cols] += jnp.sum(resid, axis=0, keepdims=True)
                for b in range(NB):
                    h = hist[b * LAG : (b + 1) * LAG, inner]
                    stats[b : b + 1, cols] += jnp.sum(h * resid, axis=0, keepdims=True)

        for step, place in ((1, 1), (3, 0)):
            for half in range(2):
                copy(
                    resid_out.at[chunk, half],
                    got.at[chunk, half, place],
                    3,
                    chunk,
                    across(half, step),
                ).start()
        for block in range(TM):
            stim_sum[block] += lax.dot_general(
                stim[:, rows],
                resid_rows[:, block * TILE : (block + 1) * TILE],
                (((1,), (0,)), ((), ())),
                preferred_element_type=F32,
            )

    def forward_resid(chunk):
        arrived(got.at[chunk, :, pl.ds(0, 2)], 3, chunk)
        for half in range(2):
            far = got.at[chunk, half, 2]
            copy(
                lower(got.at[chunk, half, 1]), lower(far), 4, chunk, across(half, 1)
            ).start()
            copy(
                upper(got.at[chunk, half, 0]), upper(far), 4, chunk, across(half, 3)
            ).start()

    def send_named(chunk):
        arrived(got.at[chunk, :, 2], 4, chunk)
        for half in range(2):
            stage[half, :TILES_DEV] = resid_out[chunk, half]
            for step, place in ((1, 0), (2, 2), (3, 1)):
                stage[half, step * TILES_DEV : (step + 1) * TILES_DEV] = got[chunk, half, place]
            for receiver in (2, 1, 3, 0):

                @pl.loop(0, SIDE)
                def _(step):
                    owner = across(half, step)
                    for k in range(CAP):
                        local = (
                            names[along(half, receiver), owner * CAP + k] - owner * TILES_DEV
                        )
                        local = jnp.minimum(jnp.maximum(local, 0), TILES_DEV - 1)
                        pick[chunk, half, receiver, step, k] = stage[
                            half, step * TILES_DEV + local
                        ]

                if receiver:
                    copy(
                        pick.at[chunk, half, receiver],
                        resid_in.at[chunk, half, receiver],
                        5,
                        chunk,
                        along(half, receiver),
                    ).start()

    def take_resid(chunk):
        arrived(resid_in.at[chunk, :, pl.ds(1, SIDE - 1)], 5, chunk)
        for half in range(2):
            stage[half, : SLOTS // SIDE] = pick[chunk, half, 0].reshape(SLOTS // SIDE, HALF, TILE)
            stage[half, SLOTS // SIDE : SLOTS] = resid_in[chunk, half, 1:].reshape(
                SLOTS - SLOTS // SIDE, HALF, TILE
            )

    def chosen_tile(s, f):
        owner = target[f, s] // TILES_DEV
        gone_x = lax.rem(owner // SIDE - here_x + SIDE, SIDE)
        gone_y = lax.rem(owner % SIDE - here_y + SIDE, SIDE)
        back_x = lax.rem(SIDE - gone_x, SIDE)
        back_y = lax.rem(SIDE - gone_y, SIDE)
        rank = (target[f, s] == names[unit, owner * CAP + 1]).astype(jnp.int32)
        return jnp.concatenate(
            [
                stage[0, (back_x * SIDE + gone_y) * CAP + rank],
                stage[1, (back_y * SIDE + gone_x) * CAP + rank],
            ],
            axis=0,
        )

    def add_grad(chunk, s):
        grad[s] += lax.dot_general(
            mixed[pl.ds(pl.multiple_of(chunk * LAG, LAG), LAG), s * TILE : (s + 1) * TILE],
            jnp.concatenate([chosen_tile(s, f) for f in range(FAN)], axis=1),
            (((0,), (0,)), ((), ())),
            preferred_element_type=F32,
        )

    def stats_copy(step):
        return pltpu.make_async_remote_copy(
            src_ref=stats,
            dst_ref=stats_in.at[step],
            send_sem=sem_stats.at[0],
            recv_sem=sem_stats.at[1],
            device_id=(unit, around(step)),
            device_id_type=MESH,
        )

    def stim_copy(step):
        return pltpu.make_async_remote_copy(
            src_ref=stim_sum.at[around(step)],
            dst_ref=stim_in.at[step],
            send_sem=sem_stim.at[0],
            recv_sem=sem_stim.at[1],
            device_id=(unit, around(step)),
            device_id_type=MESH,
        )

    def all_arrived(place, sems):
        others = place.at[pl.ds(1, TM - 1)]
        pltpu.make_async_remote_copy(
            src_ref=others,
            dst_ref=others,
            send_sem=sems.at[0],
            recv_sem=sems.at[1],
            device_id=(unit, around(1)),
            device_id_type=MESH,
        ).wait()

    last = CHUNKS - 1

    def during(turn, delay, step):
        @pl.when((turn >= delay) & (turn < delay + CHUNKS))
        def _():
            step(lax.rem(turn - delay + 1, CHUNKS))

    @pl.loop(0, 10)
    def _(turn):
        during(turn, 0, functools.partial(send_partials, turn))

        @pl.when(turn == 1)
        def _():
            for half in range(2):
                for step in range(1, SIDE):
                    names_copy(half, step).wait()

            for load in loads[2:]:
                load.wait()

        during(turn, 1, add_sources)

        during(turn, 2, pass_sums)

        during(turn, 3, make_resid)

        @pl.when(turn == 3 + last)
        def _():
            @pl.loop(1, TM)
            def _(step):
                stats_copy(step).start()
                stim_copy(step).start()

        during(turn, 4, forward_resid)

        during(turn, 5, send_named)

        @pl.when(turn >= 7)
        def _():
            chunk = lax.rem(turn - 7 + 1, CHUNKS)
            take_resid(chunk)
            for s in range(TILES_DEV):
                add_grad(chunk, s)

    share = TILE // TM
    half_tiles = TILES_DEV // 2

    def pair_copy(half, z):
        given = pl.ds(pl.multiple_of((z * 2 + 1 - core) * share, share), share)
        return pltpu.make_async_remote_copy(
            src_ref=grad.at[pl.ds(half * half_tiles, half_tiles), given],
            dst_ref=pair_in.at[half, z],
            send_sem=sem_pair.at[0, half, z],
            recv_sem=sem_pair.at[1, half, z],
            device_id=(unit, here_z * 2 + 1 - core),
            device_id_type=MESH,
        )

    forth, back = lax.rem(here_z + 1, SIDE), lax.rem(here_z + 3, SIDE)
    ways = (forth, back)

    def far_copy(half):
        return pltpu.make_async_remote_copy(
            src_ref=pair_out.at[half, lax.rem(here_z + 2, SIDE)],
            dst_ref=zed_far.at[half],
            send_sem=sem_far.at[0, half],
            recv_sem=sem_far.at[1, half],
            device_id=(unit, ways[half] * 2 + core),
            device_id_type=MESH,
        )

    def zed_copy(half, way):
        return pltpu.make_async_remote_copy(
            src_ref=pair_out.at[half, ways[way]],
            dst_ref=zed_in.at[half, way],
            send_sem=sem_zed.at[0, half, way],
            recv_sem=sem_zed.at[1, half, way],
            device_id=(unit, ways[way] * 2 + core),
            device_id_type=MESH,
        )

    def both(half, z):
        kept = pl.ds(pl.multiple_of((z * 2 + core) * share, share), share)
        return grad[half * half_tiles : (half + 1) * half_tiles, kept, :] + pair_in[half, z]

    take_resid(0)
    for half in range(2):
        for s in range(half * half_tiles, (half + 1) * half_tiles):
            add_grad(0, s)
        for step in (2, 3 - 2 * half, 1 + 2 * half, 0):
            pair_copy(half, lax.rem(here_z + step, SIDE)).start()
    for half in range(2):
        for z in (lax.rem(here_z + 2, SIDE), ways[1 - half]):
            pair_copy(half, z).wait_recv()
            pair_out[half, z] = both(half, z).astype(BF16)
        far_copy(half).start()
        zed_copy(half, 1 - half).start()
    for half in range(2):
        z = ways[half]
        pair_copy(half, z).wait_recv()
        own = both(half, z)
        far_copy(half).wait_recv()
        pair_out[half, z] = (own + zed_far[half].astype(F32)).astype(BF16)
        zed_copy(half, half).start()
    for half in range(2):
        pair_copy(half, here_z).wait_recv()
        final[half * half_tiles : (half + 1) * half_tiles] = both(half, here_z)

    all_arrived(stats_in, sem_stats)
    all_arrived(stim_in, sem_stim)
    stats_in[0] = stats[...]
    total = stats_in[tm]
    for block in range(1, TM):
        total = total + stats_in[lax.rem(tm - block + TM, TM)]
    out_stats[...] = total
    stim_total = stim_sum[tm]
    for step in range(1, TM):
        stim_total = stim_total + stim_in[step]
    out_stim[...] = stim_total

    others = pl.ds(1, SIDE - 1)
    for kind, place in enumerate(
        (
            partial_in.at[:, :, others],
            far_in,
            near_in,
            got.at[:, :, pl.ds(0, 2)],
            got.at[:, :, 2],
            resid_in.at[:, :, others],
        )
    ):
        copy(place, place, kind, 0, along(0, 1)).wait_send()
    for half in range(2):
        for z in range(SIDE):
            pair_copy(half, z).wait_send()
    for half in range(2):
        tiles = slice(half * half_tiles, (half + 1) * half_tiles)
        total = final[tiles]
        far_copy(half).wait_send()
        for way in range(2):
            zed_copy(half, way).wait()
            total = total + zed_in[half, way].astype(F32)
        out_coupling[tiles] = total


def finish_kernel(stats, stim, coupling, out_bias, out_hist, out_stim, out_coupling):
    time_total = float(TIME_DEV * TM)
    out_hist[...] = stats[:NB, :] / time_total
    out_bias[...] = stats[NB : NB + 1, :] / time_total
    out_stim[...] = stim[...] / time_total
    for f in range(FAN):
        out_coupling[:, f] = coupling[:, :, f * TILE : (f + 1) * TILE] / time_total


def shards(
    spikes, stimulus, bias, hist_weight, stim_filter, coupling_mix, coupling_target, coupling_weight
):
    smem = pl.BlockSpec(memory_space=pltpu.SMEM)
    vmem = pl.BlockSpec(memory_space=pltpu.VMEM)
    anywhere = pl.BlockSpec(memory_space=pl.ANY)
    dma = pltpu.SemaphoreType.DMA
    share = TILE // TM
    sums = pl.pallas_call(
        main_kernel,
        out_shape=[
            pltpu.VMEM((16, UNITS_DEV), F32),
            pltpu.VMEM((STIM, TILE), F32),
            pltpu.VMEM((TILES_DEV, share, FAN * TILE), F32),
        ],
        in_specs=[smem] * 2 + [anywhere] * 7,
        out_specs=[vmem] * 3,
        scratch_shapes=[
            pltpu.VMEM((TIME_DEV, UNITS_DEV), jnp.int32),
            pltpu.VMEM((STIM, TIME_DEV), BF16),
            pltpu.VMEM((1, UNITS_DEV), F32),
            pltpu.VMEM((NB, UNITS_DEV), F32),
            pltpu.VMEM((STIM, UNITS_DEV), BF16),
            pltpu.VMEM((NB * LAG, 2 * LAG), BF16),
            pltpu.VMEM((2 * LAG, 2 * LAG), BF16),
            pltpu.VMEM((TIME_DEV + LAG, UNITS_DEV), BF16),
            pltpu.VMEM((LAG, UNITS_DEV), BF16),
            pltpu.VMEM((ENTRIES + 1, TILE, TILE), BF16),
            pltpu.VMEM((NB * LAG, WIDE), F32),
            pltpu.VMEM((TIME_DEV, UNITS_DEV), BF16),
            pltpu.VMEM((CHUNKS, 2, SIDE, SIDE, CAP, HALF, TILE), BF16),
            pltpu.VMEM((CHUNKS, 2, SIDE, SIDE, CAP, HALF, TILE), BF16),
            pltpu.VMEM((CHUNKS, 2, SIDE, TILES_DEV, HALF, TILE), BF16),
            pltpu.VMEM((CHUNKS, 2, 2, TILES_DEV // 2, HALF, TILE), BF16),
            pltpu.VMEM((CHUNKS, 2, 2, TILES_DEV, HALF, TILE), BF16),
            pltpu.VMEM((2, SLOTS + 1, HALF, TILE), BF16),
            pltpu.VMEM((LAG, UNITS_DEV), BF16),
            pltpu.VMEM((CHUNKS, 2, TILES_DEV, HALF, TILE), BF16),
            pltpu.VMEM((CHUNKS, 2, SIDE - 1, TILES_DEV, HALF, TILE), BF16),
            pltpu.VMEM((CHUNKS, 2, SIDE, SIDE, CAP, HALF, TILE), BF16),
            pltpu.VMEM((CHUNKS, 2, SIDE, SIDE, CAP, HALF, TILE), BF16),
            pltpu.SMEM((PEERS, SLOTS), jnp.int32),
            pltpu.VMEM((TILES_DEV, TILE, FAN * TILE), F32),
            pltpu.VMEM((16, UNITS_DEV), F32),
            pltpu.VMEM((TM, 16, UNITS_DEV), F32),
            pltpu.VMEM((TM, STIM, TILE), F32),
            pltpu.VMEM((TM, STIM, TILE), F32),
            pltpu.VMEM((2, SIDE, TILES_DEV // 2, share, FAN * TILE), F32),
            pltpu.VMEM((2, SIDE, TILES_DEV // 2, share, FAN * TILE), BF16),
            pltpu.VMEM((2, TILES_DEV // 2, share, FAN * TILE), BF16),
            pltpu.VMEM((2, 2, TILES_DEV // 2, share, FAN * TILE), BF16),
            pltpu.VMEM((TILES_DEV, share, FAN * TILE), F32),
            dma((6,)),
            dma((CHUNKS,)),
            dma((2,)),
            dma((2, 2, SIDE)),
            dma((6,)),
            dma((6, CHUNKS)),
            dma((2,)),
            dma((2,)),
            dma((2, 2, SIDE)),
            dma((2, 2)),
            dma((2, 2, 2)),
        ],
        compiler_params=pltpu.CompilerParams(
            collective_id=0, has_side_effects=True, vmem_limit_bytes=56 * 1024 * 1024
        ),
    )(
        coupling_target.T,
        coupling_mix,
        spikes,
        stimulus.T,
        bias.reshape(1, UNITS_DEV),
        hist_weight,
        stim_filter.T,
        coupling_weight.reshape(ENTRIES, TILE, TILE),
        jnp.asarray(toeplitz_table()),
    )
    grad_bias, grad_hist, grad_stim, grad_coupling = pl.pallas_call(
        finish_kernel,
        out_shape=[
            jax.ShapeDtypeStruct((1, UNITS_DEV), F32),
            jax.ShapeDtypeStruct((NB, UNITS_DEV), F32),
            jax.ShapeDtypeStruct((STIM, TILE), F32),
            jax.ShapeDtypeStruct((TILES_DEV, FAN, share, TILE), F32),
        ],
        in_specs=[vmem] * 3,
        out_specs=[vmem] * 4,
    )(*[pltpu.with_memory_space_constraint(total, pltpu.VMEM) for total in sums])
    return (grad_bias.reshape(UNITS_DEV), grad_hist, grad_stim.T, grad_coupling)


def solution(mesh):
    return jax.shard_map(
        shards,
        mesh=mesh,
        in_specs=(
            P("tm", "unit"),
            P("tm", None),
            P("unit"),
            P(None, "unit"),
            P("unit", None),
            P(),
            P("unit", None),
            P("unit", None, None, None),
        ),
        out_specs=(
            P("unit"),
            P(None, "unit"),
            P(("unit", "tm"), None),
            P("unit", None, "tm", None),
        ),
        check_vma=False,
    )
```

```python
import functools
import math

import jax
import jax.numpy as jnp
import ml_dtypes
import numpy as np
from jax import lax
from jax.experimental import pallas as pl
from jax.experimental.pallas import tpu as pltpu
from jax.sharding import PartitionSpec as P

TILE = 128
FAN = 4
CAP = 2
NB = 10
LAG = 128
SIDE = 4
PEERS = SIDE * SIDE
HALF = LAG // 2
SLOTS = PEERS * CAP
TILES_DEV = 8
UNITS_DEV = TILES_DEV * TILE
TIME_DEV = 512
CHUNKS = TIME_DEV // LAG
STIM = 64
TM = 8
WIDE = 2 * TILE
ENTRIES = TILES_DEV * FAN
MESH = pl.DeviceIdType.MESH
F32 = jnp.float32
BF16 = jnp.bfloat16


def toeplitz_table():
    low = math.log(2.0)
    spacing = (math.log(LAG + 1.0) - low) / (NB - 1)
    stretched = np.log(np.arange(1, LAG + 1) + 1.0)
    centers = low + spacing * np.arange(NB)
    phases = (stretched[None, :] - centers[:, None]) * (math.pi / (2.0 * spacing))
    shapes = 0.5 * (1.0 + np.cos(np.clip(phases, -math.pi, math.pi)))
    basis = (shapes / shapes.sum(axis=1, keepdims=True)).astype(np.float32)
    table = np.zeros((NB, LAG, 2 * LAG), np.float32)
    for row in range(LAG):
        table[:, row, row : row + LAG] = basis[:, ::-1]
    return table.reshape(NB * LAG, 2 * LAG).astype(ml_dtypes.bfloat16)


def main_kernel(
    target,
    mix,
    spikes_hbm,
    stim_hbm,
    bias_hbm,
    hist_weight_hbm,
    filt_hbm,
    weights_hbm,
    toeplitz_hbm,
    out_stats,
    out_stim,
    out_coupling,
    spikes,
    stim,
    bias,
    hist_weight,
    filt,
    toeplitz,
    blend_filter,
    ext,
    halo,
    weights,
    hist,
    mixed,
    partial_out,
    partial_in,
    dense,
    far_in,
    near_in,
    stage,
    resid_rows,
    resid_out,
    got,
    pick,
    resid_in,
    names,
    grad,
    stats,
    stats_in,
    stim_sum,
    stim_in,
    pair_give,
    pair_in,
    pair_out,
    zed_far,
    zed_in,
    final,
    sem_load,
    sem_spikes,
    sem_halo,
    sem_names,
    sem_send,
    sem_recv,
    sem_stats,
    sem_stim,
    sem_pair,
    sem_far,
    sem_zed,
):
    unit = lax.axis_index("unit")
    tm = lax.axis_index("tm")
    here_x, here_y = unit // SIDE, unit % SIDE
    here_z, core = tm // 2, tm % 2

    def device(step_x, step_y):
        return lax.rem(here_x + step_x, SIDE) * SIDE + lax.rem(here_y + step_y, SIDE)

    def along(half, step):
        return device(0, step) if half else device(step, 0)

    def across(half, step):
        return device(step, 0) if half else device(0, step)

    def around(step):
        return lax.rem(tm + step, TM)

    barrier = pltpu.get_barrier_semaphore()

    for step in range(1, SIDE):
        for half in range(2):
            pl.semaphore_signal(
                barrier, inc=1, device_id=(along(half, step), tm), device_id_type=MESH
            )

    @pl.loop(1, TM)
    def _(step):
        pl.semaphore_signal(barrier, inc=1, device_id=(unit, around(step)), device_id_type=MESH)

    def spikes_copy(chunk):
        rows = pl.ds(pl.multiple_of(chunk * LAG, LAG), LAG)
        return pltpu.make_async_copy(
            spikes_hbm.at[rows, :], spikes.at[rows, :], sem_spikes.at[chunk]
        )

    loads = [
        pltpu.make_async_copy(source, place, sem_load.at[k])
        for k, (source, place) in enumerate(
            (
                (toeplitz_hbm, toeplitz),
                (weights_hbm, weights.at[pl.ds(0, ENTRIES)]),
                (stim_hbm, stim),
                (bias_hbm, bias),
                (hist_weight_hbm, hist_weight),
                (filt_hbm, filt),
            )
        )
    ]
    spikes_copy(0).start()
    spikes_copy(1).start()
    loads[0].start()
    spikes_copy(3).start()
    loads[1].start()
    spikes_copy(2).start()
    for load in loads[2:]:
        load.start()

    @pl.loop(0, PEERS)
    def _(owner):
        first, last = owner * TILES_DEV, owner * TILES_DEV + TILES_DEV - 1
        low, high = jnp.int32(PEERS * TILES_DEV), jnp.int32(-1)
        for s in range(TILES_DEV):
            for f in range(FAN):
                tile = target[f, s]
                low = jnp.where(tile >= first, jnp.minimum(low, tile), low)
                high = jnp.where(tile <= last, jnp.maximum(high, tile), high)
        names[unit, owner * CAP] = low
        names[unit, owner * CAP + 1] = high

    weights[ENTRIES] = jnp.zeros((TILE, TILE), BF16)
    for half in range(2):
        stage[half, SLOTS] = jnp.zeros((HALF, TILE), BF16)
    stats[...] = jnp.zeros_like(stats)
    stim_sum[...] = jnp.zeros_like(stim_sum)
    grad[...] = jnp.zeros_like(grad)

    def take_spikes(chunk):
        spikes_copy(chunk).wait()
        ext[(chunk + 1) * LAG : (chunk + 2) * LAG, :] = spikes[
            chunk * LAG : (chunk + 1) * LAG, :
        ].astype(BF16)

    take_spikes(0)
    take_spikes(1)
    loads[0].wait()
    combined = jnp.zeros((LAG, 2 * LAG), F32)
    for b in range(NB):
        combined = combined + mix[b] * toeplitz[b * LAG : (b + 1) * LAG, :].astype(F32)
    upper = combined.astype(BF16)
    blend_filter[:LAG, :] = upper
    blend_filter[LAG:, :] = (combined - upper.astype(F32)).astype(BF16)

    def mix_rows(chunk):
        start = pl.multiple_of(chunk * LAG, LAG)
        for part in range(UNITS_DEV // WIDE):
            wide = slice(part * WIDE, (part + 1) * WIDE)
            both = jnp.dot(
                blend_filter[...], ext[pl.ds(start, 2 * LAG), wide], preferred_element_type=F32
            )
            mixed[pl.ds(start, LAG), wide] = (both[:LAG] + both[LAG:]).astype(BF16)

    def visit(chunk, count, steps):
        rows = pl.ds(pl.multiple_of(chunk * LAG, LAG), LAG)

        @pl.loop(0, count)
        def _(turn):
            step_x, step_y = steps(turn)
            owner = device(step_x, step_y)
            low, high = names[unit, owner * CAP], names[unit, owner * CAP + 1]

            def weight_of(s, tile):
                at = jnp.int32(ENTRIES)
                for f in range(FAN):
                    at = jnp.where(target[f, s] == tile, s * FAN + f, at)
                return weights[at]

            total = jnp.zeros((LAG, WIDE), F32)
            for s in range(0, TILES_DEV, 2):
                block = jnp.concatenate(
                    [
                        jnp.concatenate([weight_of(s, low), weight_of(s, high)], axis=1),
                        jnp.concatenate([weight_of(s + 1, low), weight_of(s + 1, high)], axis=1),
                    ],
                    axis=0,
                )
                total = total + jnp.dot(
                    mixed[rows, s * TILE : (s + 2) * TILE], block, preferred_element_type=F32
                )
            rounded = total.astype(BF16)
            for k in range(CAP):
                piece = rounded[:, k * TILE : (k + 1) * TILE]
                partial_out[chunk, 0, step_x, step_y, k] = piece[:HALF]
                partial_out[chunk, 1, step_y, step_x, k] = piece[HALF:]

    order = (1 + 2 * core, 3 - 2 * core, 2)

    def visit_first(chunk):
        visit(chunk, SIDE, lambda turn: (order[0], turn))
        visit(chunk, 3, lambda turn: (2 * turn - turn // 2 * order[0], order[0]))

    mix_rows(1)
    loads[1].wait()
    visit_first(1)
    take_spikes(3)
    pl.semaphore_wait(barrier, 2 * (SIDE - 1) + TM - 1)

    halo_copy = pltpu.make_async_remote_copy(
        src_ref=ext.at[pl.ds(TIME_DEV, LAG)],
        dst_ref=halo,
        send_sem=sem_halo.at[0],
        recv_sem=sem_halo.at[1],
        device_id=(unit, around(1)),
        device_id_type=MESH,
    )

    def names_copy(half, step):
        return pltpu.make_async_remote_copy(
            src_ref=names.at[unit],
            dst_ref=names.at[unit],
            send_sem=sem_names.at[0, half, step],
            recv_sem=sem_names.at[1, half, step],
            device_id=(along(half, step), tm),
            device_id_type=MESH,
        )

    def copy(source, place, kind, chunk, receiver):
        return pltpu.make_async_remote_copy(
            src_ref=source,
            dst_ref=place,
            send_sem=sem_send.at[kind],
            recv_sem=sem_recv.at[kind, chunk],
            device_id=(receiver, tm),
            device_id_type=MESH,
        )

    def arrived(place, kind, chunk):
        copy(place, place, kind, chunk, along(0, 1)).wait_recv()

    def lower(half_ref):
        return half_ref.at[pl.ds(0, TILES_DEV // 2)]

    def upper(half_ref):
        return half_ref.at[pl.ds(TILES_DEV // 2, TILES_DEV // 2)]

    def send_partials(turn, chunk):
        @pl.when(turn == 1)
        def _():
            take_spikes(2)

        @pl.when(turn == CHUNKS - 1)
        def _():
            halo_copy.wait()
            ext[pl.ds(0, LAG), :] = halo[...] * jnp.minimum(tm, 1).astype(BF16)

        @pl.when(turn > 0)
        def _():
            mix_rows(chunk)
            visit_first(chunk)

        def send(half, step):
            copy(
                partial_out.at[chunk, half, step],
                partial_in.at[chunk, half, step],
                0,
                chunk,
                along(half, step),
            ).start()

        send(0, order[0])
        send(1, order[0])
        visit(chunk, 3, lambda turn: (order[1], 2 * turn - turn // 2 * order[0]))
        send(0, order[1])
        visit(chunk, 2, lambda turn: (2 * turn, order[1]))
        send(1, order[1])
        visit(chunk, 2, lambda turn: (order[2], 2 * turn))
        send(0, order[2])
        visit(chunk, 1, lambda turn: (0, order[2]))
        send(1, order[2])
        visit(chunk, 1, lambda turn: (0, 0))

        @pl.when(turn == 0)
        def _():
            for half in range(2):
                for step in range(1, SIDE):
                    names_copy(half, step).start()

            halo_copy.start()

    def add_sources(chunk):
        arrived(partial_in.at[chunk, :, pl.ds(1, SIDE - 1)], 0, chunk)
        for half in range(2):
            stage[half, : SLOTS // SIDE] = partial_out[chunk, half, 0].reshape(
                SLOTS // SIDE, HALF, TILE
            )
            stage[half, SLOTS // SIDE : SLOTS] = partial_in[chunk, half, 1:].reshape(
                SLOTS - SLOTS // SIDE, HALF, TILE
            )

            @pl.loop(0, SIDE)
            def _(step):
                owner = across(half, step)

                @pl.loop(0, TILES_DEV)
                def _(local):
                    tile = owner * TILES_DEV + local
                    total = jnp.zeros((HALF, TILE), F32)
                    for back in range(SIDE):
                        source = along(half, (SIDE - back) % SIDE)
                        first = back * (SIDE * CAP) + step * CAP
                        at = jnp.where(
                            names[source, owner * CAP] == tile,
                            first,
                            jnp.where(names[source, owner * CAP + 1] == tile, first + 1, SLOTS),
                        )
                        total = total + stage[half, at].astype(F32)
                    dense[chunk, half, step, local] = total.astype(BF16)

            far = dense.at[chunk, half, 2]
            copy(lower(far), far_in.at[chunk, half, 0], 1, chunk, across(half, 1)).start()
            copy(upper(far), far_in.at[chunk, half, 1], 1, chunk, across(half, 3)).start()

    def pass_sums(chunk):
        arrived(far_in.at[chunk], 1, chunk)
        middle = TILES_DEV // 2
        for half in range(2):
            dense[chunk, half, 1, :middle] = (
                dense[chunk, half, 1, :middle].astype(F32) + far_in[chunk, half, 0].astype(F32)
            ).astype(BF16)
            dense[chunk, half, 3, middle:] = (
                dense[chunk, half, 3, middle:].astype(F32) + far_in[chunk, half, 1].astype(F32)
            ).astype(BF16)
            for place, step in ((0, 1), (1, 3)):
                copy(
                    dense.at[chunk, half, step],
                    near_in.at[chunk, half, place],
                    2,
                    chunk,
                    across(half, step),
                ).start()

    def make_resid(chunk):
        start = pl.multiple_of(chunk * LAG, LAG)
        rows = pl.ds(start, LAG)
        spike_rows = pl.ds(pl.multiple_of(start + LAG, LAG), LAG)
        arrived(near_in.at[chunk], 2, chunk)

        @pl.loop(0, UNITS_DEV // WIDE)
        def _(part):
            left = pl.multiple_of(part * WIDE, WIDE)
            wide = pl.ds(left, WIDE)
            hist[...] = jnp.dot(
                toeplitz[...], ext[pl.ds(start, 2 * LAG), wide], preferred_element_type=F32
            )
            drive = bias[:, wide] + lax.dot_general(
                stim[:, rows], filt[:, wide], (((0,), (0,)), ((), ())), preferred_element_type=F32
            )
            for side in range(2):
                inner = slice(side * TILE, (side + 1) * TILE)
                cols = pl.ds(pl.multiple_of(left + side * TILE, TILE), TILE)
                tile = part * 2 + side
                logit = drive[:, inner]
                for b in range(NB):
                    h = hist[b * LAG : (b + 1) * LAG, inner]
                    logit = logit + hist_weight[b : b + 1, cols] * h
                coupling = jnp.concatenate(
                    [
                        dense[chunk, half, 0, tile].astype(F32)
                        + near_in[chunk, half, 0, tile].astype(F32)
                        + near_in[chunk, half, 1, tile].astype(F32)
                        for half in range(2)
                    ],
                    axis=0,
                )
                resid = ext[spike_rows, cols].astype(F32) - jnp.exp(logit + coupling)
                rounded = resid.astype(BF16)
                for half in range(2):
                    resid_out[chunk, half, tile] = rounded[half * HALF : (half + 1) * HALF]
                resid_rows[:, cols] = rounded
                stats[NB : NB + 1, cols] += jnp.sum(resid, axis=0, keepdims=True)
                for b in range(NB):
                    h = hist[b * LAG : (b + 1) * LAG, inner]
                    stats[b : b + 1, cols] += jnp.sum(h * resid, axis=0, keepdims=True)

        for step, place in ((1, 1), (3, 0)):
            for half in range(2):
                copy(
                    resid_out.at[chunk, half],
                    got.at[chunk, half, place],
                    3,
                    chunk,
                    across(half, step),
                ).start()
        for block in range(TM):
            stim_sum[block] += lax.dot_general(
                stim[:, rows],
                resid_rows[:, block * TILE : (block + 1) * TILE],
                (((1,), (0,)), ((), ())),
                preferred_element_type=F32,
            )

    def forward_resid(chunk):
        arrived(got.at[chunk, :, pl.ds(0, 2)], 3, chunk)
        for half in range(2):
            far = got.at[chunk, half, 2]
            copy(
                lower(got.at[chunk, half, 1]), lower(far), 4, chunk, across(half, 1)
            ).start()
            copy(
                upper(got.at[chunk, half, 0]), upper(far), 4, chunk, across(half, 3)
            ).start()

    def send_named(chunk):
        arrived(got.at[chunk, :, 2], 4, chunk)
        for half in range(2):
            stage[half, :TILES_DEV] = resid_out[chunk, half]
            for step, place in ((1, 0), (2, 2), (3, 1)):
                stage[half, step * TILES_DEV : (step + 1) * TILES_DEV] = got[chunk, half, place]
            for receiver in (2, 1, 3, 0):

                @pl.loop(0, SIDE)
                def _(step):
                    owner = across(half, step)
                    for k in range(CAP):
                        local = (
                            names[along(half, receiver), owner * CAP + k] - owner * TILES_DEV
                        )
                        local = jnp.minimum(jnp.maximum(local, 0), TILES_DEV - 1)
                        pick[chunk, half, receiver, step, k] = stage[
                            half, step * TILES_DEV + local
                        ]

                if receiver:
                    copy(
                        pick.at[chunk, half, receiver],
                        resid_in.at[chunk, half, receiver],
                        5,
                        chunk,
                        along(half, receiver),
                    ).start()

    def take_resid(chunk):
        arrived(resid_in.at[chunk, :, pl.ds(1, SIDE - 1)], 5, chunk)
        for half in range(2):
            stage[half, : SLOTS // SIDE] = pick[chunk, half, 0].reshape(SLOTS // SIDE, HALF, TILE)
            stage[half, SLOTS // SIDE : SLOTS] = resid_in[chunk, half, 1:].reshape(
                SLOTS - SLOTS // SIDE, HALF, TILE
            )

    def chosen_tile(s, f):
        owner = target[f, s] // TILES_DEV
        gone_x = lax.rem(owner // SIDE - here_x + SIDE, SIDE)
        gone_y = lax.rem(owner % SIDE - here_y + SIDE, SIDE)
        back_x = lax.rem(SIDE - gone_x, SIDE)
        back_y = lax.rem(SIDE - gone_y, SIDE)
        rank = (target[f, s] == names[unit, owner * CAP + 1]).astype(jnp.int32)
        return jnp.concatenate(
            [
                stage[0, (back_x * SIDE + gone_y) * CAP + rank],
                stage[1, (back_y * SIDE + gone_x) * CAP + rank],
            ],
            axis=0,
        )

    def add_grad(chunk, s):
        grad[s] += lax.dot_general(
            mixed[pl.ds(pl.multiple_of(chunk * LAG, LAG), LAG), s * TILE : (s + 1) * TILE],
            jnp.concatenate([chosen_tile(s, f) for f in range(FAN)], axis=1),
            (((0,), (0,)), ((), ())),
            preferred_element_type=F32,
        )

    def stats_copy(step):
        return pltpu.make_async_remote_copy(
            src_ref=stats,
            dst_ref=stats_in.at[step],
            send_sem=sem_stats.at[0],
            recv_sem=sem_stats.at[1],
            device_id=(unit, around(step)),
            device_id_type=MESH,
        )

    def stim_copy(step):
        return pltpu.make_async_remote_copy(
            src_ref=stim_sum.at[around(step)],
            dst_ref=stim_in.at[step],
            send_sem=sem_stim.at[0],
            recv_sem=sem_stim.at[1],
            device_id=(unit, around(step)),
            device_id_type=MESH,
        )

    def all_arrived(place, sems):
        others = place.at[pl.ds(1, TM - 1)]
        pltpu.make_async_remote_copy(
            src_ref=others,
            dst_ref=others,
            send_sem=sems.at[0],
            recv_sem=sems.at[1],
            device_id=(unit, around(1)),
            device_id_type=MESH,
        ).wait()

    last = CHUNKS - 1

    def during(turn, delay, step):
        @pl.when((turn >= delay) & (turn < delay + CHUNKS))
        def _():
            step(lax.rem(turn - delay + 1, CHUNKS))

    @pl.loop(0, 10)
    def _(turn):
        during(turn, 0, functools.partial(send_partials, turn))

        @pl.when(turn == 1)
        def _():
            for half in range(2):
                for step in range(1, SIDE):
                    names_copy(half, step).wait()

            for load in loads[2:]:
                load.wait()

        during(turn, 1, add_sources)

        during(turn, 2, pass_sums)

        during(turn, 3, make_resid)

        @pl.when(turn == 3 + last)
        def _():
            @pl.loop(1, TM)
            def _(step):
                stats_copy(step).start()
                stim_copy(step).start()

        during(turn, 4, forward_resid)

        during(turn, 5, send_named)

        @pl.when(turn >= 7)
        def _():
            chunk = lax.rem(turn - 7 + 1, CHUNKS)
            take_resid(chunk)
            for s in range(TILES_DEV):
                add_grad(chunk, s)

    share = TILE // TM
    half_tiles = TILES_DEV // 2

    def pair_copy(half, z):
        return pltpu.make_async_remote_copy(
            src_ref=pair_give.at[half, z],
            dst_ref=pair_in.at[half, z],
            send_sem=sem_pair.at[0, half, z],
            recv_sem=sem_pair.at[1, half, z],
            device_id=(unit, here_z * 2 + 1 - core),
            device_id_type=MESH,
        )

    forth, back = lax.rem(here_z + 1, SIDE), lax.rem(here_z + 3, SIDE)
    ways = (forth, back)

    def far_copy(half):
        return pltpu.make_async_remote_copy(
            src_ref=pair_out.at[half, lax.rem(here_z + 2, SIDE)],
            dst_ref=zed_far.at[half],
            send_sem=sem_far.at[0, half],
            recv_sem=sem_far.at[1, half],
            device_id=(unit, ways[half] * 2 + core),
            device_id_type=MESH,
        )

    def zed_copy(half, way):
        return pltpu.make_async_remote_copy(
            src_ref=pair_out.at[half, ways[way]],
            dst_ref=zed_in.at[half, way],
            send_sem=sem_zed.at[0, half, way],
            recv_sem=sem_zed.at[1, half, way],
            device_id=(unit, ways[way] * 2 + core),
            device_id_type=MESH,
        )

    def both(half, z):
        kept = pl.ds(pl.multiple_of((z * 2 + core) * share, share), share)
        return grad[half * half_tiles : (half + 1) * half_tiles, kept, :] + pair_in[half, z].astype(F32)

    take_resid(0)
    for half in range(2):
        for s in range(half * half_tiles, (half + 1) * half_tiles):
            add_grad(0, s)
        for step in (2, 3 - 2 * half, 1 + 2 * half, 0):
            z = lax.rem(here_z + step, SIDE)
            given = pl.ds(pl.multiple_of((z * 2 + 1 - core) * share, share), share)
            pair_give[half, z] = grad[
                half * half_tiles : (half + 1) * half_tiles, given, :
            ].astype(BF16)
            pair_copy(half, z).start()
    for half in range(2):
        for z in (lax.rem(here_z + 2, SIDE), ways[1 - half]):
            pair_copy(half, z).wait_recv()
            pair_out[half, z] = both(half, z).astype(BF16)
        far_copy(half).start()
        zed_copy(half, 1 - half).start()
    for half in range(2):
        z = ways[half]
        pair_copy(half, z).wait_recv()
        own = both(half, z)
        far_copy(half).wait_recv()
        pair_out[half, z] = (own + zed_far[half].astype(F32)).astype(BF16)
        zed_copy(half, half).start()
    for half in range(2):
        pair_copy(half, here_z).wait_recv()
        final[half * half_tiles : (half + 1) * half_tiles] = both(half, here_z)

    all_arrived(stats_in, sem_stats)
    all_arrived(stim_in, sem_stim)
    stats_in[0] = stats[...]
    total = stats_in[tm]
    for block in range(1, TM):
        total = total + stats_in[lax.rem(tm - block + TM, TM)]
    out_stats[...] = total
    stim_total = stim_sum[tm]
    for step in range(1, TM):
        stim_total = stim_total + stim_in[step]
    out_stim[...] = stim_total

    others = pl.ds(1, SIDE - 1)
    for kind, place in enumerate(
        (
            partial_in.at[:, :, others],
            far_in,
            near_in,
            got.at[:, :, pl.ds(0, 2)],
            got.at[:, :, 2],
            resid_in.at[:, :, others],
        )
    ):
        copy(place, place, kind, 0, along(0, 1)).wait_send()
    for half in range(2):
        for z in range(SIDE):
            pair_copy(half, z).wait_send()
    for half in range(2):
        tiles = slice(half * half_tiles, (half + 1) * half_tiles)
        total = final[tiles]
        far_copy(half).wait_send()
        for way in range(2):
            zed_copy(half, way).wait()
            total = total + zed_in[half, way].astype(F32)
        out_coupling[tiles] = total


def finish_kernel(stats, stim, coupling, out_bias, out_hist, out_stim, out_coupling):
    time_total = float(TIME_DEV * TM)
    out_hist[...] = stats[:NB, :] / time_total
    out_bias[...] = stats[NB : NB + 1, :] / time_total
    out_stim[...] = stim[...] / time_total
    for f in range(FAN):
        out_coupling[:, f] = coupling[:, :, f * TILE : (f + 1) * TILE] / time_total


def shards(
    spikes, stimulus, bias, hist_weight, stim_filter, coupling_mix, coupling_target, coupling_weight
):
    smem = pl.BlockSpec(memory_space=pltpu.SMEM)
    vmem = pl.BlockSpec(memory_space=pltpu.VMEM)
    anywhere = pl.BlockSpec(memory_space=pl.ANY)
    dma = pltpu.SemaphoreType.DMA
    share = TILE // TM
    sums = pl.pallas_call(
        main_kernel,
        out_shape=[
            pltpu.VMEM((16, UNITS_DEV), F32),
            pltpu.VMEM((STIM, TILE), F32),
            pltpu.VMEM((TILES_DEV, share, FAN * TILE), F32),
        ],
        in_specs=[smem] * 2 + [anywhere] * 7,
        out_specs=[vmem] * 3,
        scratch_shapes=[
            pltpu.VMEM((TIME_DEV, UNITS_DEV), jnp.int32),
            pltpu.VMEM((STIM, TIME_DEV), BF16),
            pltpu.VMEM((1, UNITS_DEV), F32),
            pltpu.VMEM((NB, UNITS_DEV), F32),
            pltpu.VMEM((STIM, UNITS_DEV), BF16),
            pltpu.VMEM((NB * LAG, 2 * LAG), BF16),
            pltpu.VMEM((2 * LAG, 2 * LAG), BF16),
            pltpu.VMEM((TIME_DEV + LAG, UNITS_DEV), BF16),
            pltpu.VMEM((LAG, UNITS_DEV), BF16),
            pltpu.VMEM((ENTRIES + 1, TILE, TILE), BF16),
            pltpu.VMEM((NB * LAG, WIDE), F32),
            pltpu.VMEM((TIME_DEV, UNITS_DEV), BF16),
            pltpu.VMEM((CHUNKS, 2, SIDE, SIDE, CAP, HALF, TILE), BF16),
            pltpu.VMEM((CHUNKS, 2, SIDE, SIDE, CAP, HALF, TILE), BF16),
            pltpu.VMEM((CHUNKS, 2, SIDE, TILES_DEV, HALF, TILE), BF16),
            pltpu.VMEM((CHUNKS, 2, 2, TILES_DEV // 2, HALF, TILE), BF16),
            pltpu.VMEM((CHUNKS, 2, 2, TILES_DEV, HALF, TILE), BF16),
            pltpu.VMEM((2, SLOTS + 1, HALF, TILE), BF16),
            pltpu.VMEM((LAG, UNITS_DEV), BF16),
            pltpu.VMEM((CHUNKS, 2, TILES_DEV, HALF, TILE), BF16),
            pltpu.VMEM((CHUNKS, 2, SIDE - 1, TILES_DEV, HALF, TILE), BF16),
            pltpu.VMEM((CHUNKS, 2, SIDE, SIDE, CAP, HALF, TILE), BF16),
            pltpu.VMEM((CHUNKS, 2, SIDE, SIDE, CAP, HALF, TILE), BF16),
            pltpu.SMEM((PEERS, SLOTS), jnp.int32),
            pltpu.VMEM((TILES_DEV, TILE, FAN * TILE), F32),
            pltpu.VMEM((16, UNITS_DEV), F32),
            pltpu.VMEM((TM, 16, UNITS_DEV), F32),
            pltpu.VMEM((TM, STIM, TILE), F32),
            pltpu.VMEM((TM, STIM, TILE), F32),
            pltpu.VMEM((2, SIDE, TILES_DEV // 2, share, FAN * TILE), BF16),
            pltpu.VMEM((2, SIDE, TILES_DEV // 2, share, FAN * TILE), BF16),
            pltpu.VMEM((2, SIDE, TILES_DEV // 2, share, FAN * TILE), BF16),
            pltpu.VMEM((2, TILES_DEV // 2, share, FAN * TILE), BF16),
            pltpu.VMEM((2, 2, TILES_DEV // 2, share, FAN * TILE), BF16),
            pltpu.VMEM((TILES_DEV, share, FAN * TILE), F32),
            dma((6,)),
            dma((CHUNKS,)),
            dma((2,)),
            dma((2, 2, SIDE)),
            dma((6,)),
            dma((6, CHUNKS)),
            dma((2,)),
            dma((2,)),
            dma((2, 2, SIDE)),
            dma((2, 2)),
            dma((2, 2, 2)),
        ],
        compiler_params=pltpu.CompilerParams(
            collective_id=0, has_side_effects=True, vmem_limit_bytes=56 * 1024 * 1024
        ),
    )(
        coupling_target.T,
        coupling_mix,
        spikes,
        stimulus.T,
        bias.reshape(1, UNITS_DEV),
        hist_weight,
        stim_filter.T,
        coupling_weight.reshape(ENTRIES, TILE, TILE),
        jnp.asarray(toeplitz_table()),
    )
    grad_bias, grad_hist, grad_stim, grad_coupling = pl.pallas_call(
        finish_kernel,
        out_shape=[
            jax.ShapeDtypeStruct((1, UNITS_DEV), F32),
            jax.ShapeDtypeStruct((NB, UNITS_DEV), F32),
            jax.ShapeDtypeStruct((STIM, TILE), F32),
            jax.ShapeDtypeStruct((TILES_DEV, FAN, share, TILE), F32),
        ],
        in_specs=[vmem] * 3,
        out_specs=[vmem] * 4,
    )(*[pltpu.with_memory_space_constraint(total, pltpu.VMEM) for total in sums])
    return (grad_bias.reshape(UNITS_DEV), grad_hist, grad_stim.T, grad_coupling)


def solution(mesh):
    return jax.shard_map(
        shards,
        mesh=mesh,
        in_specs=(
            P("tm", "unit"),
            P("tm", None),
            P("unit"),
            P(None, "unit"),
            P("unit", None),
            P(),
            P("unit", None),
            P("unit", None, None, None),
        ),
        out_specs=(
            P("unit"),
            P(None, "unit"),
            P(("unit", "tm"), None),
            P("unit", None, "tm", None),
        ),
        check_vma=False,
    )
```
